32 devices in a mesh: gx: 4 (over y, core), gy: 8 (over z, x).
Axes of the slice: x: 2, y: 2, z: 4, core: 2. Of those that a mesh axis runs over, the one named last changes fastest.
Arguments:
- source: float32 [128, 128, 128], P('gx', 'gy'), may hold values from -30 to 30
- permittivity: float32 [128, 128, 128], P('gx', 'gy'), may hold values from 2 to 80
- screening: float32 [128, 128, 128], P('gx', 'gy'), may hold values from 0 to 16
- potential: float32 [128, 128, 128], P('gx', 'gy'), may hold values from -3 to 3
- fixed_cell: int32 [128, 128, 128], P('gx', 'gy'), may hold values 0 or 1
Outputs:
- result: float32 [128, 128, 128], P('gx', 'gy')
The draws below stay inside these ranges and needn't reach their ends.
All inputs are finite; a program needn't handle non-finite values. No bound on the sum of `fixed_cell` on one device may be relied on, other than what follows from the above.
Results may differ from the reference program's by a relative error of at most 0.0003.
Values sent between devices are 32-bit elements; how exact they have to be, the bound alone decides.
No kernel may reach another device: no remote copies, remote signals or barrier semaphores. Data moves between devices by JAX's collectives and lax.ppermute only.
A program may use at most 128 MiB of HBM per device.

```python
import math
import jax
import jax.numpy as jnp
from jax import lax

CX = 32
CY = 16
NZ = 128
NX = 128
NY = 128


def solute_region(key):
    blocks_x = NX // CX
    blocks_y = NY // CY
    base = jax.random.fold_in(key, 7071)
    key_x, key_y, key_z, key_r = jax.random.split(base, 4)
    centre_x = jax.random.randint(key_x, (blocks_x, blocks_y), 0, CX) + CX * jnp.arange(blocks_x, dtype=jnp.int32)[:, None]
    centre_y = jax.random.randint(key_y, (blocks_x, blocks_y), 0, CY) + CY * jnp.arange(blocks_y, dtype=jnp.int32)[None, :]
    centre_z = jax.random.randint(key_z, (blocks_x, blocks_y), 0, NZ)
    radius = jax.random.randint(key_r, (blocks_x, blocks_y), CY // 2, CY + CY // 2 + 1)
    first = jnp.arange(NX, dtype=jnp.int32)
    second = jnp.arange(NY, dtype=jnp.int32)
    third = jnp.arange(NZ, dtype=jnp.int32)
    block_x = first // CX
    block_y = second // CY
    inside = jnp.zeros((NX, NY, NZ), dtype=jnp.bool_)
    for offset_x in (-1, 0, 1):
        for offset_y in (-1, 0, 1):
            near_x = jnp.clip(block_x + offset_x, 0, blocks_x - 1)
            near_y = jnp.clip(block_y + offset_y, 0, blocks_y - 1)
            pick_x = centre_x[near_x[:, None], near_y[None, :]]
            pick_y = centre_y[near_x[:, None], near_y[None, :]]
            pick_z = centre_z[near_x[:, None], near_y[None, :]]
            pick_r = radius[near_x[:, None], near_y[None, :]]
            gap_x = first[:, None] - pick_x
            gap_y = second[None, :] - pick_y
            planar = gap_x * gap_x + gap_y * gap_y
            gap_z = third[None, None, :] - pick_z[:, :, None]
            reach = (pick_r * pick_r)[:, :, None]
            inside = inside | (planar[:, :, None] + gap_z * gap_z <= reach)
    return inside


def draw_permittivity(key, part):
    inside = solute_region(key)
    noise = jax.random.uniform(jax.random.fold_in(key, 311), (NX, NY, NZ), jnp.float32)
    solute = 2.0 * jnp.exp(noise * math.log(2.0))
    solvent = 40.0 * jnp.exp(noise * math.log(2.0))
    return jnp.where(inside, solute, solvent).astype(jnp.float32)


def draw_screening(key, part):
    inside = solute_region(key)
    noise = jax.random.uniform(jax.random.fold_in(key, 733), (NX, NY, NZ), jnp.float32)
    solvent = 4.0 * jnp.exp(noise * math.log(4.0))
    return jnp.where(inside, 0.0, solvent).astype(jnp.float32)


def plant(drawn, key, smallest, top_value):
    shape = drawn.shape
    spot = [jax.random.randint(jax.random.fold_in(key, axis), (), 0, shape[axis]) for axis in range(len(shape))]
    drawn = drawn.at[tuple(spot)].set(smallest)
    longest = shape.index(max(shape))
    spot[longest] = (spot[longest] + 1) % shape[longest]
    return drawn.at[tuple(spot)].set(top_value)


def steps_of(own_key, dims, pieces, smallest, high):
    def one(axis_at, shards_of):
        steps = jax.random.uniform(jax.random.fold_in(jax.random.fold_in(own_key, 6), axis_at), (shards_of,), jnp.float32, smallest / len(pieces), high / len(pieces))
        return jnp.repeat(jnp.exp(steps), dims[axis_at] // shards_of).reshape((-1,) + (1,) * (len(dims) - axis_at - 1))

    level = one(*pieces[0])
    for cut in pieces[1:]:
        level = level * one(*cut)
    return level


def centred(stream_key, extent, width, most, shards=(), kind=jnp.bfloat16):
    array = width * jax.random.normal(stream_key, extent, jnp.float32)
    if shards:
        array = array * steps_of(stream_key, extent, shards, -0.22, 0.18)
    return jnp.clip(array, -most, most).astype(kind)


def setup_inputs(seed: int = 0) -> dict:
    keys = jax.random.split(jax.random.key(seed), 6)
    return {
        "source": centred(keys[0], (NX, NY, NZ), 5.0, 30.0, ((0, 4), (1, 8)), jnp.float32),
        "permittivity": draw_permittivity(jax.random.fold_in(keys[5], 71), 0),
        "screening": draw_screening(jax.random.fold_in(keys[5], 71), 0),
        "potential": centred(keys[3], (NX, NY, NZ), 0.5, 3.0, ((0, 4), (1, 8)), jnp.float32),
        "fixed_cell": plant((jax.random.randint(keys[4], (NX, NY, NZ), 0, 8) < 1).astype(jnp.int32), jax.random.fold_in(keys[4], 1), 0, 1),
    }


def neighbour(field, direction):
    axis = direction // 2
    size = field.shape[axis]
    zero = jnp.zeros_like(lax.slice_in_dim(field, 0, 1, axis=axis))
    if direction % 2 == 0:
        return jnp.concatenate([lax.slice_in_dim(field, 1, size, axis=axis), zero], axis=axis)
    return jnp.concatenate([zero, lax.slice_in_dim(field, 0, size - 1, axis=axis)], axis=axis)


def face(cells, direction):
    return 0.5 * (cells + neighbour(cells, direction))


def centre_of(cells):
    total = face(cells, 0)
    for direction in range(1, 6):
        total = total + face(cells, direction)
    return total


def beside_of(field, cells):
    total = face(cells, 0) * neighbour(field, 0)
    for direction in range(1, 6):
        total = total + face(cells, direction) * neighbour(field, direction)
    return total


def parity_of(shape):
    total = lax.broadcasted_iota(jnp.int32, shape, 0) + lax.broadcasted_iota(jnp.int32, shape, 1) + lax.broadcasted_iota(jnp.int32, shape, 2)
    return total % 2


def restrict(field):
    first, second, third = field.shape
    return field.reshape(first // 2, 2, second // 2, 2, third // 2, 2).mean(axis=(1, 3, 5))


def prolong(field):
    return jnp.repeat(jnp.repeat(jnp.repeat(field, 2, axis=0), 2, axis=1), 2, axis=2)


def coarse_apply(field, cells, centre, react, factor):
    return factor * (centre * field - beside_of(field, cells)) + react * field


def coarse_sweeps(field, rhs, cells, centre, react, factor, parity, sweeps):
    for sweep in range(sweeps):
        for colour in (0, 1):
            applied = coarse_apply(field, cells, centre, react, factor)
            update = field - (applied - rhs) / (factor * centre + react)
            field = jnp.where(parity == colour, update, field)
    return field


def reference(source, permittivity, screening, potential, fixed_cell):
    free = fixed_cell == 0
    centre0 = centre_of(permittivity)
    parity0 = parity_of(source.shape)

    def mapped(field):
        return centre0 * field - beside_of(field, permittivity) + screening * jnp.sinh(field) - source

    def fine_half(field, colour):
        update = field - mapped(field) / (centre0 + screening * jnp.cosh(field))
        return jnp.where(free & (parity0 == colour), update, field)

    field = fine_half(potential, 0)
    field = fine_half(field, 1)
    fine_residual = jnp.where(free, -mapped(field), jnp.float32(0.0))
    react = screening * jnp.cosh(field)
    perm1 = restrict(permittivity)
    react1 = restrict(react)
    rhs1 = restrict(fine_residual)
    centre1 = centre_of(perm1)
    parity1 = parity_of(rhs1.shape)
    err1 = coarse_sweeps(jnp.zeros_like(rhs1), rhs1, perm1, centre1, react1, 0.25, parity1, 2)
    rhs2 = restrict(rhs1 - coarse_apply(err1, perm1, centre1, react1, 0.25))
    perm2 = restrict(perm1)
    react2 = restrict(react1)
    centre2 = centre_of(perm2)
    parity2 = parity_of(rhs2.shape)
    err2 = coarse_sweeps(jnp.zeros_like(rhs2), rhs2, perm2, centre2, react2, 0.0625, parity2, 4)
    err1 = err1 + prolong(err2)
    err1 = coarse_sweeps(err1, rhs1, perm1, centre1, react1, 0.25, parity1, 2)
    field = jnp.where(free, field + prolong(err1), field)
    field = fine_half(field, 0)
    field = fine_half(field, 1)
    return field
```

```python
import jax
import jax.numpy as jnp
from jax import lax
from jax.experimental import pallas as pl
from jax.experimental.pallas import tpu as pltpu
from jax.sharding import PartitionSpec as P

F32 = jnp.float32
BX, BY, NL = 32, 16, 128
H0 = 3
FX_ = BX + 2 * H0
YE = 24
X1 = BX // 2
H1 = 8
G1 = X1 + 2 * H1
LN2 = 0.6931471805599453


def rot(value, shift, axis):
    return pltpu.roll(value, shift % value.shape[axis], axis)


def iota(shape, axis):
    return lax.broadcasted_iota(jnp.int32, shape, axis)


def sds(*shape):
    return jax.ShapeDtypeStruct(shape, F32)


def by_parity(axis, action):
    odd = lax.axis_index(axis) % 2

    @pl.when(odd == 0)
    def _():
        action(0, 1)

    @pl.when(odd == 1)
    def _():
        action(1, 0)


def call(kernel, out_shape, scratch=(), vmem=24, name=None):
    return pl.pallas_call(
        kernel,
        out_shape=out_shape,
        scratch_shapes=list(scratch),
        compiler_params=pltpu.CompilerParams(vmem_limit_bytes=vmem << 20),
        name=name,
    )


def pack_y(pot, per, src, scr, fix, out0, out1):
    outs = (out0, out1)
    zlane = iota((BX // 2, NL), 1)

    def free_of(value):
        return jnp.where(value == 0, F32(1.0), F32(0.0))

    def row(ref, r):
        return ref[pl.ds(r, BX, stride=BY), :]

    def half(ref, r, parity):
        even = ref[pl.ds(r, BX // 2, stride=2 * BY), :]
        odd = ref[pl.ds(BY + r, BX // 2, stride=2 * BY), :]
        return jnp.where((r + zlane) % 2 == parity, even, odd)

    def side(out, r1, r2, r3):
        rows = [
            row(pot, r1), row(per, r1), row(src, r1), row(scr, r1), free_of(row(fix, r1)),
            row(pot, r2), row(per, r2), free_of(row(fix, r2)),
        ]
        for k, value in enumerate(rows):
            out[BX * k : BX * (k + 1), :] = value
        base = BX * len(rows)
        for k, value in enumerate([half(pot, r3, 1), half(per, r3, 1), half(src, r2, 0), half(scr, r2, 0)]):
            out[base + k * BX // 2 : base + (k + 1) * BX // 2, :] = value

    def action(hi, lo):
        side(outs[hi], BY - 1, BY - 2, BY - 3)
        side(outs[lo], 0, 1, 2)

    by_parity("gy", action)


def pack_x(pot, per, src, scr, fix, got0, got1, hpot, hper, hsrc, hscr, hfree, out0, out1):
    gots, outs = (got0, got1), (out0, out1)
    halos = (hpot, hper, hsrc, hscr, hfree)
    for h in halos:
        h[...] = jnp.zeros_like(h)

    def place(got, slots):
        def whole(ref, k, slot):
            ref[pl.ds(slot, BX, stride=8), :] = got[BX * k : BX * (k + 1), :]

        def halved(ref, k, slot):
            value = got[BX * 8 + k * BX // 2 : BX * 8 + (k + 1) * BX // 2, :]
            ref[pl.ds(slot, BX // 2, stride=16), :] = value
            ref[pl.ds(8 + slot, BX // 2, stride=16), :] = value

        s1, s2, s3 = slots
        for k, ref in enumerate(halos):
            whole(ref, k, s1)
        whole(hpot, 5, s2)
        whole(hper, 6, s2)
        whole(hfree, 7, s2)
        halved(hpot, 0, s3)
        halved(hper, 1, s3)
        halved(hsrc, 2, s2)
        halved(hscr, 3, s2)

    def action_y(hi, lo):
        place(gots[hi], (0, 1, 2))
        place(gots[lo], (7, 6, 5))

    by_parity("gy", action_y)

    def slab(out, planes):
        k = 0
        for ref, h, depth in ((pot, hpot, 3), (per, hper, 3), (src, hsrc, 2), (scr, hscr, 2), (fix, hfree, 2)):
            for x in planes[:depth]:
                own = ref[BY * x : BY * (x + 1), :]
                if ref is fix:
                    own = jnp.where(own == 0, F32(1.0), F32(0.0))
                out[YE * k : YE * k + BY, :] = own
                out[YE * k + BY : YE * (k + 1), :] = h[8 * x : 8 * (x + 1), :]
                k += 1

    def action_x(hi, lo):
        slab(outs[hi], (BX - 1, BX - 2, BX - 3))
        slab(outs[lo], (0, 1, 2))

    by_parity("gx", action_x)


def nonlinear(u, scr):
    up = jnp.exp(u - F32(LN2))
    down = jnp.exp(-u - F32(LN2))
    return scr * (up - down), scr * (up + down)


def off_sum(v, i, plane, fx, fyp, fym, fzp, fzm):
    return (
        (fx[i] * v[i + 1] + fx[i - 1] * v[i - 1])
        + (fyp[i] * rot(plane, -1, 0) + fym[i] * rot(plane, 1, 0))
        + (fzp[i] * v_z(plane, 1) + fzm[i] * v_z(plane, -1))
    )


def v_z(plane, step):
    return rot(plane, -step, 1)


def fine_half(u, i, colour, shift, refs):
    c, fx, fyp, fym, fzp, fzm, src, scr, free = refs
    plane = u[i]
    sh, ch = nonlinear(plane, scr[i])
    value = c[i] * plane - off_sum(u, i, plane, fx, fyp, fym, fzp, fzm) + sh - src[i]
    update = plane - value / (c[i] + ch)
    parity = (iota((YE, NL), 0) + iota((YE, NL), 1) + (i + shift)) % 2
    u[i] = jnp.where((parity == colour) & (free[i] > 0.5), update, plane)


def faces_of(p, i, scale, zstep, fx, fyp, fym, fzp, fzm):
    lane = iota((YE, NL), 1)
    plane = p[i]
    half = F32(0.5 * scale)
    fx[i] = half * (plane + p[i + 1])
    fyp[i] = half * (plane + rot(plane, -1, 0))
    fym[i] = half * (plane + rot(plane, 1, 0))
    fzp[i] = jnp.where(lane >= NL - zstep, F32(0.0), half * (plane + rot(plane, -zstep, 1)))
    fzm[i] = jnp.where(lane < zstep, F32(0.0), half * (plane + rot(plane, zstep, 1)))


def lane_pairs(value, step):
    lane = iota(value.shape, value.ndim - 1)
    return value + jnp.where((lane // step) % 2 == 0, rot(value, -step, value.ndim - 1), rot(value, step, value.ndim - 1))


def fine_pre(pot, per, src, scr, fix, hpot, hper, hsrc, hscr, hfree, got0, got1,
             u, c, fx, fyp, fym, fzp, fzm, esrc, escr, efree, c1, g1, m0, m1,
             ep, tr, tc, tp, p1):
    gots, outs = (got0, got1), (m0, m1)

    def own(x, _):
        i = x + H0
        at = pl.multiple_of(x * BY, 8)
        ht = pl.multiple_of(x * 8, 8)
        for ref, h, ext in ((pot, hpot, u), (per, hper, ep), (src, hsrc, esrc), (scr, hscr, escr), (fix, hfree, efree)):
            value = ref[pl.ds(at, BY), :]
            if ref is fix:
                value = jnp.where(value == 0, F32(1.0), F32(0.0))
            ext[i, 0:BY, :] = value
            ext[i, BY:YE, :] = h[pl.ds(ht, 8), :]
        return 0

    lax.fori_loop(0, BX, own, 0, unroll=4)

    def place(got, planes):
        k = 0
        for ext, depth in ((u, 3), (ep, 3), (esrc, 2), (escr, 2), (efree, 2)):
            for i in planes[:depth]:
                ext[i] = got[YE * k : YE * (k + 1), :]
                k += 1

    def action_x(hi, lo):
        place(gots[hi], (BX + H0, BX + H0 + 1, BX + H0 + 2))
        place(gots[lo], (H0 - 1, H0 - 2, H0 - 3))

    by_parity("gx", action_x)
    for ext in (esrc, escr, efree):
        ext[0] = jnp.zeros((YE, NL), F32)
        ext[FX_ - 1] = jnp.zeros((YE, NL), F32)

    fx[0] = F32(0.5) * (ep[0] + ep[1])
    refs = (c, fx, fyp, fym, fzp, fzm, esrc, escr, efree)

    def first(i, _):
        faces_of(ep, i, 1.0, 1, fx, fyp, fym, fzp, fzm)
        lane = iota((YE, NL), 1)
        ends = jnp.where((lane == 0) | (lane == NL - 1), F32(0.5) * ep[i], F32(0.0))
        c[i] = (fx[i] + fx[i - 1]) + (fyp[i] + fym[i]) + (fzp[i] + fzm[i]) + ends
        fine_half(u, i, 0, 1, refs)
        return 0

    lax.fori_loop(1, FX_ - 1, first, 0, unroll=2)

    def second(i, _):
        fine_half(u, i, 1, 1, refs)
        return 0

    lax.fori_loop(2, FX_ - 2, second, 0, unroll=2)

    def down(x1, _):
        rs, cs = [], []
        for k in (0, 1):
            i = 2 * x1 + k + H0
            plane = u[i]
            sh, ch = nonlinear(plane, escr[i])
            value = c[i] * plane - off_sum(u, i, plane, fx, fyp, fym, fzp, fzm) + sh - esrc[i]
            rs.append(jnp.where(efree[i] > 0.5, -value, F32(0.0))[0:BY])
            cs.append(ch[0:BY])
        at = pl.multiple_of(x1 * BY, 8)
        tr[pl.ds(at, BY), :] = lane_pairs(rs[0] + rs[1], 1)
        tc[pl.ds(at, BY), :] = lane_pairs(cs[0] + cs[1], 1)
        return 0

    lax.fori_loop(0, X1, down, 0, unroll=2)

    def coarse_p(k, _):
        at = pl.multiple_of(k * YE, 8)
        tp[pl.ds(at, YE), :] = lane_pairs(ep[2 * k + 1] + ep[2 * k + 2], 1)
        return 0

    lax.fori_loop(0, X1 + 2, coarse_p, 0, unroll=2)

    eighth = F32(0.125)
    sub = iota((8, NL), 0)
    lane = iota((8, NL), 1)

    def gather_p(k, _):
        p1[k] = eighth * (tp[pl.ds(k * YE, 8, stride=2), :] + tp[pl.ds(k * YE + 1, 8, stride=2), :])
        return 0

    lax.fori_loop(0, X1 + 2, gather_p, 0, unroll=2)

    def make(x1, _):
        k = x1 + 1
        p = p1[k]
        base = k * YE
        high = eighth * (tp[pl.ds(base + 2, 8, stride=2), :] + tp[pl.ds(base + 3, 8, stride=2), :])
        edge = tp[pl.ds(pl.multiple_of(base + 16, 8), 8), :]
        edge = eighth * (edge + rot(edge, 1, 0))
        low = jnp.where(sub == 0, rot(edge, 1, 0), rot(p, 1, 0))
        front = jnp.where(lane >= NL - 2, F32(0.0), rot(p, -2, 1))
        back = jnp.where(lane < 2, F32(0.0), rot(p, 2, 1))
        near = (p1[k + 1] + p1[k - 1]) + (high + low) + (front + back)
        centre = F32(3.0) * p + F32(0.5) * near
        at = x1 * BY
        r = eighth * (tr[pl.ds(at, 8, stride=2), :] + tr[pl.ds(at + 1, 8, stride=2), :])
        react = eighth * (tc[pl.ds(at, 8, stride=2), :] + tc[pl.ds(at + 1, 8, stride=2), :])
        diag = F32(0.25) * centre + react
        c1[x1] = react
        g1[x1] = diag
        message = jnp.where(lane % 2 == 0, r, F32(1.0) / diag)
        m0[pl.ds(pl.multiple_of(x1 * 8, 8), 8), :] = message
        m1[pl.ds(pl.multiple_of(x1 * 8, 8), 8), :] = message
        return 0

    lax.fori_loop(0, X1, make, 0, unroll=2)

    for a in range(X1 // 2):
        message = jnp.where(lane % 2 == 0, p1[1 + 2 * a], p1[2 + 2 * a])
        for m in outs:
            m[X1 * 8 + 8 * a : X1 * 8 + 8 * a + 8, :] = message

    zl = iota((BX // 2, NL), 1)
    base = X1 * 8 + X1 * 4

    def odd_row(out, y):
        even = u[pl.ds(H0, BX // 2, stride=2), y, :]
        odd = u[pl.ds(H0 + 1, BX // 2, stride=2), y, :]
        out[base : base + BX // 2, :] = jnp.where((y + zl) % 2 == 1, even, odd)

    def action_y(hi, lo):
        odd_row(outs[hi], BY - 2)
        odd_row(outs[lo], 1)

    by_parity("gy", action_y)


YMSG = X1 * 8 + X1 * 4 + BX // 2
XMSG = H1 * YE + (H1 // 2) * YE + BY


def pack_x1(m0, m1, got0, got1, u, out0, out1):
    own, gots, outs = m0, (got0, got1), (out0, out1)
    odd_y = lax.axis_index("gy") % 2

    def go(hi, lo):
        def slab(out, first, x):
            at = 0
            for a in range(H1):
                for ref in (own, gots[hi], gots[lo]):
                    out[at : at + 8, :] = ref[8 * (first + a) : 8 * (first + a) + 8, :]
                    at += 8
            for a in range(H1 // 2):
                row = X1 * 8 + 8 * (first // 2 + a)
                for ref in (own, gots[hi], gots[lo]):
                    out[at : at + 8, :] = ref[row : row + 8, :]
                    at += 8
            out[at : at + BY, :] = u[x + H0, 0:BY, :]

        def action(xhi, xlo):
            slab(outs[xhi], X1 - H1, BX - 2)
            slab(outs[xlo], 0, 1)

        by_parity("gx", action)

    @pl.when(odd_y == 0)
    def _():
        go(0, 1)

    @pl.when(odd_y == 1)
    def _():
        go(1, 0)


def coarse_half(e, r, d, i, colour, refs, zstep):
    fx, fyp, fym, fzp, fzm = refs
    plane = e[i]
    beside = (
        (fx[i] * e[i + 1] + fx[i - 1] * e[i - 1])
        + (fyp[i] * rot(plane, -1, 0) + fym[i] * rot(plane, 1, 0))
        + (fzp[i] * rot(plane, -zstep, 1) + fzm[i] * rot(plane, zstep, 1))
    )
    parity = (iota((YE, NL), 0) + iota((YE, NL), 1) // zstep + i) % 2
    e[i] = jnp.where(parity == colour, (r[i] + beside) * d[i], plane)


def dup_even(value):
    lane = iota(value.shape, value.ndim - 1)
    return jnp.where(lane % 2 == 0, value, rot(value, 1, value.ndim - 1))


def dup_odd(value):
    lane = iota(value.shape, value.ndim - 1)
    return jnp.where(lane % 2 == 1, value, rot(value, -1, value.ndim - 1))


def mid_pre(m0, gy0, gy1, gx0, gx1, c1, g1,
            e, r, d, fx, fyp, fym, fzp, fzm, msg,
            p, t, tr, tc, pc):
    gys, gxs = (gy0, gy1), (gx0, gx1)
    odd_y = lax.axis_index("gy") % 2

    def own(hi, lo):
        def planes(a, _):
            rows = [ref[pl.ds(pl.multiple_of(8 * a, 8), 8), :] for ref in (m0, gys[hi], gys[lo])]
            for k, value in enumerate(rows):
                r[H1 + a, 8 * k : 8 * k + 8, :] = dup_even(value)
                d[H1 + a, 8 * k : 8 * k + 8, :] = dup_odd(value)
            return 0

        lax.fori_loop(0, X1, planes, 0, unroll=2)

        def coefs(a, _):
            at = pl.multiple_of(X1 * 8 + 8 * a, 8)
            for k, ref in enumerate((m0, gys[hi], gys[lo])):
                value = ref[pl.ds(at, 8), :]
                p[H1 + 2 * a, 8 * k : 8 * k + 8, :] = dup_even(value)
                p[H1 + 2 * a + 1, 8 * k : 8 * k + 8, :] = dup_odd(value)
            return 0

        lax.fori_loop(0, X1 // 2, coefs, 0, unroll=2)

    @pl.when(odd_y == 0)
    def _():
        own(0, 1)

    @pl.when(odd_y == 1)
    def _():
        own(1, 0)

    def beyond(ref, first):
        def planes(a, _):
            value = ref[pl.ds(pl.multiple_of(YE * a, 8), YE), :]
            r[first + a] = dup_even(value)
            d[first + a] = dup_odd(value)
            return 0

        lax.fori_loop(0, H1, planes, 0, unroll=2)
        for a in range(H1 // 2):
            value = ref[H1 * YE + YE * a : H1 * YE + YE * (a + 1), :]
            p[first + 2 * a] = dup_even(value)
            p[first + 2 * a + 1] = dup_odd(value)

    def action(hi, lo):
        beyond(gxs[hi], H1 + X1)
        beyond(gxs[lo], 0)

    by_parity("gx", action)

    p[G1] = jnp.zeros((YE, NL), F32)
    refs = (fx, fyp, fym, fzp, fzm)

    def begin(i, _):
        faces_of(p, i, 0.25, 2, fx, fyp, fym, fzp, fzm)
        parity = (iota((YE, NL), 0) + iota((YE, NL), 1) // 2 + i) % 2
        e[i] = jnp.where(parity == 0, r[i] * d[i], F32(0.0))
        return 0

    lax.fori_loop(0, G1, begin, 0, unroll=2)
    for k, colour in ((1, 1), (2, 0), (3, 1)):

        def half(i, _, colour=colour):
            coarse_half(e, r, d, i, colour, refs, 2)
            return 0

        lax.fori_loop(k, G1 - k, half, 0, unroll=4)

    def down(x2, _):
        total, reacts = None, None
        for k in (0, 1):
            a = 2 * x2 + k
            i = a + H1
            plane = e[i]
            beside = (
                (fx[i] * e[i + 1] + fx[i - 1] * e[i - 1])
                + (fyp[i] * rot(plane, -1, 0) + fym[i] * rot(plane, 1, 0))
                + (fzp[i] * rot(plane, -2, 1) + fzm[i] * rot(plane, 2, 1))
            )
            left = (r[i] + beside)[0:8] - g1[a] * plane[0:8]
            total = left if total is None else total + left
            reacts = c1[a] if reacts is None else reacts + c1[a]
        at = pl.multiple_of(x2 * 8, 8)
        tr[pl.ds(at, 8), :] = lane_pairs(total, 2)
        tc[pl.ds(at, 8), :] = lane_pairs(reacts, 2)
        return 0

    lax.fori_loop(0, X1 // 2, down, 0, unroll=2)

    def coarse_p(x2, _):
        t[pl.ds(pl.multiple_of(x2 * YE, 8), YE), :] = lane_pairs(p[2 * x2] + p[2 * x2 + 1], 2)
        return 0

    lax.fori_loop(0, G1 // 2, coarse_p, 0, unroll=2)

    eighth = F32(0.125)
    n2, m2 = X1 // 2, G1 // 2

    def compact(ref, first, rows, stride):
        lane = iota((rows, NL), 1)
        out = None
        for j in range(4):
            value = ref[pl.ds(first + 2 * j, rows, stride=stride), :] + ref[pl.ds(first + 2 * j + 1, rows, stride=stride), :]
            out = value if out is None else jnp.where(lane % 4 == j, value, out)
        return eighth * out

    r2 = compact(tr, 0, n2, 8)
    react2 = compact(tc, 0, n2, 8)
    for k in range(3):
        pc[k] = compact(t, 8 * k, m2, YE)
    h2 = H1 // 2
    centre_p = pc[0, h2 : h2 + n2, :]
    j4 = iota((n2, NL), 1) % 4
    lane = iota((n2, NL), 1)
    high = jnp.where(j4 < 3, rot(centre_p, -1, 1), rot(pc[1, h2 : h2 + n2, :], 3, 1))
    low = jnp.where(j4 > 0, rot(centre_p, 1, 1), rot(pc[2, h2 : h2 + n2, :], -3, 1))
    front = jnp.where(lane >= NL - 4, F32(0.0), rot(centre_p, -4, 1))
    back = jnp.where(lane < 4, F32(0.0), rot(centre_p, 4, 1))
    near = (pc[0, h2 + 1 : h2 + 1 + n2, :] + pc[0, h2 - 1 : h2 - 1 + n2, :]) + (high + low) + (front + back)
    diag2 = F32(0.0625) * (F32(3.0) * centre_p + F32(0.5) * near) + react2
    msg[0:8, :] = r2
    msg[8:16, :] = F32(1.0) / diag2
    msg[16:24, :] = centre_p


def finish(at, got, e, r, d, fx1, fyp1, fym1, fzp1, fzm1,
           u, c, fx, fyp, fym, fzp, fzm, src, scr, free, gy0, gy1, gx0, gx1,
           result,
           e2, p2, r2, d2, k2, tx, eu):
    wx, wy = got.shape[0], got.shape[1]
    rows = wx * 8
    e2[...] = jnp.zeros_like(e2)
    p2[0] = jnp.zeros((rows, NL), F32)
    p2[wy + 1] = jnp.zeros((rows, NL), F32)

    def spread(b, _):
        for a in range(wx):
            r2[b, 8 * a : 8 * a + 8, :] = got[a, b, 0:8, :]
            d2[b, 8 * a : 8 * a + 8, :] = got[a, b, 8:16, :]
            p2[b + 1, 8 * a : 8 * a + 8, :] = got[a, b, 16:24, :]
        return 0

    lax.fori_loop(0, wy, spread, 0)
    sub = iota((rows, NL), 0)
    lane = iota((rows, NL), 1)
    j4 = lane % 4
    parity2 = (sub + j4 + lane // 4) % 2

    def shifted(ref, b):
        plane = ref[b + 1]
        return (
            rot(plane, -1, 0), rot(plane, 1, 0),
            jnp.where(j4 < 3, rot(plane, -1, 1), rot(ref[b + 2], 3, 1)),
            jnp.where(j4 > 0, rot(plane, 1, 1), rot(ref[b], -3, 1)),
            rot(plane, -4, 1), rot(plane, 4, 1),
        )

    edges = (sub == rows - 1, sub == 0, None, None, lane >= NL - 4, lane < 4)

    def begin(b, _):
        plane = p2[b + 1]
        for k, (value, edge) in enumerate(zip(shifted(p2, b), edges, strict=True)):
            face = F32(0.03125) * (plane + value)
            k2[k, b] = face if edge is None else jnp.where(edge, F32(0.0), face)
        e2[b + 1, 0:rows, :] = jnp.where(parity2 == 0, r2[b] * d2[b], F32(0.0))
        return 0

    lax.fori_loop(0, wy, begin, 0)

    def half2(step, _):
        colour = step % 2

        def one(b, _):
            total = r2[b]
            for k, value in enumerate(shifted(e2, b)):
                total = total + k2[k, b] * value
            e2[b + 1] = jnp.where(parity2 == colour, total * d2[b], e2[b + 1])
            return 0

        lax.fori_loop(0, wy, one, 0, unroll=2)
        return 0

    lax.fori_loop(1, 8, half2, 0)

    ox, oy = at[0], at[1]
    for k, step in enumerate((0, 1, -1)):
        b = oy + step + 1
        for m, (dx, first, size, to) in enumerate(((0, 0, 8, 4), (1, 0, 4, 12), (-1, 4, 4, 0))):
            a = ox + dx
            inside = (a >= 0) & (a < wx)
            block = e2[b, pl.ds(pl.multiple_of(jnp.clip(a, 0, wx - 1) * 8, 8), 8), :]
            block = jnp.where(inside, block, F32(0.0))
            l8 = iota((8, NL), 1)
            for j in range(4):
                value = jnp.where(l8 % 4 == 0, rot(block, -j, 1), F32(0.0))
                value = value + rot(value, 1, 1)
                value = value + rot(value, 2, 1)
                for y in (0, 1):
                    tx[pl.ds(to * YE + 8 * k + 2 * j + y, size, stride=YE), :] = value[first : first + size]

    def correct(x2, _):
        value = tx[pl.ds(pl.multiple_of(x2 * YE, 8), YE), :]
        eu[2 * x2] = e[2 * x2] + value
        eu[2 * x2 + 1] = e[2 * x2 + 1] + value
        return 0

    lax.fori_loop(1, G1 // 2 - 1, correct, 0, unroll=2)
    refs1 = (fx1, fyp1, fym1, fzp1, fzm1)
    for k, colour in ((4, 0), (5, 1), (6, 0), (7, 1)):

        def half1(i, _, colour=colour):
            coarse_half(eu, r, d, i, colour, refs1, 2)
            return 0

        lax.fori_loop(k, G1 - k, half1, 0, unroll=4)

    base = X1 * 8 + X1 * 4

    def rows_y(got_, y):
        value = got_[base : base + BX // 2, :]
        u[pl.ds(H0, BX // 2, stride=2), y, :] = value
        u[pl.ds(H0 + 1, BX // 2, stride=2), y, :] = value

    def action_y(hi, lo):
        rows_y((gy0, gy1)[hi], BY + 1)
        rows_y((gy0, gy1)[lo], YE - 2)

    by_parity("gy", action_y)

    def action_x(hi, lo):
        u[H0 + BX + 1, 0:BY, :] = (gx0, gx1)[hi][XMSG - BY : XMSG, :]
        u[H0 - 2, 0:BY, :] = (gx0, gx1)[lo][XMSG - BY : XMSG, :]

    by_parity("gx", action_x)

    def add(k, _):
        plane = eu[k + H1 - 1]
        for y in (0, 1):
            tx[pl.ds(k * YE + y, 8, stride=2), :] = plane[0:8]
        wide = tx[pl.ds(pl.multiple_of(k * YE, 8), BY), :]
        s8 = iota((8, NL), 0)
        hi = plane[8:16]
        lo = plane[16:24]
        halo = jnp.where(s8 < 2, jnp.where(s8 == 0, hi, rot(hi, 1, 0)), jnp.where(s8 == 7, lo, rot(lo, -1, 0)))
        for z in (0, 1):
            i = 2 * k + z + H0 - 2
            u[i, 0:BY, :] = jnp.where(free[i, 0:BY, :] > 0.5, u[i, 0:BY, :] + wide, u[i, 0:BY, :])
            u[i, BY:YE, :] = jnp.where(free[i, BY:YE, :] > 0.5, u[i, BY:YE, :] + halo, u[i, BY:YE, :])
        return 0

    lax.fori_loop(0, X1 + 2, add, 0, unroll=2)
    refs = (c, fx, fyp, fym, fzp, fzm, src, scr, free)

    def third(i, _):
        fine_half(u, i, 0, 1, refs)
        return 0

    lax.fori_loop(2, FX_ - 2, third, 0, unroll=2)

    def last(i, _):
        fine_half(u, i, 1, 1, refs)
        result[pl.ds(pl.multiple_of((i - H0) * BY, 8), BY), :] = u[i, 0:BY, :]
        return 0

    lax.fori_loop(H0, H0 + BX, last, 0, unroll=2)


def swap(pair, axis):
    count = lax.axis_size(axis)
    got = []
    for first, message in enumerate(pair):
        route = []
        for i in range(first, count - 1, 2):
            route += [(i, i + 1), (i + 1, i)]
        got.append(lax.ppermute(message, axis, route))
    return tuple(got)


def body(source, permittivity, screening, potential, fixed_cell):
    gx, gy = lax.axis_size("gx"), lax.axis_size("gy")
    args = [a.reshape(BX * BY, NL) for a in (potential, permittivity, source, screening, fixed_cell)]

    y0 = call(pack_y, (sds(10 * BX, NL),) * 2, name="pack_y")(*args)
    y0 = swap(y0, "gy")
    *halos, x0, x1 = call(pack_x, (sds(BX * 8, NL),) * 5 + (sds(12 * YE, NL),) * 2, name="pack_x")(*args, *y0)
    gotx = swap((x0, x1), "gx")

    ext = (FX_, YE, NL)
    fine = call(
        fine_pre,
        (sds(*ext),) * 10 + (sds(X1, 8, NL),) * 2 + (sds(YMSG, NL),) * 2,
        [
            pltpu.VMEM(ext, F32),
            pltpu.VMEM((X1 * BY, NL), F32),
            pltpu.VMEM((X1 * BY, NL), F32),
            pltpu.VMEM(((X1 + 2) * YE, NL), F32),
            pltpu.VMEM((X1 + 2, 8, NL), F32),
        ],
        name="fine_pre",
    )(*args, *halos, *gotx)
    state, (c1, g1, m0, m1) = fine[:10], fine[10:]
    goty1 = swap((m0, m1), "gy")
    x1msg = call(pack_x1, (sds(XMSG, NL),) * 2, name="pack_x1")(m0, m1, *goty1, state[0])
    gotx1 = swap(x1msg, "gx")

    mid = (G1, YE, NL)
    *level1, message = call(
        mid_pre,
        (sds(*mid),) * 8 + (sds(24, NL),),
        [
            pltpu.VMEM((G1 + 1, YE, NL), F32),
            pltpu.VMEM((G1 // 2 * YE, NL), F32),
            pltpu.VMEM((X1 // 2 * 8, NL), F32),
            pltpu.VMEM((X1 // 2 * 8, NL), F32),
            pltpu.VMEM((3, G1 // 2, NL), F32),
        ],
        name="mid_pre",
    )(m0, *goty1, *gotx1, c1, g1)

    everyone = gx * gy
    gathered = lax.all_to_all(jnp.broadcast_to(message[None], (everyone, 24, NL)), ("gx", "gy"), 0, 0)
    gathered = gathered.reshape(gx, gy, 24, NL)
    wx, wy = min(gx, 5), min(gy, 8)
    ix, iy = lax.axis_index("gx"), lax.axis_index("gy")
    fx = jnp.clip(ix - 2, 0, gx - wx)
    fy = jnp.clip(iy - 3, 0, gy - wy)
    if (wx, wy) != (gx, gy):
        gathered = lax.dynamic_slice(gathered, (fx, fy, 0, 0), (wx, wy, 24, NL))
    at = jnp.stack([ix - fx, iy - fy]).astype(jnp.int32)

    spec = pl.BlockSpec(memory_space=pltpu.VMEM)
    inputs = (gathered, *level1, *state, *goty1, *gotx1)
    result = pl.pallas_call(
        finish_kernel(len(inputs)),
        out_shape=sds(BX * BY, NL),
        in_specs=[pl.BlockSpec(memory_space=pltpu.SMEM)] + [spec] * len(inputs),
        out_specs=spec,
        scratch_shapes=[
            pltpu.VMEM((wy + 2, wx * 8, NL), F32),
            pltpu.VMEM((wy + 2, wx * 8, NL), F32),
            pltpu.VMEM((wy, wx * 8, NL), F32),
            pltpu.VMEM((wy, wx * 8, NL), F32),
            pltpu.VMEM((6, wy, wx * 8, NL), F32),
            pltpu.VMEM(((X1 + 2) * YE, NL), F32),
            pltpu.VMEM(mid, F32),
            pltpu.VMEM(ext, F32),
        ],
        compiler_params=pltpu.CompilerParams(vmem_limit_bytes=24 << 20),
        name="finish",
    )(at, *inputs)
    return result.reshape(BX, BY, NL)


def finish_kernel(count):
    def kernel(*refs):
        at, ins, result, scratch = refs[0], list(refs[1 : 1 + count]), refs[1 + count], list(refs[2 + count :])
        field = scratch.pop()
        before = ins[9]
        field[...] = before[...]
        ins[9] = field
        finish(at, *ins, result, *scratch)

    return kernel


def solution(mesh):
    placed = (P("gx", "gy", None),) * 5
    return jax.shard_map(
        body, mesh=mesh, in_specs=placed, out_specs=P("gx", "gy", None), check_vma=False
    )
```

```python
import jax
import jax.numpy as jnp
from jax import lax
from jax.experimental import pallas as pl
from jax.experimental.pallas import tpu as pltpu
from jax.sharding import PartitionSpec as P

F32 = jnp.float32
BX, BY, NL = 32, 16, 128
H0 = 3
FX_ = BX + 2 * H0
YE = 24
X1 = BX // 2
H1 = 8
G1 = X1 + 2 * H1
GF = 4
GM = 6
LN2 = 0.6931471805599453


def rot(value, shift, axis):
    return pltpu.roll(value, shift % value.shape[axis], axis)


def iota(shape, axis):
    return lax.broadcasted_iota(jnp.int32, shape, axis)


def sds(*shape):
    return jax.ShapeDtypeStruct(shape, F32)


def by_parity(axis, action):
    odd = lax.axis_index(axis) % 2

    @pl.when(odd == 0)
    def _():
        action(0, 1)

    @pl.when(odd == 1)
    def _():
        action(1, 0)


def call(kernel, out_shape, scratch=(), vmem=24, hbm=0):
    specs = {"in_specs": [pl.BlockSpec(memory_space=pltpu.HBM)] * hbm} if hbm else {}
    return pl.pallas_call(
        kernel,
        out_shape=out_shape,
        **specs,
        scratch_shapes=list(scratch),
        compiler_params=pltpu.CompilerParams(vmem_limit_bytes=vmem << 20),
    )


def pack_y(hpot, hper, hsrc, hscr, hfix, pot, per, src, scr, fix, out0, out1, sems):
    outs = (out0, out1)
    pairs = ((hpot, pot), (hper, per), (hsrc, src), (hscr, scr), (hfix, fix))
    copies = [pltpu.make_async_copy(a, b, sems.at[k]) for k, (a, b) in enumerate(pairs)]
    for copy in copies:
        copy.start()
    for copy in copies:
        copy.wait()
    zlane = iota((BX // 2, NL), 1)

    def free_of(value):
        return jnp.where(value == 0, F32(1.0), F32(0.0))

    def row(ref, r):
        return ref[pl.ds(r, BX, stride=BY), :]

    def half(ref, r, parity):
        even = ref[pl.ds(r, BX // 2, stride=2 * BY), :]
        odd = ref[pl.ds(BY + r, BX // 2, stride=2 * BY), :]
        return jnp.where((r + zlane) % 2 == parity, even, odd)

    def side(out, r1, r2, r3):
        rows = [
            row(pot, r1), row(per, r1), row(src, r1), row(scr, r1), free_of(row(fix, r1)),
            row(pot, r2), row(per, r2), free_of(row(fix, r2)),
        ]
        for k, value in enumerate(rows):
            out[BX * k : BX * (k + 1), :] = value
        base = BX * len(rows)
        for k, value in enumerate([half(pot, r3, 1), half(per, r3, 1), half(src, r2, 0), half(scr, r2, 0)]):
            out[base + k * BX // 2 : base + (k + 1) * BX // 2, :] = value

    def action(hi, lo):
        side(outs[hi], BY - 1, BY - 2, BY - 3)
        side(outs[lo], 0, 1, 2)

    by_parity("gy", action)


def pack_x(pot, per, src, scr, fix, got0, got1, hpot, hper, hsrc, hscr, hfree, out0, out1):
    gots, outs = (got0, got1), (out0, out1)
    halos = (hpot, hper, hsrc, hscr, hfree)
    for h in halos:
        h[...] = jnp.zeros_like(h)

    def place(got, slots):
        def whole(ref, k, slot):
            ref[pl.ds(slot, BX, stride=8), :] = got[BX * k : BX * (k + 1), :]

        def halved(ref, k, slot):
            value = got[BX * 8 + k * BX // 2 : BX * 8 + (k + 1) * BX // 2, :]
            ref[pl.ds(slot, BX // 2, stride=16), :] = value
            ref[pl.ds(8 + slot, BX // 2, stride=16), :] = value

        s1, s2, s3 = slots
        for k, ref in enumerate(halos):
            whole(ref, k, s1)
        whole(hpot, 5, s2)
        whole(hper, 6, s2)
        whole(hfree, 7, s2)
        halved(hpot, 0, s3)
        halved(hper, 1, s3)
        halved(hsrc, 2, s2)
        halved(hscr, 3, s2)

    def action_y(hi, lo):
        place(gots[hi], (0, 1, 2))
        place(gots[lo], (7, 6, 5))

    by_parity("gy", action_y)

    def slab(out, planes):
        k = 0
        for ref, h, depth in ((pot, hpot, 3), (per, hper, 3), (src, hsrc, 2), (scr, hscr, 2), (fix, hfree, 2)):
            for x in planes[:depth]:
                own = ref[BY * x : BY * (x + 1), :]
                if ref is fix:
                    own = jnp.where(own == 0, F32(1.0), F32(0.0))
                out[YE * k : YE * k + BY, :] = own
                out[YE * k + BY : YE * (k + 1), :] = h[8 * x : 8 * (x + 1), :]
                k += 1

    def action_x(hi, lo):
        slab(outs[hi], (BX - 1, BX - 2, BX - 3))
        slab(outs[lo], (0, 1, 2))

    by_parity("gx", action_x)


def nonlinear(u, scr):
    up = jnp.exp(u - F32(LN2))
    down = jnp.exp(-u - F32(LN2))
    return scr * (up - down), scr * (up + down)


def beside_of(v, fa, at, n, zstep):
    fx, fyp, fym, fzp, fzm = fa
    here = pl.ds(at, n)
    f = fx[pl.ds(at - 1, n + 1)]
    mid = v[1 : n + 1]
    return (
        (f[1:] * v[2:] + f[:n] * v[:n])
        + (fyp[here] * rot(mid, -1, 1) + fym[here] * rot(mid, 1, 1))
        + (fzp[here] * rot(mid, -zstep, 2) + fzm[here] * rot(mid, zstep, 2))
    )


def checker(at, n, shift, zstep):
    shape = (n, YE, NL)
    return (iota(shape, 0) + iota(shape, 1) + iota(shape, 2) // zstep + (at + shift)) % 2


def planes_of(u, at, n, refs):
    c, fx, fyp, fym, fzp, fzm, src, scr, _ = refs
    here = pl.ds(at, n)
    v = u[pl.ds(at - 1, n + 2)]
    plane = v[1 : n + 1]
    sh, ch = nonlinear(plane, scr[here])
    centre = c[here]
    value = centre * plane - beside_of(v, (fx, fyp, fym, fzp, fzm), at, n, 1) + sh - src[here]
    return plane, value, centre, ch


def fine_half(u, at, n, colour, refs):
    plane, value, centre, ch = planes_of(u, at, n, refs)
    update = plane - value / (centre + ch)
    keep = (checker(at, n, 1, 1) == colour) & (refs[-1][pl.ds(at, n)] > 0.5)
    u[pl.ds(at, n)] = jnp.where(keep, update, plane)


def groups(first, count, n, step):
    assert count % n == 0

    def one(g, _):
        step(first + g * n)
        return 0

    lax.fori_loop(0, count // n, one, 0)


def faces_of(p, at, n, scale, zstep, fx, fyp, fym, fzp, fzm):
    here = pl.ds(at, n)
    lane = iota((n, YE, NL), 2)
    v = p[pl.ds(at, n + 1)]
    plane = v[:n]
    half = F32(0.5 * scale)
    fx[here] = half * (plane + v[1:])
    fyp[here] = half * (plane + rot(plane, -1, 1))
    fym[here] = half * (plane + rot(plane, 1, 1))
    fzp[here] = jnp.where(lane >= NL - zstep, F32(0.0), half * (plane + rot(plane, -zstep, 2)))
    fzm[here] = jnp.where(lane < zstep, F32(0.0), half * (plane + rot(plane, zstep, 2)))


def lane_pairs(value, step):
    lane = iota(value.shape, value.ndim - 1)
    return value + jnp.where((lane // step) % 2 == 0, rot(value, -step, value.ndim - 1), rot(value, step, value.ndim - 1))


def fine_pre(pot, per, src, scr, fix, hpot, hper, hsrc, hscr, hfree, got0, got1,
             u, c, fx, fyp, fym, fzp, fzm, esrc, escr, efree, c1, g1, m0, m1,
             ep, tr, tc, tp, p1):
    gots, outs = (got0, got1), (m0, m1)

    def own(x, _):
        i = x + H0
        at = pl.multiple_of(x * BY, 8)
        ht = pl.multiple_of(x * 8, 8)
        for ref, h, ext in ((pot, hpot, u), (per, hper, ep), (src, hsrc, esrc), (scr, hscr, escr), (fix, hfree, efree)):
            value = ref[pl.ds(at, BY), :]
            if ref is fix:
                value = jnp.where(value == 0, F32(1.0), F32(0.0))
            ext[i, 0:BY, :] = value
            ext[i, BY:YE, :] = h[pl.ds(ht, 8), :]
        return 0

    lax.fori_loop(0, BX, own, 0, unroll=4)

    def place(got, planes):
        k = 0
        for ext, depth in ((u, 3), (ep, 3), (esrc, 2), (escr, 2), (efree, 2)):
            for i in planes[:depth]:
                ext[i] = got[YE * k : YE * (k + 1), :]
                k += 1

    def action_x(hi, lo):
        place(gots[hi], (BX + H0, BX + H0 + 1, BX + H0 + 2))
        place(gots[lo], (H0 - 1, H0 - 2, H0 - 3))

    by_parity("gx", action_x)
    for ext in (esrc, escr, efree):
        ext[0] = jnp.zeros((YE, NL), F32)
        ext[FX_ - 1] = jnp.zeros((YE, NL), F32)

    fx[0] = F32(0.5) * (ep[0] + ep[1])
    refs = (c, fx, fyp, fym, fzp, fzm, esrc, escr, efree)

    def first(at):
        n = GF
        faces_of(ep, at, n, 1.0, 1, fx, fyp, fym, fzp, fzm)
        here = pl.ds(at, n)
        lane = iota((n, YE, NL), 2)
        ends = jnp.where((lane == 0) | (lane == NL - 1), F32(0.5) * ep[here], F32(0.0))
        f = fx[pl.ds(at - 1, n + 1)]
        c[here] = (f[1:] + f[:n]) + (fyp[here] + fym[here]) + (fzp[here] + fzm[here]) + ends
        fine_half(u, at, n, 0, refs)

    groups(1, FX_ - 2, GF, first)
    groups(1, FX_ - 2, GF, lambda at: fine_half(u, at, GF, 1, refs))

    def down(at):
        n = 4
        _, value, _, ch = planes_of(u, at, n, refs)
        left = jnp.where(efree[pl.ds(at, n)] > 0.5, -value, F32(0.0))
        for a in range(0, n, 2):
            to = pl.multiple_of((at - H0 + a) * (BY // 2), 8)
            tr[pl.ds(to, BY), :] = lane_pairs(left[a, 0:BY] + left[a + 1, 0:BY], 1)
            tc[pl.ds(to, BY), :] = lane_pairs(ch[a, 0:BY] + ch[a + 1, 0:BY], 1)

    groups(H0, BX, 4, down)

    def coarse_p(k, _):
        at = pl.multiple_of(k * YE, 8)
        tp[pl.ds(at, YE), :] = lane_pairs(ep[2 * k + 1] + ep[2 * k + 2], 1)
        return 0

    lax.fori_loop(0, X1 + 2, coarse_p, 0, unroll=2)

    eighth = F32(0.125)
    sub = iota((8, NL), 0)
    lane = iota((8, NL), 1)

    def gather_p(k, _):
        p1[k] = eighth * (tp[pl.ds(k * YE, 8, stride=2), :] + tp[pl.ds(k * YE + 1, 8, stride=2), :])
        return 0

    lax.fori_loop(0, X1 + 2, gather_p, 0, unroll=2)

    def make(x1, _):
        k = x1 + 1
        p = p1[k]
        base = k * YE
        high = eighth * (tp[pl.ds(base + 2, 8, stride=2), :] + tp[pl.ds(base + 3, 8, stride=2), :])
        edge = tp[pl.ds(pl.multiple_of(base + 16, 8), 8), :]
        edge = eighth * (edge + rot(edge, 1, 0))
        low = jnp.where(sub == 0, rot(edge, 1, 0), rot(p, 1, 0))
        front = jnp.where(lane >= NL - 2, F32(0.0), rot(p, -2, 1))
        back = jnp.where(lane < 2, F32(0.0), rot(p, 2, 1))
        near = (p1[k + 1] + p1[k - 1]) + (high + low) + (front + back)
        centre = F32(3.0) * p + F32(0.5) * near
        at = x1 * BY
        r = eighth * (tr[pl.ds(at, 8, stride=2), :] + tr[pl.ds(at + 1, 8, stride=2), :])
        react = eighth * (tc[pl.ds(at, 8, stride=2), :] + tc[pl.ds(at + 1, 8, stride=2), :])
        diag = F32(0.25) * centre + react
        c1[x1] = react
        g1[x1] = diag
        message = jnp.where(lane % 2 == 0, r, F32(1.0) / diag)
        m0[pl.ds(pl.multiple_of(x1 * 8, 8), 8), :] = message
        m1[pl.ds(pl.multiple_of(x1 * 8, 8), 8), :] = message
        return 0

    lax.fori_loop(0, X1, make, 0, unroll=2)

    for a in range(X1 // 2):
        message = jnp.where(lane % 2 == 0, p1[1 + 2 * a], p1[2 + 2 * a])
        for m in outs:
            m[X1 * 8 + 8 * a : X1 * 8 + 8 * a + 8, :] = message

    zl = iota((BX // 2, NL), 1)
    base = X1 * 8 + X1 * 4

    def odd_row(out, y):
        even = u[pl.ds(H0, BX // 2, stride=2), y, :]
        odd = u[pl.ds(H0 + 1, BX // 2, stride=2), y, :]
        out[base : base + BX // 2, :] = jnp.where((y + zl) % 2 == 1, even, odd)

    def action_y(hi, lo):
        odd_row(outs[hi], BY - 2)
        odd_row(outs[lo], 1)

    by_parity("gy", action_y)


YMSG = X1 * 8 + X1 * 4 + BX // 2
XMSG = H1 * YE + (H1 // 2) * YE + BY


def pack_x1(m0, m1, got0, got1, u, out0, out1):
    own, gots, outs = m0, (got0, got1), (out0, out1)
    odd_y = lax.axis_index("gy") % 2

    def go(hi, lo):
        def slab(out, first, x):
            at = 0
            for a in range(H1):
                for ref in (own, gots[hi], gots[lo]):
                    out[at : at + 8, :] = ref[8 * (first + a) : 8 * (first + a) + 8, :]
                    at += 8
            for a in range(H1 // 2):
                row = X1 * 8 + 8 * (first // 2 + a)
                for ref in (own, gots[hi], gots[lo]):
                    out[at : at + 8, :] = ref[row : row + 8, :]
                    at += 8
            out[at : at + BY, :] = u[x + H0, 0:BY, :]

        def action(xhi, xlo):
            slab(outs[xhi], X1 - H1, BX - 2)
            slab(outs[xlo], 0, 1)

        by_parity("gx", action)

    @pl.when(odd_y == 0)
    def _():
        go(0, 1)

    @pl.when(odd_y == 1)
    def _():
        go(1, 0)


def coarse_half(e, r, d, at, n, colour, refs, zstep):
    v = e[pl.ds(at - 1, n + 2)]
    here = pl.ds(at, n)
    update = (r[here] + beside_of(v, refs, at, n, zstep)) * d[here]
    e[here] = jnp.where(checker(at, n, 0, zstep) == colour, update, v[1 : n + 1])


def dup_even(value):
    lane = iota(value.shape, value.ndim - 1)
    return jnp.where(lane % 2 == 0, value, rot(value, 1, value.ndim - 1))


def dup_odd(value):
    lane = iota(value.shape, value.ndim - 1)
    return jnp.where(lane % 2 == 1, value, rot(value, -1, value.ndim - 1))


def mid_pre(m0, gy0, gy1, gx0, gx1, c1, g1,
            e, r, d, fx, fyp, fym, fzp, fzm, msg,
            p, t, tr, tc, pc):
    gys, gxs = (gy0, gy1), (gx0, gx1)
    odd_y = lax.axis_index("gy") % 2

    def own(hi, lo):
        def planes(a, _):
            rows = [ref[pl.ds(pl.multiple_of(8 * a, 8), 8), :] for ref in (m0, gys[hi], gys[lo])]
            for k, value in enumerate(rows):
                r[H1 + a, 8 * k : 8 * k + 8, :] = dup_even(value)
                d[H1 + a, 8 * k : 8 * k + 8, :] = dup_odd(value)
            return 0

        lax.fori_loop(0, X1, planes, 0, unroll=2)

        def coefs(a, _):
            at = pl.multiple_of(X1 * 8 + 8 * a, 8)
            for k, ref in enumerate((m0, gys[hi], gys[lo])):
                value = ref[pl.ds(at, 8), :]
                p[H1 + 2 * a, 8 * k : 8 * k + 8, :] = dup_even(value)
                p[H1 + 2 * a + 1, 8 * k : 8 * k + 8, :] = dup_odd(value)
            return 0

        lax.fori_loop(0, X1 // 2, coefs, 0, unroll=2)

    @pl.when(odd_y == 0)
    def _():
        own(0, 1)

    @pl.when(odd_y == 1)
    def _():
        own(1, 0)

    def beyond(ref, first):
        def planes(a, _):
            value = ref[pl.ds(pl.multiple_of(YE * a, 8), YE), :]
            r[first + a] = dup_even(value)
            d[first + a] = dup_odd(value)
            return 0

        lax.fori_loop(0, H1, planes, 0, unroll=2)
        for a in range(H1 // 2):
            value = ref[H1 * YE + YE * a : H1 * YE + YE * (a + 1), :]
            p[first + 2 * a] = dup_even(value)
            p[first + 2 * a + 1] = dup_odd(value)

    def action(hi, lo):
        beyond(gxs[hi], H1 + X1)
        beyond(gxs[lo], 0)

    by_parity("gx", action)

    p[G1] = jnp.zeros((YE, NL), F32)
    refs = (fx, fyp, fym, fzp, fzm)

    def begin(at):
        n = 4
        here = pl.ds(at, n)
        faces_of(p, at, n, 0.25, 2, fx, fyp, fym, fzp, fzm)
        e[here] = jnp.where(checker(at, n, 0, 2) == 0, r[here] * d[here], F32(0.0))

    groups(0, G1, 4, begin)
    for colour in (1, 0, 1):
        groups(1, G1 - 2, GM, lambda at, colour=colour: coarse_half(e, r, d, at, GM, colour, refs, 2))

    def down(at):
        n = 4
        v = e[pl.ds(at - 1, n + 2)]
        here = pl.ds(at, n)
        left = (r[here] + beside_of(v, refs, at, n, 2))[:, 0:8] - g1[pl.ds(at - H1, n)] * v[1 : n + 1, 0:8]
        react = c1[pl.ds(at - H1, n)]
        for a in range(0, n, 2):
            to = pl.multiple_of((at - H1 + a) * 4, 8)
            tr[pl.ds(to, 8), :] = lane_pairs(left[a] + left[a + 1], 2)
            tc[pl.ds(to, 8), :] = lane_pairs(react[a] + react[a + 1], 2)

    groups(H1, X1, 4, down)

    def coarse_p(x2, _):
        t[pl.ds(pl.multiple_of(x2 * YE, 8), YE), :] = lane_pairs(p[2 * x2] + p[2 * x2 + 1], 2)
        return 0

    lax.fori_loop(0, G1 // 2, coarse_p, 0, unroll=2)

    eighth = F32(0.125)
    n2, m2 = X1 // 2, G1 // 2

    def compact(ref, first, rows, stride):
        lane = iota((rows, NL), 1)
        out = None
        for j in range(4):
            value = ref[pl.ds(first + 2 * j, rows, stride=stride), :] + ref[pl.ds(first + 2 * j + 1, rows, stride=stride), :]
            out = value if out is None else jnp.where(lane % 4 == j, value, out)
        return eighth * out

    r2 = compact(tr, 0, n2, 8)
    react2 = compact(tc, 0, n2, 8)
    for k in range(3):
        pc[k] = compact(t, 8 * k, m2, YE)
    h2 = H1 // 2
    centre_p = pc[0, h2 : h2 + n2, :]
    j4 = iota((n2, NL), 1) % 4
    lane = iota((n2, NL), 1)
    high = jnp.where(j4 < 3, rot(centre_p, -1, 1), rot(pc[1, h2 : h2 + n2, :], 3, 1))
    low = jnp.where(j4 > 0, rot(centre_p, 1, 1), rot(pc[2, h2 : h2 + n2, :], -3, 1))
    front = jnp.where(lane >= NL - 4, F32(0.0), rot(centre_p, -4, 1))
    back = jnp.where(lane < 4, F32(0.0), rot(centre_p, 4, 1))
    near = (pc[0, h2 + 1 : h2 + 1 + n2, :] + pc[0, h2 - 1 : h2 - 1 + n2, :]) + (high + low) + (front + back)
    diag2 = F32(0.0625) * (F32(3.0) * centre_p + F32(0.5) * near) + react2
    inverse2 = F32(1.0) / diag2

    def every(k, _):
        msg[k, 0:8, :] = r2
        msg[k, 8:16, :] = inverse2
        msg[k, 16:24, :] = centre_p
        return 0

    lax.fori_loop(0, msg.shape[0], every, 0)


def finish(at, got, e, r, d, fx1, fyp1, fym1, fzp1, fzm1,
           u, c, fx, fyp, fym, fzp, fzm, src, scr, free, gy0, gy1, gx0, gx1,
           result,
           e2, p2, r2, d2, k2, tx, eu):
    wx, wy = got.shape[0], got.shape[1]
    rows = wx * 8
    e2[...] = jnp.zeros_like(e2)
    p2[0] = jnp.zeros((rows, NL), F32)
    p2[wy + 1] = jnp.zeros((rows, NL), F32)

    def spread(b, _):
        for a in range(wx):
            r2[b, 8 * a : 8 * a + 8, :] = got[a, b, 0:8, :]
            d2[b, 8 * a : 8 * a + 8, :] = got[a, b, 8:16, :]
            p2[b + 1, 8 * a : 8 * a + 8, :] = got[a, b, 16:24, :]
        return 0

    lax.fori_loop(0, wy, spread, 0)
    sub = iota((rows, NL), 0)
    lane = iota((rows, NL), 1)
    j4 = lane % 4
    parity2 = (sub + j4 + lane // 4) % 2

    span = 4 if wy % 4 == 0 else 1

    def shifted(v):
        mid = v[1 : span + 1]
        near = j4[None] < 3
        return (
            rot(mid, -1, 1), rot(mid, 1, 1),
            jnp.where(near, rot(mid, -1, 2), rot(v[2:], 3, 2)),
            jnp.where(j4[None] > 0, rot(mid, 1, 2), rot(v[:span], -3, 2)),
            rot(mid, -4, 2), rot(mid, 4, 2),
        )

    edges = (sub == rows - 1, sub == 0, None, None, lane >= NL - 4, lane < 4)

    def begin(b):
        here = pl.ds(b, span)
        v = p2[pl.ds(b, span + 2)]
        for k, (value, edge) in enumerate(zip(shifted(v), edges, strict=True)):
            face = F32(0.03125) * (v[1 : span + 1] + value)
            k2[k, here] = face if edge is None else jnp.where(edge[None], F32(0.0), face)
        e2[pl.ds(b + 1, span)] = jnp.where(parity2[None] == 0, r2[here] * d2[here], F32(0.0))

    groups(0, wy, span, begin)

    def half2(step, _):
        colour = step % 2

        def one(b):
            here = pl.ds(b, span)
            v = e2[pl.ds(b, span + 2)]
            total = r2[here]
            for k, value in enumerate(shifted(v)):
                total = total + k2[k, here] * value
            e2[pl.ds(b + 1, span)] = jnp.where(parity2[None] == colour, total * d2[here], v[1 : span + 1])

        groups(0, wy, span, one)
        return 0

    lax.fori_loop(1, 8, half2, 0)

    ox, oy = at[0], at[1]
    for k, step in enumerate((0, 1, -1)):
        b = oy + step + 1
        for dx, first, size, to in ((0, 0, 8, 4), (1, 0, 4, 12), (-1, 4, 4, 0)):
            a = ox + dx
            inside = (a >= 0) & (a < wx)
            block = e2[b, pl.ds(pl.multiple_of(jnp.clip(a, 0, wx - 1) * 8, 8), 8), :]
            block = jnp.where(inside, block, F32(0.0))
            l8 = iota((8, NL), 1)
            for j in range(4):
                value = jnp.where(l8 % 4 == 0, rot(block, -j, 1), F32(0.0))
                value = value + rot(value, 1, 1)
                value = value + rot(value, 2, 1)
                for y in (0, 1):
                    tx[pl.ds(to * YE + 8 * k + 2 * j + y, size, stride=YE), :] = value[first : first + size]

    def correct(x2, _):
        value = tx[pl.ds(pl.multiple_of(x2 * YE, 8), YE), :]
        eu[2 * x2] = e[2 * x2] + value
        eu[2 * x2 + 1] = e[2 * x2 + 1] + value
        return 0

    lax.fori_loop(1, G1 // 2 - 1, correct, 0, unroll=2)
    refs1 = (fx1, fyp1, fym1, fzp1, fzm1)
    for first, count, colour in ((4, 24, 0), (4, 24, 1), (4, 24, 0), (7, 18, 1)):
        groups(first, count, GM, lambda at, colour=colour: coarse_half(eu, r, d, at, GM, colour, refs1, 2))

    base = X1 * 8 + X1 * 4

    def rows_y(got_, y):
        value = got_[base : base + BX // 2, :]
        u[pl.ds(H0, BX // 2, stride=2), y, :] = value
        u[pl.ds(H0 + 1, BX // 2, stride=2), y, :] = value

    def action_y(hi, lo):
        rows_y((gy0, gy1)[hi], BY + 1)
        rows_y((gy0, gy1)[lo], YE - 2)

    by_parity("gy", action_y)

    def action_x(hi, lo):
        u[H0 + BX + 1, 0:BY, :] = (gx0, gx1)[hi][XMSG - BY : XMSG, :]
        u[H0 - 2, 0:BY, :] = (gx0, gx1)[lo][XMSG - BY : XMSG, :]

    by_parity("gx", action_x)

    def add(k, _):
        plane = eu[k + H1 - 1]
        for y in (0, 1):
            tx[pl.ds(k * YE + y, 8, stride=2), :] = plane[0:8]
        wide = tx[pl.ds(pl.multiple_of(k * YE, 8), BY), :]
        s8 = iota((8, NL), 0)
        hi = plane[8:16]
        lo = plane[16:24]
        halo = jnp.where(s8 < 2, jnp.where(s8 == 0, hi, rot(hi, 1, 0)), jnp.where(s8 == 7, lo, rot(lo, -1, 0)))
        for z in (0, 1):
            i = 2 * k + z + H0 - 2
            u[i, 0:BY, :] = jnp.where(free[i, 0:BY, :] > 0.5, u[i, 0:BY, :] + wide, u[i, 0:BY, :])
            u[i, BY:YE, :] = jnp.where(free[i, BY:YE, :] > 0.5, u[i, BY:YE, :] + halo, u[i, BY:YE, :])
        return 0

    lax.fori_loop(0, X1 + 2, add, 0, unroll=2)
    refs = (c, fx, fyp, fym, fzp, fzm, src, scr, free)

    groups(1, FX_ - 2, GF, lambda at: fine_half(u, at, GF, 0, refs))

    def last(at):
        n = 4
        plane, value, centre, ch = planes_of(u, at, n, refs)
        update = plane - value / (centre + ch)
        keep = (checker(at, n, 1, 1) == 1) & (free[pl.ds(at, n)] > 0.5)
        out = jnp.where(keep, update, plane)[:, 0:BY]
        result[pl.ds(pl.multiple_of((at - H0) * BY, 8), n * BY), :] = out.reshape(n * BY, NL)

    groups(H0, BX, 4, last)


def swap(pair, axis):
    count = lax.axis_size(axis)
    got = [None, None]
    for first in (1, 0):
        route = []
        for i in range(first, count - 1, 2):
            route += [(i, i + 1), (i + 1, i)]
        got[first] = lax.ppermute(pair[first], axis, route)
    return tuple(got)


def body(source, permittivity, screening, potential, fixed_cell):
    gx, gy = lax.axis_size("gx"), lax.axis_size("gy")
    args = [a.reshape(BX * BY, NL) for a in (potential, permittivity, source, screening, fixed_cell)]
    args = [pltpu.with_memory_space_constraint(a, pltpu.HBM) for a in args]

    whole = (sds(BX * BY, NL),) * 4 + (jax.ShapeDtypeStruct((BX * BY, NL), jnp.int32),)
    *args, y0, y1 = call(pack_y, whole + (sds(10 * BX, NL),) * 2, [pltpu.SemaphoreType.DMA((5,))], hbm=5)(*args)
    y0 = (y0, y1)
    y0 = swap(y0, "gy")
    *halos, x0, x1 = call(pack_x, (sds(BX * 8, NL),) * 5 + (sds(12 * YE, NL),) * 2)(*args, *y0)
    gotx = swap((x0, x1), "gx")

    ext = (FX_, YE, NL)
    fine = call(
        fine_pre,
        (sds(*ext),) * 10 + (sds(X1, 8, NL),) * 2 + (sds(YMSG, NL),) * 2,
        [
            pltpu.VMEM(ext, F32),
            pltpu.VMEM((X1 * BY, NL), F32),
            pltpu.VMEM((X1 * BY, NL), F32),
            pltpu.VMEM(((X1 + 2) * YE, NL), F32),
            pltpu.VMEM((X1 + 2, 8, NL), F32),
        ],
    )(*args, *halos, *gotx)
    state, (c1, g1, m0, m1) = fine[:10], fine[10:]
    goty1 = swap((m0, m1), "gy")
    x1msg = call(pack_x1, (sds(XMSG, NL),) * 2)(m0, m1, *goty1, state[0])
    gotx1 = swap(x1msg, "gx")

    mid = (G1, YE, NL)
    *level1, message = call(
        mid_pre,
        (sds(*mid),) * 8 + (sds(gx * gy, 24, NL),),
        [
            pltpu.VMEM((G1 + 1, YE, NL), F32),
            pltpu.VMEM((G1 // 2 * YE, NL), F32),
            pltpu.VMEM((X1 // 2 * 8, NL), F32),
            pltpu.VMEM((X1 // 2 * 8, NL), F32),
            pltpu.VMEM((3, G1 // 2, NL), F32),
        ],
    )(m0, *goty1, *gotx1, c1, g1)

    gathered = lax.all_to_all(message, ("gx", "gy"), 0, 0).reshape(gx, gy, 24, NL)
    wx, wy = min(gx, 5), min(gy, 8)
    if (wx, wy) != (gx, gy):
        first = (*window(gx, gy, wx, wy)[:2], 0, 0)
        gathered = lax.dynamic_slice(gathered, first, (wx, wy, 24, NL))

    inputs = (gathered, *level1, *state, *goty1, *gotx1)
    result = pl.pallas_call(
        finish_kernel(len(inputs), (gx, gy, wx, wy)),
        out_shape=sds(BX * BY, NL),
        scratch_shapes=[
            pltpu.VMEM((wy + 2, wx * 8, NL), F32),
            pltpu.VMEM((wy + 2, wx * 8, NL), F32),
            pltpu.VMEM((wy, wx * 8, NL), F32),
            pltpu.VMEM((wy, wx * 8, NL), F32),
            pltpu.VMEM((6, wy, wx * 8, NL), F32),
            pltpu.VMEM(((X1 + 2) * YE, NL), F32),
            pltpu.VMEM(mid, F32),
            pltpu.VMEM(ext, F32),
        ],
        compiler_params=pltpu.CompilerParams(vmem_limit_bytes=24 << 20),
        name="finish",
    )(*inputs)
    return result.reshape(BX, BY, NL)


def window(gx, gy, wx, wy):
    ix, iy = lax.axis_index("gx"), lax.axis_index("gy")
    fx = jnp.clip(ix - 2, 0, gx - wx)
    fy = jnp.clip(iy - 3, 0, gy - wy)
    return fx, fy, ix - fx, iy - fy


def finish_kernel(count, sizes):
    def kernel(*refs):
        ins, result, scratch = list(refs[:count]), refs[count], list(refs[1 + count :])
        field = scratch.pop()
        before = ins[9]
        field[...] = before[...]
        ins[9] = field
        finish(window(*sizes)[2:], *ins, result, *scratch)

    return kernel


def solution(mesh):
    placed = (P("gx", "gy", None),) * 5

    return jax.shard_map(body, mesh=mesh, in_specs=placed, out_specs=P("gx", "gy", None), check_vma=False)
```

```python
import jax
import jax.numpy as jnp
from jax import lax
from jax.experimental import pallas as pl
from jax.experimental.pallas import tpu as pltpu
from jax.sharding import PartitionSpec as P

F32 = jnp.float32
BX, BY, NL = 32, 16, 128
YE = 24
X1 = BX // 2
H1 = 8
G1 = X1 + 2 * H1
NF = X1 + 4
NM = G1 // 2 + 2
GF = 3
GM = 4
LN2 = 0.6931471805599453


def rot(value, shift, axis):
    return pltpu.roll(value, shift % value.shape[axis], axis)


def iota(shape, axis):
    return lax.broadcasted_iota(jnp.int32, shape, axis)


def sds(*shape):
    return jax.ShapeDtypeStruct(shape, F32)


def by_parity(axis, action):
    odd = lax.axis_index(axis) % 2

    @pl.when(odd == 0)
    def _():
        action(0, 1)

    @pl.when(odd == 1)
    def _():
        action(1, 0)


def call(kernel, out_shape, scratch=(), vmem=24, hbm=0):
    specs = {"in_specs": [pl.BlockSpec(memory_space=pltpu.HBM)] * hbm} if hbm else {}
    return pl.pallas_call(
        kernel,
        out_shape=out_shape,
        **specs,
        scratch_shapes=list(scratch),
        compiler_params=pltpu.CompilerParams(vmem_limit_bytes=vmem << 20),
    )


def pack_y(hpot, hper, hsrc, hscr, hfix, pot, per, src, scr, fix, out0, out1, sems):
    outs = (out0, out1)
    pairs = ((hpot, pot), (hper, per), (hsrc, src), (hscr, scr), (hfix, fix))
    copies = [pltpu.make_async_copy(a, b, sems.at[k]) for k, (a, b) in enumerate(pairs)]
    for copy in copies:
        copy.start()
    for copy in copies:
        copy.wait()
    zlane = iota((BX // 2, NL), 1)

    def free_of(value):
        return jnp.where(value == 0, F32(1.0), F32(0.0))

    def row(ref, r):
        return ref[pl.ds(r, BX, stride=BY), :]

    def half(ref, r, parity):
        even = ref[pl.ds(r, BX // 2, stride=2 * BY), :]
        odd = ref[pl.ds(BY + r, BX // 2, stride=2 * BY), :]
        return jnp.where((r + zlane) % 2 == parity, even, odd)

    def side(out, r1, r2, r3):
        rows = [
            row(pot, r1), row(per, r1), row(src, r1), row(scr, r1), free_of(row(fix, r1)),
            row(pot, r2), row(per, r2), free_of(row(fix, r2)),
        ]
        for k, value in enumerate(rows):
            out[BX * k : BX * (k + 1), :] = value
        base = BX * len(rows)
        for k, value in enumerate([half(pot, r3, 1), half(per, r3, 1), half(src, r2, 0), half(scr, r2, 0)]):
            out[base + k * BX // 2 : base + (k + 1) * BX // 2, :] = value

    def action(hi, lo):
        side(outs[hi], BY - 1, BY - 2, BY - 3)
        side(outs[lo], 0, 1, 2)

    by_parity("gy", action)


def pack_x(pot, per, src, scr, fix, got0, got1, hpot, hper, hsrc, hscr, hfree, out0, out1):
    gots, outs = (got0, got1), (out0, out1)
    halos = (hpot, hper, hsrc, hscr, hfree)
    for h in halos:
        h[...] = jnp.zeros_like(h)

    def place(got, slots):
        def whole(ref, k, slot):
            ref[pl.ds(slot, BX, stride=8), :] = got[BX * k : BX * (k + 1), :]

        def halved(ref, k, slot):
            value = got[BX * 8 + k * BX // 2 : BX * 8 + (k + 1) * BX // 2, :]
            ref[pl.ds(slot, BX // 2, stride=16), :] = value
            ref[pl.ds(8 + slot, BX // 2, stride=16), :] = value

        s1, s2, s3 = slots
        for k, ref in enumerate(halos):
            whole(ref, k, s1)
        whole(hpot, 5, s2)
        whole(hper, 6, s2)
        whole(hfree, 7, s2)
        halved(hpot, 0, s3)
        halved(hper, 1, s3)
        halved(hsrc, 2, s2)
        halved(hscr, 3, s2)

    def action_y(hi, lo):
        place(gots[hi], (0, 1, 2))
        place(gots[lo], (7, 6, 5))

    by_parity("gy", action_y)

    def slab(out, planes):
        k = 0
        for ref, h, depth in ((pot, hpot, 3), (per, hper, 3), (src, hsrc, 2), (scr, hscr, 2), (fix, hfree, 2)):
            for x in planes[:depth]:
                own = ref[BY * x : BY * (x + 1), :]
                if ref is fix:
                    own = jnp.where(own == 0, F32(1.0), F32(0.0))
                out[YE * k : YE * k + BY, :] = own
                out[YE * k + BY : YE * (k + 1), :] = h[8 * x : 8 * (x + 1), :]
                k += 1

    def action_x(hi, lo):
        slab(outs[hi], (BX - 1, BX - 2, BX - 3))
        slab(outs[lo], (0, 1, 2))

    by_parity("gx", action_x)


def nonlinear(u, scr):
    up = jnp.exp(u - F32(LN2))
    down = jnp.exp(-u - F32(LN2))
    return scr * (up - down), scr * (up + down)


def colour_mask(n, zstep):
    shape = (n, YE, NL)
    return (iota(shape, 1) + iota(shape, 2) // zstep) % 2 == 0


def beside_of(other, colour, faces, at, n, zstep):
    fin, fout, fyp, fym, fzp, fzm = faces
    here = pl.ds(at, n)
    v = other[1 - colour, pl.ds(at - 1, n + 2)]
    mid = v[1 : n + 1]
    first = colour_mask(n, zstep)
    across = jnp.where(first, v[:n], v[2:]) if colour == 0 else jnp.where(first, v[2:], v[:n])
    return (
        (fin[here] * mid + fout[colour, here] * across)
        + (fyp[colour, here] * rot(mid, -1, 1) + fym[colour, here] * rot(mid, 1, 1))
        + (fzp[colour, here] * rot(mid, -zstep, 2) + fzm[colour, here] * rot(mid, zstep, 2))
    )


def pairs_of(u, at, n, colour, refs):
    c, fin, fout, fyp, fym, fzp, fzm, src, scr, _ = refs
    here = pl.ds(at, n)
    plane = u[colour, here]
    sh, ch = nonlinear(plane, scr[colour, here])
    centre = c[colour, here]
    beside = beside_of(u, colour, (fin, fout, fyp, fym, fzp, fzm), at, n, 1)
    return plane, centre * plane - beside + sh - src[colour, here], centre, ch


def fine_new(u, at, n, colour, refs):
    plane, value, centre, ch = pairs_of(u, at, n, colour, refs)
    return jnp.where(refs[-1][colour, pl.ds(at, n)] > 0.5, plane - value / (centre + ch), plane)


def fine_half(u, at, n, colour, refs):
    u[colour, pl.ds(at, n)] = fine_new(u, at, n, colour, refs)


def groups(first, count, n, step):
    assert count % n == 0

    def one(g, _):
        step(first + g * n)
        return 0

    lax.fori_loop(0, count // n, one, 0)


def faces_of(p, at, n, scale, zstep, fin, fout, fyp, fym, fzp, fzm):
    here = pl.ds(at, n)
    lane = iota((n, YE, NL), 2)
    first = colour_mask(n, zstep)
    half = F32(0.5 * scale)
    for colour in (0, 1):
        plane = p[colour, here]
        v = p[1 - colour, pl.ds(at - 1, n + 2)]
        mid = v[1 : n + 1]
        across = jnp.where(first, v[:n], v[2:]) if colour == 0 else jnp.where(first, v[2:], v[:n])
        if colour == 0:
            fin[here] = half * (plane + mid)
        fout[colour, here] = half * (plane + across)
        fyp[colour, here] = half * (plane + rot(mid, -1, 1))
        fym[colour, here] = half * (plane + rot(mid, 1, 1))
        fzp[colour, here] = jnp.where(lane >= NL - zstep, F32(0.0), half * (plane + rot(mid, -zstep, 2)))
        fzm[colour, here] = jnp.where(lane < zstep, F32(0.0), half * (plane + rot(mid, zstep, 2)))


def lane_pairs(value, step):
    lane = iota(value.shape, value.ndim - 1)
    return value + jnp.where((lane // step) % 2 == 0, rot(value, -step, value.ndim - 1), rot(value, step, value.ndim - 1))


def fine_pre(pot, per, src, scr, fix, hpot, hper, hsrc, hscr, hfree, got0, got1,
             u, c, fin, fout, fyp, fym, fzp, fzm, esrc, escr, efree, csum, g1, m0, m1,
             ep, tr, tc, tp, p1):
    gots, outs = (got0, got1), (m0, m1)
    first = colour_mask(1, 1)[0]

    def own(k, _):
        for ref, h, ext in ((pot, hpot, u), (per, hper, ep), (src, hsrc, esrc), (scr, hscr, escr), (fix, hfree, efree)):
            value = ref[pl.ds(pl.multiple_of(2 * k * BY, 8), 2 * BY), :]
            if ref is fix:
                value = jnp.where(value == 0, F32(1.0), F32(0.0))
            halo = h[pl.ds(pl.multiple_of(16 * k, 8), 16), :]
            for rows, one, two in (
                (slice(0, BY), value[:BY], value[BY:]),
                (slice(BY, YE), halo[:8], halo[8:]),
            ):
                ext[0, k + 2, rows, :] = jnp.where(first[rows], one, two)
                ext[1, k + 2, rows, :] = jnp.where(first[rows], two, one)
        return 0

    lax.fori_loop(0, X1, own, 0, unroll=2)

    def place(got, near, far, flip):
        k = 0
        for ext, depth in ((u, 3), (ep, 3), (esrc, 2), (escr, 2), (efree, 2)):
            planes = [got[YE * (k + j) : YE * (k + j + 1), :] for j in range(depth)]
            k += depth
            one, two = (planes[1], planes[0]) if flip else (planes[0], planes[1])
            ext[0, near] = jnp.where(first, one, two)
            ext[1, near] = jnp.where(first, two, one)
            third = planes[2] if depth == 3 else jnp.zeros((YE, NL), F32)
            ext[0, far] = third
            ext[1, far] = third

    def action_x(hi, lo):
        place(gots[hi], X1 + 2, X1 + 3, False)
        place(gots[lo], 1, 0, True)

    by_parity("gx", action_x)
    refs = (c, fin, fout, fyp, fym, fzp, fzm, esrc, escr, efree)

    def begin(at):
        n = GF
        faces_of(ep, at, n, 1.0, 1, fin, fout, fyp, fym, fzp, fzm)
        here = pl.ds(at, n)
        lane = iota((n, YE, NL), 2)
        for colour in (0, 1):
            ends = jnp.where((lane == 0) | (lane == NL - 1), F32(0.5) * ep[colour, here], F32(0.0))
            c[colour, here] = (
                (fin[here] + fout[colour, here]) + (fyp[colour, here] + fym[colour, here])
                + (fzp[colour, here] + fzm[colour, here]) + ends
            )
        fine_half(u, at, n, 0, refs)

    groups(1, X1 + 2, GF, begin)
    groups(1, X1 + 2, GF, lambda at: fine_half(u, at, GF, 1, refs))

    def down(at):
        n = 2
        left, react = F32(0.0), F32(0.0)
        for colour in (0, 1):
            _, value, _, ch = pairs_of(u, at, n, colour, refs)
            left += jnp.where(efree[colour, pl.ds(at, n)] > 0.5, -value, F32(0.0))
            react += ch
        to = pl.multiple_of((at - 2) * BY, 8)
        tr[pl.ds(to, n * BY), :] = lane_pairs(left[:, 0:BY], 1).reshape(n * BY, NL)
        tc[pl.ds(to, n * BY), :] = lane_pairs(react[:, 0:BY], 1).reshape(n * BY, NL)

    groups(2, X1, 2, down)

    def coarse_p(k, _):
        at = pl.multiple_of(k * YE, 8)
        tp[pl.ds(at, YE), :] = lane_pairs(ep[0, k + 1] + ep[1, k + 1], 1)
        return 0

    lax.fori_loop(0, X1 + 2, coarse_p, 0, unroll=2)

    eighth = F32(0.125)
    sub = iota((8, NL), 0)
    lane = iota((8, NL), 1)

    def gather_p(k, _):
        p1[k] = eighth * (tp[pl.ds(k * YE, 8, stride=2), :] + tp[pl.ds(k * YE + 1, 8, stride=2), :])
        return 0

    lax.fori_loop(0, X1 + 2, gather_p, 0, unroll=2)

    first8 = (sub + lane // 2) % 2 == 0

    def coarse(x1):
        k = x1 + 1
        p = p1[k]
        base = k * YE
        high = eighth * (tp[pl.ds(base + 2, 8, stride=2), :] + tp[pl.ds(base + 3, 8, stride=2), :])
        edge = tp[pl.ds(pl.multiple_of(base + 16, 8), 8), :]
        edge = eighth * (edge + rot(edge, 1, 0))
        low = jnp.where(sub == 0, rot(edge, 1, 0), rot(p, 1, 0))
        front = jnp.where(lane >= NL - 2, F32(0.0), rot(p, -2, 1))
        back = jnp.where(lane < 2, F32(0.0), rot(p, 2, 1))
        near = (p1[k + 1] + p1[k - 1]) + (high + low) + (front + back)
        centre = F32(3.0) * p + F32(0.5) * near
        at = x1 * BY
        r = eighth * (tr[pl.ds(at, 8, stride=2), :] + tr[pl.ds(at + 1, 8, stride=2), :])
        react = eighth * (tc[pl.ds(at, 8, stride=2), :] + tc[pl.ds(at + 1, 8, stride=2), :])
        diag = F32(0.25) * centre + react
        message = jnp.where(lane % 2 == 0, r, F32(1.0) / diag)
        m0[pl.ds(pl.multiple_of(x1 * 8, 8), 8), :] = message
        m1[pl.ds(pl.multiple_of(x1 * 8, 8), 8), :] = message
        return diag, react

    def make(k, _):
        diag0, react0 = coarse(2 * k)
        diag1, react1 = coarse(2 * k + 1)
        csum[k] = react0 + react1
        g1[0, k] = jnp.where(first8, diag0, diag1)
        g1[1, k] = jnp.where(first8, diag1, diag0)
        return 0

    lax.fori_loop(0, X1 // 2, make, 0)

    for a in range(X1 // 2):
        message = jnp.where(lane % 2 == 0, p1[1 + 2 * a], p1[2 + 2 * a])
        for m in outs:
            m[X1 * 8 + 8 * a : X1 * 8 + 8 * a + 8, :] = message

    base = X1 * 8 + X1 * 4

    def odd_row(out, y):
        out[base : base + X1, :] = u[1, pl.ds(2, X1), y, :]

    def action_y(hi, lo):
        odd_row(outs[hi], BY - 2)
        odd_row(outs[lo], 1)

    by_parity("gy", action_y)


YMSG = X1 * 8 + X1 * 4 + BX // 2
XMSG = H1 * YE + (H1 // 2) * YE + BY


def pack_x1(m0, m1, got0, got1, u, out0, out1):
    own, gots, outs = m0, (got0, got1), (out0, out1)
    odd_y = lax.axis_index("gy") % 2

    def go(hi, lo):
        def slab(out, first, x):
            at = 0
            for a in range(H1):
                for ref in (own, gots[hi], gots[lo]):
                    out[at : at + 8, :] = ref[8 * (first + a) : 8 * (first + a) + 8, :]
                    at += 8
            for a in range(H1 // 2):
                row = X1 * 8 + 8 * (first // 2 + a)
                for ref in (own, gots[hi], gots[lo]):
                    out[at : at + 8, :] = ref[row : row + 8, :]
                    at += 8
            out[at : at + BY, :] = u[1, x, 0:BY, :]

        def action(xhi, xlo):
            slab(outs[xhi], X1 - H1, X1 + 1)
            slab(outs[xlo], 0, 2)

        by_parity("gx", action)

    @pl.when(odd_y == 0)
    def _():
        go(0, 1)

    @pl.when(odd_y == 1)
    def _():
        go(1, 0)


def coarse_half(e, r, d, at, n, colour, faces, zstep):
    here = pl.ds(at, n)
    e[colour, here] = (r[colour, here] + beside_of(e, colour, faces, at, n, zstep)) * d[colour, here]


def dup_even(value):
    lane = iota(value.shape, value.ndim - 1)
    return jnp.where(lane % 2 == 0, value, rot(value, 1, value.ndim - 1))


def dup_odd(value):
    lane = iota(value.shape, value.ndim - 1)
    return jnp.where(lane % 2 == 1, value, rot(value, -1, value.ndim - 1))


def mid_pre(m0, gy0, gy1, gx0, gx1, csum, g1,
            e, r, d, fin, fout, fyp, fym, fzp, fzm, msg,
            p, t, tr, tc, pc):
    gys, gxs = (gy0, gy1), (gx0, gx1)
    odd_y = lax.axis_index("gy") % 2
    first = colour_mask(1, 2)[0]

    def put(k, rows, one, two, both):
        mask = first[rows]
        for colour in (0, 1):
            a, b = (one, two) if colour == 0 else (two, one)
            value = jnp.where(mask, a, b)
            r[colour, k, rows, :] = dup_even(value)
            d[colour, k, rows, :] = dup_odd(value)
        a, b = dup_even(both), dup_odd(both)
        p[0, k, rows, :] = jnp.where(mask, a, b)
        p[1, k, rows, :] = jnp.where(mask, b, a)

    def own(hi, lo):
        def pairs(k, _):
            for j, ref in enumerate((m0, gys[hi], gys[lo])):
                two = ref[pl.ds(pl.multiple_of(16 * k, 8), 16), :]
                both = ref[pl.ds(pl.multiple_of(X1 * 8 + 8 * k, 8), 8), :]
                put(1 + H1 // 2 + k, slice(8 * j, 8 * j + 8), two[:8], two[8:], both)
            return 0

        lax.fori_loop(0, X1 // 2, pairs, 0, unroll=2)

    @pl.when(odd_y == 0)
    def _():
        own(0, 1)

    @pl.when(odd_y == 1)
    def _():
        own(1, 0)

    def beyond(ref, at):
        def pairs(k, _):
            one = ref[pl.ds(pl.multiple_of(2 * YE * k, 8), YE), :]
            two = ref[pl.ds(pl.multiple_of(2 * YE * k + YE, 8), YE), :]
            both = ref[pl.ds(pl.multiple_of(H1 * YE + YE * k, 8), YE), :]
            put(at + k, slice(0, YE), one, two, both)
            return 0

        lax.fori_loop(0, H1 // 2, pairs, 0, unroll=2)

    def action(hi, lo):
        beyond(gxs[hi], 1 + H1 // 2 + X1 // 2)
        beyond(gxs[lo], 1)

    by_parity("gx", action)
    for ref in (p, e):
        for colour in (0, 1):
            ref[colour, 0] = jnp.zeros((YE, NL), F32)
            ref[colour, NM - 1] = jnp.zeros((YE, NL), F32)
    faces = (fin, fout, fyp, fym, fzp, fzm)

    def begin(at):
        here = pl.ds(at, 2)
        faces_of(p, at, 2, 0.25, 2, *faces)
        e[0, here] = r[0, here] * d[0, here]

    groups(1, NM - 2, 2, begin)
    for colour in (1, 0, 1):
        groups(1, NM - 2, GM, lambda at, colour=colour: coarse_half(e, r, d, at, GM, colour, faces, 2))

    def down(at):
        n = 2
        here = pl.ds(at, n)
        k = pl.ds(at - 1 - H1 // 2, n)
        left = F32(0.0)
        for colour in (0, 1):
            part = r[colour, here] + beside_of(e, colour, faces, at, n, 2)
            left += part[:, 0:8] - g1[colour, k] * e[colour, here, 0:8, :]
        to = pl.multiple_of((at - 1 - H1 // 2) * 8, 8)
        tr[pl.ds(to, n * 8), :] = lane_pairs(left, 2).reshape(n * 8, NL)
        tc[pl.ds(to, n * 8), :] = lane_pairs(csum[k], 2).reshape(n * 8, NL)

    groups(1 + H1 // 2, X1 // 2, 2, down)

    def coarse_p(x2, _):
        t[pl.ds(pl.multiple_of(x2 * YE, 8), YE), :] = lane_pairs(p[0, x2 + 1] + p[1, x2 + 1], 2)
        return 0

    lax.fori_loop(0, G1 // 2, coarse_p, 0, unroll=2)

    eighth = F32(0.125)
    n2, m2 = X1 // 2, G1 // 2

    def compact(ref, first, rows, stride):
        lane = iota((rows, NL), 1)
        out = None
        for j in range(4):
            value = ref[pl.ds(first + 2 * j, rows, stride=stride), :] + ref[pl.ds(first + 2 * j + 1, rows, stride=stride), :]
            out = value if out is None else jnp.where(lane % 4 == j, value, out)
        return eighth * out

    r2 = compact(tr, 0, n2, 8)
    react2 = compact(tc, 0, n2, 8)
    for k in range(3):
        pc[k] = compact(t, 8 * k, m2, YE)
    h2 = H1 // 2
    centre_p = pc[0, h2 : h2 + n2, :]
    j4 = iota((n2, NL), 1) % 4
    lane = iota((n2, NL), 1)
    high = jnp.where(j4 < 3, rot(centre_p, -1, 1), rot(pc[1, h2 : h2 + n2, :], 3, 1))
    low = jnp.where(j4 > 0, rot(centre_p, 1, 1), rot(pc[2, h2 : h2 + n2, :], -3, 1))
    front = jnp.where(lane >= NL - 4, F32(0.0), rot(centre_p, -4, 1))
    back = jnp.where(lane < 4, F32(0.0), rot(centre_p, 4, 1))
    near = (pc[0, h2 + 1 : h2 + 1 + n2, :] + pc[0, h2 - 1 : h2 - 1 + n2, :]) + (high + low) + (front + back)
    diag2 = F32(0.0625) * (F32(3.0) * centre_p + F32(0.5) * near) + react2
    inverse2 = F32(1.0) / diag2

    def every(k, _):
        msg[k, 0:8, :] = r2
        msg[k, 8:16, :] = inverse2
        msg[k, 16:24, :] = centre_p
        return 0

    lax.fori_loop(0, msg.shape[0], every, 0)


def finish(at, got, e, r, d, fin1, fout1, fyp1, fym1, fzp1, fzm1,
           before, c, fin, fout, fyp, fym, fzp, fzm, src, scr, free, gy0, gy1, gx0, gx1,
           result,
           e2, p2, r2, d2, k2, tx, eu, u, hal):
    wx, wy = got.shape[0], got.shape[1]
    rows = wx * 8
    e2[...] = jnp.zeros_like(e2)
    p2[0] = jnp.zeros((rows, NL), F32)
    p2[wy + 1] = jnp.zeros((rows, NL), F32)

    def spread(b, _):
        for a in range(wx):
            r2[b, 8 * a : 8 * a + 8, :] = got[a, b, 0:8, :]
            d2[b, 8 * a : 8 * a + 8, :] = got[a, b, 8:16, :]
            p2[b + 1, 8 * a : 8 * a + 8, :] = got[a, b, 16:24, :]
        return 0

    lax.fori_loop(0, wy, spread, 0)
    sub = iota((rows, NL), 0)
    lane = iota((rows, NL), 1)
    j4 = lane % 4
    parity2 = (sub + j4 + lane // 4) % 2

    span = 4 if wy % 4 == 0 else 1

    def shifted(v):
        mid = v[1 : span + 1]
        near = j4[None] < 3
        return (
            rot(mid, -1, 1), rot(mid, 1, 1),
            jnp.where(near, rot(mid, -1, 2), rot(v[2:], 3, 2)),
            jnp.where(j4[None] > 0, rot(mid, 1, 2), rot(v[:span], -3, 2)),
            rot(mid, -4, 2), rot(mid, 4, 2),
        )

    edges = (sub == rows - 1, sub == 0, None, None, lane >= NL - 4, lane < 4)

    def begin(b):
        here = pl.ds(b, span)
        v = p2[pl.ds(b, span + 2)]
        for k, (value, edge) in enumerate(zip(shifted(v), edges, strict=True)):
            face = F32(0.03125) * (v[1 : span + 1] + value)
            k2[k, here] = face if edge is None else jnp.where(edge[None], F32(0.0), face)
        e2[pl.ds(b + 1, span)] = jnp.where(parity2[None] == 0, r2[here] * d2[here], F32(0.0))

    groups(0, wy, span, begin)

    def half2(step, _):
        colour = step % 2

        def one(b):
            here = pl.ds(b, span)
            v = e2[pl.ds(b, span + 2)]
            total = r2[here]
            for k, value in enumerate(shifted(v)):
                total = total + k2[k, here] * value
            e2[pl.ds(b + 1, span)] = jnp.where(parity2[None] == colour, total * d2[here], v[1 : span + 1])

        groups(0, wy, span, one)
        return 0

    lax.fori_loop(1, 8, half2, 0)

    ox, oy = at[0], at[1]
    for k, step in enumerate((0, 1, -1)):
        b = oy + step + 1
        for dx, first, size, to in ((0, 0, 8, 4), (1, 0, 4, 12), (-1, 4, 4, 0)):
            a = ox + dx
            inside = (a >= 0) & (a < wx)
            block = e2[b, pl.ds(pl.multiple_of(jnp.clip(a, 0, wx - 1) * 8, 8), 8), :]
            block = jnp.where(inside, block, F32(0.0))
            l8 = iota((8, NL), 1)
            for j in range(4):
                value = jnp.where(l8 % 4 == 0, rot(block, -j, 1), F32(0.0))
                value = value + rot(value, 1, 1)
                value = value + rot(value, 2, 1)
                for y in (0, 1):
                    tx[pl.ds(to * YE + 8 * k + 2 * j + y, size, stride=YE), :] = value[first : first + size]

    def correct(x2, _):
        value = tx[pl.ds(pl.multiple_of(x2 * YE, 8), YE), :]
        for colour in (0, 1):
            eu[colour, x2 + 1] = e[colour, x2 + 1] + value
        return 0

    lax.fori_loop(0, G1 // 2, correct, 0, unroll=2)
    faces1 = (fin1, fout1, fyp1, fym1, fzp1, fzm1)
    for at1, count, n, colour in ((3, 12, 4, 0), (3, 12, 4, 1), (4, 10, 5, 0), (4, 10, 5, 1)):
        groups(at1, count, n, lambda at, n=n, colour=colour: coarse_half(eu, r, d, at, n, colour, faces1, 2))

    base = X1 * 8 + X1 * 4

    def action_y(hi, lo):
        hal[pl.ds(1, X1, stride=8), :] = (gy0, gy1)[hi][base : base + X1, :]
        hal[pl.ds(6, X1, stride=8), :] = (gy0, gy1)[lo][base : base + X1, :]

    by_parity("gy", action_y)
    first = colour_mask(1, 1)[0]
    first1 = colour_mask(1, 2)[0]
    s8 = iota((8, NL), 0)
    added = (s8 == 1) | (s8 == 6)
    own_rows = slice(0, BY)

    def widen(k, plane, now1, halo1):
        for y in (0, 1):
            tx[pl.ds(k * YE + y, 8, stride=2), :] = plane[0:8]
        wide = tx[pl.ds(pl.multiple_of(k * YE, 8), BY), :]
        hi, lo = plane[8:16], plane[16:24]
        halo = jnp.where(s8 < 2, jnp.where(s8 == 0, hi, rot(hi, 1, 0)), jnp.where(s8 == 7, lo, rot(lo, -1, 0)))
        now = ((before[0, k, own_rows, :], before[0, k, BY:YE, :]), (now1, halo1))
        for colour in (0, 1):
            one, two = now[colour]
            u[colour, k, own_rows, :] = jnp.where(free[colour, k, own_rows, :] > 0.5, one + wide, one)
            u[colour, k, BY:YE, :] = jnp.where(free[colour, k, BY:YE, :] > 0.5, two + halo, two)

    def level1_plane(m, second):
        one, two = (eu[1, m], eu[0, m]) if second else (eu[0, m], eu[1, m])
        return jnp.where(first1, one, two)

    def add(m, _):
        for second in (0, 1):
            k = 2 * m + second + 2
            halo = jnp.where(added, hal[pl.ds(pl.multiple_of(8 * (k - 2), 8), 8), :], before[1, k, BY:YE, :])
            widen(k, level1_plane(m + 1 + H1 // 2, second), before[1, k, own_rows, :], halo)
        return 0

    lax.fori_loop(0, X1 // 2, add, 0)

    def action_x(hi, lo):
        row = (gx0, gx1)[hi][XMSG - BY : XMSG, :]
        k = X1 + 2
        now = jnp.where(first[own_rows], row, before[1, k, own_rows, :])
        widen(k, level1_plane(1 + H1 // 2 + X1 // 2, 0), now, before[1, k, BY:YE, :])
        row = (gx0, gx1)[lo][XMSG - BY : XMSG, :]
        now = jnp.where(first[own_rows], before[1, 1, own_rows, :], row)
        widen(1, level1_plane(H1 // 2, 1), now, before[1, 1, BY:YE, :])

    by_parity("gx", action_x)
    for k in (0, NF - 1):
        u[1, k] = before[1, k]
    refs = (c, fin, fout, fyp, fym, fzp, fzm, src, scr, free)
    groups(1, X1 + 2, GF, lambda at: fine_half(u, at, GF, 0, refs))

    def last(at):
        n = 2
        new = fine_new(u, at, n, 1, refs)[:, own_rows]
        even = u[0, pl.ds(at, n), own_rows, :]
        mask = first[own_rows]
        for k in range(n):
            to = pl.multiple_of((at - 2 + k) * 2 * BY, 8)
            result[pl.ds(to, BY), :] = jnp.where(mask, even[k], new[k])
            result[pl.ds(to + BY, BY), :] = jnp.where(mask, new[k], even[k])

    groups(2, X1, 2, last)


def swap(pair, axis):
    count = lax.axis_size(axis)
    got = [None, None]
    for first in (1, 0):
        route = []
        for i in range(first, count - 1, 2):
            route += [(i, i + 1), (i + 1, i)]
        got[first] = lax.ppermute(pair[first], axis, route)
    return tuple(got)


def body(source, permittivity, screening, potential, fixed_cell):
    gx, gy = lax.axis_size("gx"), lax.axis_size("gy")
    args = [a.reshape(BX * BY, NL) for a in (potential, permittivity, source, screening, fixed_cell)]
    args = [pltpu.with_memory_space_constraint(a, pltpu.HBM) for a in args]

    whole = (sds(BX * BY, NL),) * 4 + (jax.ShapeDtypeStruct((BX * BY, NL), jnp.int32),)
    *args, y0, y1 = call(pack_y, whole + (sds(10 * BX, NL),) * 2, [pltpu.SemaphoreType.DMA((5,))], hbm=5)(*args)
    y0 = (y0, y1)
    y0 = swap(y0, "gy")
    *halos, x0, x1 = call(pack_x, (sds(BX * 8, NL),) * 5 + (sds(12 * YE, NL),) * 2)(*args, *y0)
    gotx = swap((x0, x1), "gx")

    ext, one = (2, NF, YE, NL), (NF, YE, NL)
    fine = call(
        fine_pre,
        (sds(*ext),) * 2 + (sds(*one),) + (sds(*ext),) * 8
        + (sds(X1 // 2, 8, NL), sds(2, X1 // 2, 8, NL)) + (sds(YMSG, NL),) * 2,
        [
            pltpu.VMEM(ext, F32),
            pltpu.VMEM((X1 * BY, NL), F32),
            pltpu.VMEM((X1 * BY, NL), F32),
            pltpu.VMEM(((X1 + 2) * YE, NL), F32),
            pltpu.VMEM((X1 + 2, 8, NL), F32),
        ],
    )(*args, *halos, *gotx)
    state, (c1, g1, m0, m1) = fine[:11], fine[11:]
    goty1 = swap((m0, m1), "gy")
    x1msg = call(pack_x1, (sds(XMSG, NL),) * 2)(m0, m1, *goty1, state[0])
    gotx1 = swap(x1msg, "gx")

    mid, mid1 = (2, NM, YE, NL), (NM, YE, NL)
    *level1, message = call(
        mid_pre,
        (sds(*mid),) * 3 + (sds(*mid1),) + (sds(*mid),) * 5 + (sds(gx * gy, 24, NL),),
        [
            pltpu.VMEM(mid, F32),
            pltpu.VMEM((G1 // 2 * YE, NL), F32),
            pltpu.VMEM((X1 // 2 * 8, NL), F32),
            pltpu.VMEM((X1 // 2 * 8, NL), F32),
            pltpu.VMEM((3, G1 // 2, NL), F32),
        ],
    )(m0, *goty1, *gotx1, c1, g1)

    gathered = lax.all_to_all(message, ("gx", "gy"), 0, 0).reshape(gx, gy, 24, NL)
    wx, wy = min(gx, 5), min(gy, 8)
    if (wx, wy) != (gx, gy):
        first = (*window(gx, gy, wx, wy)[:2], 0, 0)
        gathered = lax.dynamic_slice(gathered, first, (wx, wy, 24, NL))

    inputs = (gathered, *level1, *state, *goty1, *gotx1)
    result = pl.pallas_call(
        finish_kernel(len(inputs), (gx, gy, wx, wy)),
        out_shape=sds(BX * BY, NL),
        scratch_shapes=[
            pltpu.VMEM((wy + 2, wx * 8, NL), F32),
            pltpu.VMEM((wy + 2, wx * 8, NL), F32),
            pltpu.VMEM((wy, wx * 8, NL), F32),
            pltpu.VMEM((wy, wx * 8, NL), F32),
            pltpu.VMEM((6, wy, wx * 8, NL), F32),
            pltpu.VMEM((NF * YE, NL), F32),
            pltpu.VMEM(mid, F32),
            pltpu.VMEM(ext, F32),
            pltpu.VMEM((BX // 2 * 8, NL), F32),
        ],
        compiler_params=pltpu.CompilerParams(vmem_limit_bytes=24 << 20),
        name="finish",
    )(*inputs)
    return result.reshape(BX, BY, NL)


def window(gx, gy, wx, wy):
    ix, iy = lax.axis_index("gx"), lax.axis_index("gy")
    fx = jnp.clip(ix - 2, 0, gx - wx)
    fy = jnp.clip(iy - 3, 0, gy - wy)
    return fx, fy, ix - fx, iy - fy


def finish_kernel(count, sizes):
    def kernel(*refs):
        ins, result, scratch = list(refs[:count]), refs[count], list(refs[1 + count :])
        finish(window(*sizes)[2:], *ins, result, *scratch)

    return kernel


def solution(mesh):
    placed = (P("gx", "gy", None),) * 5

    return jax.shard_map(body, mesh=mesh, in_specs=placed, out_specs=P("gx", "gy", None), check_vma=False)
```

```python
import jax
import jax.numpy as jnp
from jax import lax
from jax.experimental import pallas as pl
from jax.experimental.pallas import tpu as pltpu
from jax.sharding import PartitionSpec as P

F32 = jnp.float32
BX, BY, NL = 32, 16, 128
YE = 24
X1 = BX // 2
H1 = 8
G1 = X1 + 2 * H1
NF = X1 + 4
NM = G1 // 2 + 2
GF = 6
GM = 8
LN2 = 0.6931471805599453


def rot(value, shift, axis):
    return pltpu.roll(value, shift % value.shape[axis], axis)


def iota(shape, axis):
    return lax.broadcasted_iota(jnp.int32, shape, axis)


def sds(*shape):
    return jax.ShapeDtypeStruct(shape, F32)


def by_parity(axis, action):
    odd = lax.axis_index(axis) % 2

    @pl.when(odd == 0)
    def _():
        action(0, 1)

    @pl.when(odd == 1)
    def _():
        action(1, 0)


def call(kernel, out_shape, scratch=(), vmem=24, hbm=0):
    specs = {"in_specs": [pl.BlockSpec(memory_space=pltpu.HBM)] * hbm} if hbm else {}
    return pl.pallas_call(
        kernel,
        out_shape=out_shape,
        **specs,
        scratch_shapes=list(scratch),
        compiler_params=pltpu.CompilerParams(vmem_limit_bytes=vmem << 20),
    )


YROWS = 10 * BX
XROWS = 12 * YE


def split_rows(ref, at):
    one, two = ref[pl.ds(at, 4, stride=2), :], ref[pl.ds(at + 1, 4, stride=2), :]
    lane = iota((4, NL), 1)
    even = (lane % 4 + lane // 4) % 2 == 0
    return jnp.concatenate([jnp.where(even, one, two), jnp.where(even, two, one)], axis=0)


def pack_y(hpot, hper, hsrc, hscr, hfix, pot, per, src, scr, fix, p2, out0, out1, sems, t, pk):
    outs = (out0, out1)
    pairs = ((hpot, pot), (hper, per), (hsrc, src), (hscr, scr), (hfix, fix))
    copies = [pltpu.make_async_copy(a, b, sems.at[k]) for k, (a, b) in enumerate(pairs)]
    for copy in copies:
        copy.start()
    for copy in copies:
        copy.wait()
    zlane = iota((BX // 2, NL), 1)

    def free_of(value):
        return jnp.where(value == 0, F32(1.0), F32(0.0))

    def row(ref, r):
        return ref[pl.ds(r, BX, stride=BY), :]

    def half(ref, r, parity):
        even = ref[pl.ds(r, BX // 2, stride=2 * BY), :]
        odd = ref[pl.ds(BY + r, BX // 2, stride=2 * BY), :]
        return jnp.where((r + zlane) % 2 == parity, even, odd)

    def side(out, r1, r2, r3):
        rows = [
            row(pot, r1), row(per, r1), row(src, r1), row(scr, r1), free_of(row(fix, r1)),
            row(pot, r2), row(per, r2), free_of(row(fix, r2)),
        ]
        for k, value in enumerate(rows):
            out[BX * k : BX * (k + 1), :] = value
        base = BX * len(rows)
        for k, value in enumerate([half(pot, r3, 1), half(per, r3, 1), half(src, r2, 0), half(scr, r2, 0)]):
            out[base + k * BX // 2 : base + (k + 1) * BX // 2, :] = value

    v = per[...].reshape(BX // 4, 4, BY, NL)
    v = (v[:, 0] + v[:, 1]) + (v[:, 2] + v[:, 3])
    t[...] = lane_pairs(lane_pairs(v, 1), 2).reshape(BX // 4 * BY, NL)
    n2 = BX // 4
    lane = iota((n2, NL), 1)
    total = None
    for j in range(4):
        r = [t[pl.ds(4 * j + k, n2, stride=BY), :] for k in range(4)]
        value = (r[0] + r[1]) + (r[2] + r[3])
        total = value if total is None else jnp.where(lane % 4 == j, value, total)
    pk[...] = F32(1.0 / 64) * total
    p2[...] = split_rows(pk, 0)

    def action(hi, lo):
        side(outs[hi], BY - 1, BY - 2, BY - 3)
        side(outs[lo], 0, 1, 2)
        for out in outs:
            out[YROWS : YROWS + 8, :] = p2[...]

    by_parity("gy", action)


def pack_x(pot, per, src, scr, fix, p2, got0, got1, hpot, hper, hsrc, hscr, hfree, out0, out1):
    gots, outs = (got0, got1), (out0, out1)
    halos = (hpot, hper, hsrc, hscr, hfree)
    for h in halos:
        h[...] = jnp.zeros_like(h)

    def place(got, slots):
        def whole(ref, k, slot):
            ref[pl.ds(slot, BX, stride=8), :] = got[BX * k : BX * (k + 1), :]

        def halved(ref, k, slot):
            value = got[BX * 8 + k * BX // 2 : BX * 8 + (k + 1) * BX // 2, :]
            ref[pl.ds(slot, BX // 2, stride=16), :] = value
            ref[pl.ds(8 + slot, BX // 2, stride=16), :] = value

        s1, s2, s3 = slots
        for k, ref in enumerate(halos):
            whole(ref, k, s1)
        whole(hpot, 5, s2)
        whole(hper, 6, s2)
        whole(hfree, 7, s2)
        halved(hpot, 0, s3)
        halved(hper, 1, s3)
        halved(hsrc, 2, s2)
        halved(hscr, 3, s2)

    def action_y(hi, lo):
        place(gots[hi], (0, 1, 2))
        place(gots[lo], (7, 6, 5))

    by_parity("gy", action_y)

    def slab(out, planes):
        k = 0
        for ref, h, depth in ((pot, hpot, 3), (per, hper, 3), (src, hsrc, 2), (scr, hscr, 2), (fix, hfree, 2)):
            for x in planes[:depth]:
                own = ref[BY * x : BY * (x + 1), :]
                if ref is fix:
                    own = jnp.where(own == 0, F32(1.0), F32(0.0))
                out[YE * k : YE * k + BY, :] = own
                out[YE * k + BY : YE * (k + 1), :] = h[8 * x : 8 * (x + 1), :]
                k += 1

    def action_p(hi, lo):
        for out in outs:
            out[XROWS : XROWS + 8, :] = p2[...]
            out[XROWS + 8 : XROWS + 16, :] = gots[hi][YROWS : YROWS + 8, :]
            out[XROWS + 16 : XROWS + 24, :] = gots[lo][YROWS : YROWS + 8, :]

    by_parity("gy", action_p)

    def action_x(hi, lo):
        slab(outs[hi], (BX - 1, BX - 2, BX - 3))
        slab(outs[lo], (0, 1, 2))

    by_parity("gx", action_x)


def nonlinear(u, scr):
    up = jnp.exp(u - F32(LN2))
    down = jnp.exp(-u - F32(LN2))
    return scr * (up - down), scr * (up + down)


def colour_mask(n, zstep):
    shape = (n, YE, NL)
    return (iota(shape, 1) + iota(shape, 2) // zstep) % 2 == 0


def beside_of(other, colour, faces, at, n, zstep):
    fin, fout, fyp, fym, fzp, fzm = faces
    here = pl.ds(at, n)
    v = other[1 - colour, pl.ds(at - 1, n + 2)]
    mid = v[1 : n + 1]
    first = colour_mask(n, zstep)
    across = jnp.where(first, v[:n], v[2:]) if colour == 0 else jnp.where(first, v[2:], v[:n])
    return (
        (fin[here] * mid + fout[colour, here] * across)
        + (fyp[colour, here] * rot(mid, -1, 1) + fym[colour, here] * rot(mid, 1, 1))
        + (fzp[colour, here] * rot(mid, -zstep, 2) + fzm[colour, here] * rot(mid, zstep, 2))
    )


def pairs_of(u, at, n, colour, refs):
    c, fin, fout, fyp, fym, fzp, fzm, src, scr, _ = refs
    here = pl.ds(at, n)
    plane = u[colour, here]
    sh, ch = nonlinear(plane, scr[colour, here])
    centre = c[colour, here]
    beside = beside_of(u, colour, (fin, fout, fyp, fym, fzp, fzm), at, n, 1)
    return plane, centre * plane - beside + sh - src[colour, here], centre, ch


def fine_new(u, at, n, colour, refs):
    plane, value, centre, ch = pairs_of(u, at, n, colour, refs)
    return jnp.where(refs[-1][colour, pl.ds(at, n)] > 0.5, plane - value / (centre + ch), plane)


def fine_half(u, at, n, colour, refs):
    u[colour, pl.ds(at, n)] = fine_new(u, at, n, colour, refs)


def groups(first, count, n, step):
    assert count % n == 0

    def one(g, _):
        step(first + g * n)
        return 0

    lax.fori_loop(0, count // n, one, 0)


def faces_of(p, at, n, scale, zstep, fin, fout, fyp, fym, fzp, fzm):
    here = pl.ds(at, n)
    lane = iota((n, YE, NL), 2)
    first = colour_mask(n, zstep)
    half = F32(0.5 * scale)
    for colour in (0, 1):
        plane = p[colour, here]
        v = p[1 - colour, pl.ds(at - 1, n + 2)]
        mid = v[1 : n + 1]
        across = jnp.where(first, v[:n], v[2:]) if colour == 0 else jnp.where(first, v[2:], v[:n])
        if colour == 0:
            fin[here] = half * (plane + mid)
        fout[colour, here] = half * (plane + across)
        fyp[colour, here] = half * (plane + rot(mid, -1, 1))
        fym[colour, here] = half * (plane + rot(mid, 1, 1))
        fzp[colour, here] = jnp.where(lane >= NL - zstep, F32(0.0), half * (plane + rot(mid, -zstep, 2)))
        fzm[colour, here] = jnp.where(lane < zstep, F32(0.0), half * (plane + rot(mid, zstep, 2)))


def lane_pairs(value, step):
    lane = iota(value.shape, value.ndim - 1)
    return value + jnp.where((lane // step) % 2 == 0, rot(value, -step, value.ndim - 1), rot(value, step, value.ndim - 1))


def fine_pre(pot, per, src, scr, fix, hpot, hper, hsrc, hscr, hfree, goty0, goty1, got0, got1,
             u, c, fin, fout, fyp, fym, fzp, fzm, esrc, escr, efree, csum, g1, m0, m1,
             ep, tr, tc, tp, p1):
    gots, outs = (got0, got1), (m0, m1)
    first = colour_mask(1, 1)[0]

    def own(k, _):
        for ref, h, ext in ((pot, hpot, u), (per, hper, ep), (src, hsrc, esrc), (scr, hscr, escr), (fix, hfree, efree)):
            value = ref[pl.ds(pl.multiple_of(2 * k * BY, 8), 2 * BY), :]
            if ref is fix:
                value = jnp.where(value == 0, F32(1.0), F32(0.0))
            halo = h[pl.ds(pl.multiple_of(16 * k, 8), 16), :]
            for rows, one, two in (
                (slice(0, BY), value[:BY], value[BY:]),
                (slice(BY, YE), halo[:8], halo[8:]),
            ):
                ext[0, k + 2, rows, :] = jnp.where(first[rows], one, two)
                ext[1, k + 2, rows, :] = jnp.where(first[rows], two, one)
        return 0

    lax.fori_loop(0, X1, own, 0, unroll=2)

    def place(got, near, far, flip):
        k = 0
        for ext, depth in ((u, 3), (ep, 3), (esrc, 2), (escr, 2), (efree, 2)):
            planes = [got[YE * (k + j) : YE * (k + j + 1), :] for j in range(depth)]
            k += depth
            one, two = (planes[1], planes[0]) if flip else (planes[0], planes[1])
            ext[0, near] = jnp.where(first, one, two)
            ext[1, near] = jnp.where(first, two, one)
            third = planes[2] if depth == 3 else jnp.zeros((YE, NL), F32)
            ext[0, far] = third
            ext[1, far] = third

    def action_x(hi, lo):
        place(gots[hi], X1 + 2, X1 + 3, False)
        place(gots[lo], 1, 0, True)

    by_parity("gx", action_x)
    refs = (c, fin, fout, fyp, fym, fzp, fzm, esrc, escr, efree)

    def begin(at):
        n = GF
        faces_of(ep, at, n, 1.0, 1, fin, fout, fyp, fym, fzp, fzm)
        here = pl.ds(at, n)
        lane = iota((n, YE, NL), 2)
        for colour in (0, 1):
            ends = jnp.where((lane == 0) | (lane == NL - 1), F32(0.5) * ep[colour, here], F32(0.0))
            c[colour, here] = (
                (fin[here] + fout[colour, here]) + (fyp[colour, here] + fym[colour, here])
                + (fzp[colour, here] + fzm[colour, here]) + ends
            )
        fine_half(u, at, n, 0, refs)

    groups(1, X1 + 2, GF, begin)
    groups(1, X1 + 2, GF, lambda at: fine_half(u, at, GF, 1, refs))

    def down(at):
        n = 4
        left, react = F32(0.0), F32(0.0)
        for colour in (0, 1):
            _, value, _, ch = pairs_of(u, at, n, colour, refs)
            left += jnp.where(efree[colour, pl.ds(at, n)] > 0.5, -value, F32(0.0))
            react += ch
        to = pl.multiple_of((at - 2) * BY, 8)
        tr[pl.ds(to, n * BY), :] = lane_pairs(left[:, 0:BY], 1).reshape(n * BY, NL)
        tc[pl.ds(to, n * BY), :] = lane_pairs(react[:, 0:BY], 1).reshape(n * BY, NL)

    groups(2, X1, 4, down)

    def coarse_p(k, _):
        at = pl.multiple_of(k * YE, 8)
        tp[pl.ds(at, YE), :] = lane_pairs(ep[0, k + 1] + ep[1, k + 1], 1)
        return 0

    lax.fori_loop(0, X1 + 2, coarse_p, 0, unroll=2)

    eighth = F32(0.125)
    sub = iota((8, NL), 0)
    lane = iota((8, NL), 1)

    def gather_p(k, _):
        p1[k] = eighth * (tp[pl.ds(k * YE, 8, stride=2), :] + tp[pl.ds(k * YE + 1, 8, stride=2), :])
        return 0

    lax.fori_loop(0, X1 + 2, gather_p, 0, unroll=2)

    first8 = (sub + lane // 2) % 2 == 0

    def coarse(x1):
        k = x1 + 1
        p = p1[k]
        base = k * YE
        high = eighth * (tp[pl.ds(base + 2, 8, stride=2), :] + tp[pl.ds(base + 3, 8, stride=2), :])
        edge = tp[pl.ds(pl.multiple_of(base + 16, 8), 8), :]
        edge = eighth * (edge + rot(edge, 1, 0))
        low = jnp.where(sub == 0, rot(edge, 1, 0), rot(p, 1, 0))
        front = jnp.where(lane >= NL - 2, F32(0.0), rot(p, -2, 1))
        back = jnp.where(lane < 2, F32(0.0), rot(p, 2, 1))
        near = (p1[k + 1] + p1[k - 1]) + (high + low) + (front + back)
        centre = F32(3.0) * p + F32(0.5) * near
        at = x1 * BY
        r = eighth * (tr[pl.ds(at, 8, stride=2), :] + tr[pl.ds(at + 1, 8, stride=2), :])
        react = eighth * (tc[pl.ds(at, 8, stride=2), :] + tc[pl.ds(at + 1, 8, stride=2), :])
        diag = F32(0.25) * centre + react
        message = jnp.where(lane % 2 == 0, r, F32(1.0) / diag)
        m0[pl.ds(pl.multiple_of(x1 * 8, 8), 8), :] = message
        m1[pl.ds(pl.multiple_of(x1 * 8, 8), 8), :] = message
        return diag, react

    def make(k, _):
        diag0, react0 = coarse(2 * k)
        diag1, react1 = coarse(2 * k + 1)
        csum[k] = react0 + react1
        g1[0, k] = jnp.where(first8, diag0, diag1)
        g1[1, k] = jnp.where(first8, diag1, diag0)
        return 0

    lax.fori_loop(0, X1 // 2, make, 0)

    for a in range(X1 // 2):
        message = jnp.where(lane % 2 == 0, p1[1 + 2 * a], p1[2 + 2 * a])
        for m in outs:
            m[X1 * 8 + 8 * a : X1 * 8 + 8 * a + 8, :] = message

    base = X1 * 8 + X1 * 4

    def odd_row(out, y):
        out[base : base + X1, :] = u[1, pl.ds(2, X1), y, :]

    def action_y(hi, lo):
        odd_row(outs[hi], BY - 2)
        odd_row(outs[lo], 1)
        outs[hi][base + X1 : base + X1 + 8, :] = (goty0, goty1)[lo][YROWS : YROWS + 8, :]
        outs[lo][base + X1 : base + X1 + 8, :] = (goty0, goty1)[hi][YROWS : YROWS + 8, :]

    by_parity("gy", action_y)


YMSG = X1 * 8 + X1 * 4 + BX // 2 + 8
XOWN = H1 * YE + (H1 // 2) * YE
XMSG = XOWN + BY + 40


def pack_x1(m0, m1, got0, got1, fx0, fx1, u, out0, out1):
    own, gots, outs, fines = m0, (got0, got1), (out0, out1), (fx0, fx1)
    odd_y = lax.axis_index("gy") % 2

    def go(hi, lo):
        def slab(out, first, x, behind):
            at = 0
            for a in range(H1):
                for ref in (own, gots[hi], gots[lo]):
                    out[at : at + 8, :] = ref[8 * (first + a) : 8 * (first + a) + 8, :]
                    at += 8
            for a in range(H1 // 2):
                row = X1 * 8 + 8 * (first // 2 + a)
                for ref in (own, gots[hi], gots[lo]):
                    out[at : at + 8, :] = ref[row : row + 8, :]
                    at += 8
            out[at : at + BY, :] = u[1, x, 0:BY, :]
            at += BY
            for got in (gots[hi], gots[lo]):
                out[at : at + 8, :] = got[YMSG - 8 : YMSG, :]
                at += 8
            out[at : at + 24, :] = behind[XROWS : XROWS + 24, :]

        def action(xhi, xlo):
            slab(outs[xhi], X1 - H1, X1 + 1, fines[xlo])
            slab(outs[xlo], 0, 2, fines[xhi])

        by_parity("gx", action)

    @pl.when(odd_y == 0)
    def _():
        go(0, 1)

    @pl.when(odd_y == 1)
    def _():
        go(1, 0)


def coarse_half(e, r, d, at, n, colour, faces, zstep):
    here = pl.ds(at, n)
    e[colour, here] = (r[colour, here] + beside_of(e, colour, faces, at, n, zstep)) * d[colour, here]


def dup_even(value):
    lane = iota(value.shape, value.ndim - 1)
    return jnp.where(lane % 2 == 0, value, rot(value, 1, value.ndim - 1))


def dup_odd(value):
    lane = iota(value.shape, value.ndim - 1)
    return jnp.where(lane % 2 == 1, value, rot(value, -1, value.ndim - 1))


def mid_pre(m0, gy0, gy1, gx0, gx1, csum, g1,
            e, r, d, fin, fout, fyp, fym, fzp, fzm, msg,
            p, t, tr, tc, pc, pk):
    gys, gxs = (gy0, gy1), (gx0, gx1)
    odd_y = lax.axis_index("gy") % 2
    first = colour_mask(1, 2)[0]

    def put(k, rows, one, two, both):
        mask = first[rows]
        for colour in (0, 1):
            a, b = (one, two) if colour == 0 else (two, one)
            value = jnp.where(mask, a, b)
            r[colour, k, rows, :] = dup_even(value)
            d[colour, k, rows, :] = dup_odd(value)
        a, b = dup_even(both), dup_odd(both)
        p[0, k, rows, :] = jnp.where(mask, a, b)
        p[1, k, rows, :] = jnp.where(mask, b, a)

    def own(hi, lo):
        def pairs(k, _):
            for j, ref in enumerate((m0, gys[hi], gys[lo])):
                two = ref[pl.ds(pl.multiple_of(16 * k, 8), 16), :]
                both = ref[pl.ds(pl.multiple_of(X1 * 8 + 8 * k, 8), 8), :]
                put(1 + H1 // 2 + k, slice(8 * j, 8 * j + 8), two[:8], two[8:], both)
            return 0

        lax.fori_loop(0, X1 // 2, pairs, 0, unroll=2)

    @pl.when(odd_y == 0)
    def _():
        own(0, 1)

    @pl.when(odd_y == 1)
    def _():
        own(1, 0)

    def beyond(ref, at):
        def pairs(k, _):
            one = ref[pl.ds(pl.multiple_of(2 * YE * k, 8), YE), :]
            two = ref[pl.ds(pl.multiple_of(2 * YE * k + YE, 8), YE), :]
            both = ref[pl.ds(pl.multiple_of(H1 * YE + YE * k, 8), YE), :]
            put(at + k, slice(0, YE), one, two, both)
            return 0

        lax.fori_loop(0, H1 // 2, pairs, 0, unroll=2)

    def action(hi, lo):
        beyond(gxs[hi], 1 + H1 // 2 + X1 // 2)
        beyond(gxs[lo], 1)

    by_parity("gx", action)
    for ref in (p, e):
        for colour in (0, 1):
            ref[colour, 0] = jnp.zeros((YE, NL), F32)
            ref[colour, NM - 1] = jnp.zeros((YE, NL), F32)
    faces = (fin, fout, fyp, fym, fzp, fzm)

    def begin(at):
        here = pl.ds(at, 2)
        faces_of(p, at, 2, 0.25, 2, *faces)
        e[0, here] = r[0, here] * d[0, here]

    groups(1, NM - 2, 2, begin)
    for colour in (1, 0, 1):
        groups(1, NM - 2, GM, lambda at, colour=colour: coarse_half(e, r, d, at, GM, colour, faces, 2))

    def down(at):
        n = 4
        here = pl.ds(at, n)
        k = pl.ds(at - 1 - H1 // 2, n)
        left = F32(0.0)
        for colour in (0, 1):
            part = r[colour, here] + beside_of(e, colour, faces, at, n, 2)
            left += part[:, 0:8] - g1[colour, k] * e[colour, here, 0:8, :]
        to = pl.multiple_of((at - 1 - H1 // 2) * 8, 8)
        tr[pl.ds(to, n * 8), :] = lane_pairs(left, 2).reshape(n * 8, NL)
        tc[pl.ds(to, n * 8), :] = lane_pairs(csum[k], 2).reshape(n * 8, NL)

    groups(1 + H1 // 2, X1 // 2, 4, down)

    def coarse_p(x2, _):
        t[pl.ds(pl.multiple_of(x2 * YE, 8), YE), :] = lane_pairs(p[0, x2 + 1] + p[1, x2 + 1], 2)
        return 0

    lax.fori_loop(0, G1 // 2, coarse_p, 0, unroll=2)

    eighth = F32(0.125)
    n2, m2 = X1 // 2, G1 // 2

    def compact(ref, first, rows, stride):
        lane = iota((rows, NL), 1)
        out = None
        for j in range(4):
            value = ref[pl.ds(first + 2 * j, rows, stride=stride), :] + ref[pl.ds(first + 2 * j + 1, rows, stride=stride), :]
            out = value if out is None else jnp.where(lane % 4 == j, value, out)
        return eighth * out

    r2 = compact(tr, 0, n2, 8)
    react2 = compact(tc, 0, n2, 8)
    for k in range(3):
        pc[k] = compact(t, 8 * k, m2, YE)
    h2 = H1 // 2
    centre_p = pc[0, h2 : h2 + n2, :]
    j4 = iota((n2, NL), 1) % 4
    lane = iota((n2, NL), 1)
    high = jnp.where(j4 < 3, rot(centre_p, -1, 1), rot(pc[1, h2 : h2 + n2, :], 3, 1))
    low = jnp.where(j4 > 0, rot(centre_p, 1, 1), rot(pc[2, h2 : h2 + n2, :], -3, 1))
    front = jnp.where(lane >= NL - 4, F32(0.0), rot(centre_p, -4, 1))
    back = jnp.where(lane < 4, F32(0.0), rot(centre_p, 4, 1))
    near = (pc[0, h2 + 1 : h2 + 1 + n2, :] + pc[0, h2 - 1 : h2 - 1 + n2, :]) + (high + low) + (front + back)
    diag2 = F32(0.0625) * (F32(3.0) * centre_p + F32(0.5) * near) + react2
    for k, value in enumerate((r2, F32(1.0) / diag2, centre_p)):
        pk[8 * k : 8 * k + 8, :] = value
    r2, inverse2, own_p = (split_rows(pk, 8 * k) for k in range(3))
    near_rows = iota((8, NL), 1) % 4 >= 2
    ahead = jnp.where(near_rows, r2, rot(own_p, -2, 1))
    behind = jnp.where(near_rows, rot(own_p, 2, 1), r2)
    count = lax.axis_size("gy")
    place = lax.axis_index("gy")

    def every(k, _):
        step = k % count - place
        msg[k, 0:8, :] = jnp.where(step == 3, ahead, jnp.where(step == -3, behind, r2))
        msg[k, 8:16, :] = inverse2
        return 0

    lax.fori_loop(0, msg.shape[0], every, 0, unroll=2)


def finish(at, got, p2own, yf0, yf1, xf0, xf1, e, r, d, fin1, fout1, fyp1, fym1, fzp1, fzm1,
           before, c, fin, fout, fyp, fym, fzp, fzm, src, scr, free, gy0, gy1, gx0, gx1,
           result,
           e2, p2, r2, d2, k2, blk, tx, eu, u, hal):
    wx, wy = got.shape[0], got.shape[1]
    rows = wx * 4
    ox, oy = at
    blk[...] = jnp.zeros_like(blk)
    e2[...] = jnp.zeros_like(e2)

    def keep(da, db, ref, first):
        blk[oy + db + 3, ox + da + 2] = ref[first : first + 8, :]

    keep(0, 0, p2own, 0)

    def blocks_y(hi, lo):
        for db, k in ((1, hi), (-1, lo)):
            keep(0, db, (yf0, yf1)[k], YROWS)
            keep(0, 2 * db, (gy0, gy1)[k], YMSG - 8)

    by_parity("gy", blocks_y)

    def blocks_x(hi, lo):
        for da, k in ((1, hi), (-1, lo)):
            fine, mid = (xf0, xf1)[k], (gx0, gx1)[k]
            for n, db in enumerate((0, 1, -1)):
                keep(da, db, fine, XROWS + 8 * n)
                keep(2 * da, db, mid, XOWN + BY + 16 + 8 * n)
            keep(da, 2, mid, XOWN + BY)
            keep(da, -2, mid, XOWN + BY + 8)

    by_parity("gx", blocks_x)
    l4 = iota((8, NL), 1) % 4
    for db in (3, -3):

        @pl.when((oy + db >= 0) & (oy + db < wy))
        def _(db=db):
            for a in range(wx):
                value = got[a, oy + db, 0:8, :]
                value = jnp.where(l4 < 2, rot(value, -2, 1), F32(0.0)) if db > 0 else jnp.where(l4 >= 2, rot(value, 2, 1), F32(0.0))
                blk[oy + db + 3, a + 2] = value

    def spread(b, _):
        for a in range(wx):
            for colour in (0, 1):
                own, to = slice(4 * colour, 4 * colour + 4), slice(4 * a, 4 * a + 4)
                r2[colour, b, to, :] = got[a, b, own, :]
                d2[colour, b, to, :] = got[a, b, 8 + 4 * colour : 12 + 4 * colour, :]
                p2[colour, b + 1, to, :] = blk[b + 3, a + 2, own, :]
        return 0

    lax.fori_loop(0, wy, spread, 0, unroll=2)
    for b in (0, wy + 1):
        for colour in (0, 1):
            p2[colour, b] = jnp.zeros((rows, NL), F32)
    shape = (wy, rows, NL)
    sub, lane = iota(shape, 1), iota(shape, 2)
    j4 = lane % 4
    even = (j4 + lane // 4) % 2 == 0

    def around(ref, colour):
        v = ref[1 - colour]
        mid = v[1 : wy + 1]
        one, two = rot(mid, 1, 1), rot(mid, -1, 1)
        return (
            mid,
            jnp.where(even, one, two) if colour == 0 else jnp.where(even, two, one),
            jnp.where(j4 < 3, rot(mid, -1, 2), rot(v[2:], 3, 2)),
            jnp.where(j4 > 0, rot(mid, 1, 2), rot(v[:wy], -3, 2)),
            rot(mid, -4, 2), rot(mid, 4, 2),
        )

    for colour in (0, 1):
        at_first = even if colour == 0 else ~even
        outside = (at_first & (sub == 0)) | (~at_first & (sub == rows - 1))
        edges = (None, outside, None, None, lane >= NL - 4, lane < 4)
        mine = p2[colour, 1 : wy + 1]
        for k, (value, edge) in enumerate(zip(around(p2, colour), edges, strict=True)):
            face = F32(0.03125) * (mine + value)
            k2[colour, k] = face if edge is None else jnp.where(edge, F32(0.0), face)
    e2[0, 1 : wy + 1] = r2[0] * d2[0]

    def half2(colour):
        total = r2[colour]
        for k, value in enumerate(around(e2, colour)):
            total = total + k2[colour, k] * value
        e2[colour, 1 : wy + 1] = total * d2[colour]

    half2(1)

    def sweep2(_, carry):
        half2(0)
        half2(1)
        return carry

    lax.fori_loop(0, 3, sweep2, 0)

    s8, l8 = iota((8, NL), 0), iota((8, NL), 1)
    even8 = (l8 % 4 + l8 // 4) % 2 == 0
    start = 4 * ox - 2
    inside = (s8 + start >= 0) & (s8 + start < rows)
    for k, step in enumerate((0, 1, -1)):
        near = []
        for colour in (0, 1):
            block = pltpu.roll(e2[colour, oy + step + 1], (rows - start) % rows, 0)[0:8]
            near.append(jnp.where(inside, block, F32(0.0)))
        planes = (jnp.where(even8, near[0], near[1]), jnp.where(even8, near[1], near[0]))
        for second in (0, 1):
            for j in range(4):
                value = jnp.where(l8 % 4 == 0, rot(planes[second], -j, 1), F32(0.0))
                value = value + rot(value, 1, 1)
                value = value + rot(value, 2, 1)
                for y in (0, 1):
                    tx[pl.ds(second * YE + 8 * k + 2 * j + y, 8, stride=2 * YE), :] = value

    def correct(x2, _):
        value = tx[pl.ds(pl.multiple_of(x2 * YE, 8), YE), :]
        for colour in (0, 1):
            eu[colour, x2 + 1] = e[colour, x2 + 1] + value
        return 0

    lax.fori_loop(0, G1 // 2, correct, 0, unroll=2)
    faces1 = (fin1, fout1, fyp1, fym1, fzp1, fzm1)
    for at1, count, n, colour in ((3, 12, 4, 0), (3, 12, 4, 1), (4, 10, 5, 0), (4, 10, 5, 1)):
        groups(at1, count, n, lambda at, n=n, colour=colour: coarse_half(eu, r, d, at, n, colour, faces1, 2))

    base = X1 * 8 + X1 * 4

    def action_y(hi, lo):
        hal[pl.ds(1, X1, stride=8), :] = (gy0, gy1)[hi][base : base + X1, :]
        hal[pl.ds(6, X1, stride=8), :] = (gy0, gy1)[lo][base : base + X1, :]

    by_parity("gy", action_y)
    first = colour_mask(1, 1)[0]
    first1 = colour_mask(1, 2)[0]
    added = (s8 == 1) | (s8 == 6)
    own_rows = slice(0, BY)

    def widen(k, plane, now1, halo1):
        for y in (0, 1):
            tx[pl.ds(k * YE + y, 8, stride=2), :] = plane[0:8]
        wide = tx[pl.ds(pl.multiple_of(k * YE, 8), BY), :]
        hi, lo = plane[8:16], plane[16:24]
        halo = jnp.where(s8 < 2, jnp.where(s8 == 0, hi, rot(hi, 1, 0)), jnp.where(s8 == 7, lo, rot(lo, -1, 0)))
        now = ((before[0, k, own_rows, :], before[0, k, BY:YE, :]), (now1, halo1))
        for colour in (0, 1):
            one, two = now[colour]
            u[colour, k, own_rows, :] = jnp.where(free[colour, k, own_rows, :] > 0.5, one + wide, one)
            u[colour, k, BY:YE, :] = jnp.where(free[colour, k, BY:YE, :] > 0.5, two + halo, two)

    def level1_plane(m, second):
        one, two = (eu[1, m], eu[0, m]) if second else (eu[0, m], eu[1, m])
        return jnp.where(first1, one, two)

    def add(m, _):
        for second in (0, 1):
            k = 2 * m + second + 2
            halo = jnp.where(added, hal[pl.ds(pl.multiple_of(8 * (k - 2), 8), 8), :], before[1, k, BY:YE, :])
            widen(k, level1_plane(m + 1 + H1 // 2, second), before[1, k, own_rows, :], halo)
        return 0

    lax.fori_loop(0, X1 // 2, add, 0)

    def action_x(hi, lo):
        row = (gx0, gx1)[hi][XOWN : XOWN + BY, :]
        k = X1 + 2
        now = jnp.where(first[own_rows], row, before[1, k, own_rows, :])
        widen(k, level1_plane(1 + H1 // 2 + X1 // 2, 0), now, before[1, k, BY:YE, :])
        row = (gx0, gx1)[lo][XOWN : XOWN + BY, :]
        now = jnp.where(first[own_rows], before[1, 1, own_rows, :], row)
        widen(1, level1_plane(H1 // 2, 1), now, before[1, 1, BY:YE, :])

    by_parity("gx", action_x)
    for k in (0, NF - 1):
        u[1, k] = before[1, k]
    refs = (c, fin, fout, fyp, fym, fzp, fzm, src, scr, free)
    groups(1, X1 + 2, GF, lambda at: fine_half(u, at, GF, 0, refs))

    def last(at):
        n = 4
        new = fine_new(u, at, n, 1, refs)[:, own_rows]
        even = u[0, pl.ds(at, n), own_rows, :]
        mask = first[own_rows]
        for k in range(n):
            to = pl.multiple_of((at - 2 + k) * 2 * BY, 8)
            result[pl.ds(to, BY), :] = jnp.where(mask, even[k], new[k])
            result[pl.ds(to + BY, BY), :] = jnp.where(mask, new[k], even[k])

    groups(2, X1, 4, last)


def swap(pair, axis):
    count = lax.axis_size(axis)
    got = [None, None]
    for first in (1, 0):
        route = []
        for i in range(first, count - 1, 2):
            route += [(i, i + 1), (i + 1, i)]
        got[first] = lax.ppermute(pair[first], axis, route)
    return tuple(got)


def body(source, permittivity, screening, potential, fixed_cell):
    gx, gy = lax.axis_size("gx"), lax.axis_size("gy")
    args = [a.reshape(BX * BY, NL) for a in (potential, permittivity, source, screening, fixed_cell)]
    args = [pltpu.with_memory_space_constraint(a, pltpu.HBM) for a in args]

    whole = (sds(BX * BY, NL),) * 4 + (jax.ShapeDtypeStruct((BX * BY, NL), jnp.int32),)
    *args, p2, y0, y1 = call(
        pack_y,
        whole + (sds(8, NL),) + (sds(YROWS + 8, NL),) * 2,
        [pltpu.SemaphoreType.DMA((5,)), pltpu.VMEM((BX // 4 * BY, NL), F32), pltpu.VMEM((8, NL), F32)],
        hbm=5,
    )(*args)
    y0 = (y0, y1)
    y0 = swap(y0, "gy")
    *halos, x0, x1 = call(pack_x, (sds(BX * 8, NL),) * 5 + (sds(XROWS + 24, NL),) * 2)(*args, p2, *y0)
    gotx = swap((x0, x1), "gx")

    ext, one = (2, NF, YE, NL), (NF, YE, NL)
    fine = call(
        fine_pre,
        (sds(*ext),) * 2 + (sds(*one),) + (sds(*ext),) * 8
        + (sds(X1 // 2, 8, NL), sds(2, X1 // 2, 8, NL)) + (sds(YMSG, NL),) * 2,
        [
            pltpu.VMEM(ext, F32),
            pltpu.VMEM((X1 * BY, NL), F32),
            pltpu.VMEM((X1 * BY, NL), F32),
            pltpu.VMEM(((X1 + 2) * YE, NL), F32),
            pltpu.VMEM((X1 + 2, 8, NL), F32),
        ],
    )(*args, *halos, *y0, *gotx)
    state, (c1, g1, m0, m1) = fine[:11], fine[11:]
    goty1 = swap((m0, m1), "gy")
    x1msg = call(pack_x1, (sds(XMSG, NL),) * 2)(m0, m1, *goty1, *gotx, state[0])
    gotx1 = swap(x1msg, "gx")

    mid, mid1 = (2, NM, YE, NL), (NM, YE, NL)
    *level1, message = call(
        mid_pre,
        (sds(*mid),) * 3 + (sds(*mid1),) + (sds(*mid),) * 5 + (sds(gx * gy, 16, NL),),
        [
            pltpu.VMEM(mid, F32),
            pltpu.VMEM((G1 // 2 * YE, NL), F32),
            pltpu.VMEM((X1 // 2 * 8, NL), F32),
            pltpu.VMEM((X1 // 2 * 8, NL), F32),
            pltpu.VMEM((3, G1 // 2, NL), F32),
            pltpu.VMEM((24, NL), F32),
        ],
    )(m0, *goty1, *gotx1, c1, g1)

    gathered = lax.all_to_all(message, ("gx", "gy"), 0, 0).reshape(gx, gy, 16, NL)
    wx, wy = min(gx, 6), min(gy, 8)
    if (wx, wy) != (gx, gy):
        first = (*window(gx, gy, wx, wy)[:2], 0, 0)
        gathered = lax.dynamic_slice(gathered, first, (wx, wy, 16, NL))

    inputs = (gathered, p2, *y0, *gotx, *level1, *state, *goty1, *gotx1)
    result = pl.pallas_call(
        finish_kernel(len(inputs), (gx, gy, wx, wy)),
        out_shape=sds(BX * BY, NL),
        scratch_shapes=[
            pltpu.VMEM((2, wy + 2, wx * 4, NL), F32),
            pltpu.VMEM((2, wy + 2, wx * 4, NL), F32),
            pltpu.VMEM((2, wy, wx * 4, NL), F32),
            pltpu.VMEM((2, wy, wx * 4, NL), F32),
            pltpu.VMEM((2, 6, wy, wx * 4, NL), F32),
            pltpu.VMEM((wy + 6, wx + 4, 8, NL), F32),
            pltpu.VMEM((NF * YE, NL), F32),
            pltpu.VMEM(mid, F32),
            pltpu.VMEM(ext, F32),
            pltpu.VMEM((BX // 2 * 8, NL), F32),
        ],
        compiler_params=pltpu.CompilerParams(vmem_limit_bytes=24 << 20),
        name="finish",
    )(*inputs)
    return result.reshape(BX, BY, NL)


def window(gx, gy, wx, wy):
    ix, iy = lax.axis_index("gx"), lax.axis_index("gy")
    fx = jnp.clip(ix - 2, 0, gx - wx)
    fy = jnp.clip(iy - 3, 0, gy - wy)
    return fx, fy, ix - fx, iy - fy


def finish_kernel(count, sizes):
    def kernel(*refs):
        ins, result, scratch = list(refs[:count]), refs[count], list(refs[1 + count :])
        finish(window(*sizes)[2:], *ins, result, *scratch)

    return kernel


def solution(mesh):
    placed = (P("gx", "gy", None),) * 5

    return jax.shard_map(body, mesh=mesh, in_specs=placed, out_specs=P("gx", "gy", None), check_vma=False)
```

```python
import jax
import jax.numpy as jnp
from jax import lax
from jax.experimental import pallas as pl
from jax.experimental.pallas import tpu as pltpu
from jax.sharding import PartitionSpec as P

F32 = jnp.float32
BX, BY, NL = 32, 16, 128
YE = 24
X1 = BX // 2
H1 = 8
G1 = X1 + 2 * H1
NF = X1 + 4
NM = G1 // 2 + 2
GF = 6
GM = 8
LN2 = 0.6931471805599453


def rot(value, shift, axis):
    return pltpu.roll(value, shift % value.shape[axis], axis)


def iota(shape, axis):
    return lax.broadcasted_iota(jnp.int32, shape, axis)


def sds(*shape):
    return jax.ShapeDtypeStruct(shape, F32)


def by_parity(axis, action):
    odd = lax.axis_index(axis) % 2

    @pl.when(odd == 0)
    def _():
        action(0, 1)

    @pl.when(odd == 1)
    def _():
        action(1, 0)


def call(kernel, out_shape, scratch=(), vmem=24, hbm=0):
    specs = {"in_specs": [pl.BlockSpec(memory_space=pltpu.HBM)] * hbm} if hbm else {}
    return pl.pallas_call(
        kernel,
        out_shape=out_shape,
        **specs,
        scratch_shapes=list(scratch),
        compiler_params=pltpu.CompilerParams(vmem_limit_bytes=vmem << 20),
    )


YROWS = 10 * BX
XROWS = 12 * 8
FIELDS = (3, 3, 2, 2, 2)


def split_rows(ref, at):
    one, two = ref[pl.ds(at, 4, stride=2), :], ref[pl.ds(at + 1, 4, stride=2), :]
    lane = iota((4, NL), 1)
    even = (lane % 4 + lane // 4) % 2 == 0
    return jnp.concatenate([jnp.where(even, one, two), jnp.where(even, two, one)], axis=0)


def pack_y(hpot, hper, hsrc, hscr, hfix, pot, per, src, scr, fix, p2, out0, out1, xm0, xm1, sems, t, pk):
    outs, mains = (out0, out1), (xm0, xm1)
    pairs = ((hpot, pot), (hper, per), (hsrc, src), (hscr, scr), (hfix, fix))
    copies = [pltpu.make_async_copy(a, b, sems.at[k]) for k, (a, b) in enumerate(pairs)]
    for copy in copies:
        copy.start()
    for copy in copies:
        copy.wait()
    zlane = iota((BX // 2, NL), 1)

    def free_of(value):
        return jnp.where(value == 0, F32(1.0), F32(0.0))

    def row(ref, r):
        return ref[pl.ds(r, BX, stride=BY), :]

    def half(ref, r, parity):
        even = ref[pl.ds(r, BX // 2, stride=2 * BY), :]
        odd = ref[pl.ds(BY + r, BX // 2, stride=2 * BY), :]
        return jnp.where((r + zlane) % 2 == parity, even, odd)

    def side(out, r1, r2, r3):
        rows = [
            row(pot, r1), row(per, r1), row(src, r1), row(scr, r1), free_of(row(fix, r1)),
            row(pot, r2), row(per, r2), free_of(row(fix, r2)),
        ]
        for k, value in enumerate(rows):
            out[BX * k : BX * (k + 1), :] = value
        base = BX * len(rows)
        for k, value in enumerate([half(pot, r3, 1), half(per, r3, 1), half(src, r2, 0), half(scr, r2, 0)]):
            out[base + k * BX // 2 : base + (k + 1) * BX // 2, :] = value

    v = per[...].reshape(BX // 4, 4, BY, NL)
    v = (v[:, 0] + v[:, 1]) + (v[:, 2] + v[:, 3])
    t[...] = lane_pairs(lane_pairs(v, 1), 2).reshape(BX // 4 * BY, NL)
    n2 = BX // 4
    lane = iota((n2, NL), 1)
    total = None
    for j in range(4):
        r = [t[pl.ds(4 * j + k, n2, stride=BY), :] for k in range(4)]
        value = (r[0] + r[1]) + (r[2] + r[3])
        total = value if total is None else jnp.where(lane % 4 == j, value, total)
    pk[...] = F32(1.0 / 64) * total
    p2[...] = split_rows(pk, 0)

    def action(hi, lo):
        side(outs[hi], BY - 1, BY - 2, BY - 3)
        side(outs[lo], 0, 1, 2)
        for out in outs:
            out[YROWS : YROWS + 8, :] = p2[...]

    by_parity("gy", action)

    def slab(out, planes):
        k = 0
        for ref, depth in zip((pot, per, src, scr, fix), FIELDS, strict=True):
            for x in planes[:depth]:
                value = ref[BY * x : BY * (x + 1), :]
                out[BY * k : BY * (k + 1), :] = free_of(value) if ref is fix else value
                k += 1

    def action_x(hi, lo):
        slab(mains[hi], (BX - 1, BX - 2, BX - 3))
        slab(mains[lo], (0, 1, 2))

    by_parity("gx", action_x)


def pack_x(p2, got0, got1, hpot, hper, hsrc, hscr, hfree, out0, out1):
    gots, outs = (got0, got1), (out0, out1)
    halos = (hpot, hper, hsrc, hscr, hfree)
    for h in halos:
        h[...] = jnp.zeros_like(h)

    def place(got, slots):
        def whole(ref, k, slot):
            ref[pl.ds(slot, BX, stride=8), :] = got[BX * k : BX * (k + 1), :]

        def halved(ref, k, slot):
            value = got[BX * 8 + k * BX // 2 : BX * 8 + (k + 1) * BX // 2, :]
            ref[pl.ds(slot, BX // 2, stride=16), :] = value
            ref[pl.ds(8 + slot, BX // 2, stride=16), :] = value

        s1, s2, s3 = slots
        for k, ref in enumerate(halos):
            whole(ref, k, s1)
        whole(hpot, 5, s2)
        whole(hper, 6, s2)
        whole(hfree, 7, s2)
        halved(hpot, 0, s3)
        halved(hper, 1, s3)
        halved(hsrc, 2, s2)
        halved(hscr, 3, s2)

    def action_y(hi, lo):
        place(gots[hi], (0, 1, 2))
        place(gots[lo], (7, 6, 5))

    by_parity("gy", action_y)

    def slab(out, planes):
        k = 0
        for h, depth in zip(halos, FIELDS, strict=True):
            for x in planes[:depth]:
                out[8 * k : 8 * (k + 1), :] = h[8 * x : 8 * (x + 1), :]
                k += 1

    def action_p(hi, lo):
        for out in outs:
            out[XROWS : XROWS + 8, :] = p2[...]
            out[XROWS + 8 : XROWS + 16, :] = gots[hi][YROWS : YROWS + 8, :]
            out[XROWS + 16 : XROWS + 24, :] = gots[lo][YROWS : YROWS + 8, :]

    by_parity("gy", action_p)

    def action_x(hi, lo):
        slab(outs[hi], (BX - 1, BX - 2, BX - 3))
        slab(outs[lo], (0, 1, 2))

    by_parity("gx", action_x)


def nonlinear(u, scr):
    up = jnp.exp(u - F32(LN2))
    down = jnp.exp(-u - F32(LN2))
    return scr * (up - down), scr * (up + down)


def colour_mask(n, zstep):
    shape = (n, YE, NL)
    return (iota(shape, 1) + iota(shape, 2) // zstep) % 2 == 0


def beside_of(other, colour, faces, at, n, zstep):
    fin, fout, fyp, fym, fzp, fzm = faces
    here = pl.ds(at, n)
    v = other[1 - colour, pl.ds(at - 1, n + 2)]
    mid = v[1 : n + 1]
    first = colour_mask(n, zstep)
    across = jnp.where(first, v[:n], v[2:]) if colour == 0 else jnp.where(first, v[2:], v[:n])
    return (
        (fin[here] * mid + fout[colour, here] * across)
        + (fyp[colour, here] * rot(mid, -1, 1) + fym[colour, here] * rot(mid, 1, 1))
        + (fzp[colour, here] * rot(mid, -zstep, 2) + fzm[colour, here] * rot(mid, zstep, 2))
    )


def pairs_of(u, at, n, colour, refs):
    c, fin, fout, fyp, fym, fzp, fzm, src, scr, _ = refs
    here = pl.ds(at, n)
    plane = u[colour, here]
    sh, ch = nonlinear(plane, scr[colour, here])
    centre = c[colour, here]
    beside = beside_of(u, colour, (fin, fout, fyp, fym, fzp, fzm), at, n, 1)
    return plane, centre * plane - beside + sh - src[colour, here], centre, ch


def fine_new(u, at, n, colour, refs):
    plane, value, centre, ch = pairs_of(u, at, n, colour, refs)
    return jnp.where(refs[-1][colour, pl.ds(at, n)] > 0.5, plane - value / (centre + ch), plane)


def fine_half(u, at, n, colour, refs):
    u[colour, pl.ds(at, n)] = fine_new(u, at, n, colour, refs)


def groups(first, count, n, step):
    assert count % n == 0

    def one(g, _):
        step(first + g * n)
        return 0

    lax.fori_loop(0, count // n, one, 0)


def faces_of(p, at, n, scale, zstep, fin, fout, fyp, fym, fzp, fzm):
    here = pl.ds(at, n)
    lane = iota((n, YE, NL), 2)
    first = colour_mask(n, zstep)
    half = F32(0.5 * scale)
    for colour in (0, 1):
        plane = p[colour, here]
        v = p[1 - colour, pl.ds(at - 1, n + 2)]
        mid = v[1 : n + 1]
        across = jnp.where(first, v[:n], v[2:]) if colour == 0 else jnp.where(first, v[2:], v[:n])
        if colour == 0:
            fin[here] = half * (plane + mid)
        fout[colour, here] = half * (plane + across)
        fyp[colour, here] = half * (plane + rot(mid, -1, 1))
        fym[colour, here] = half * (plane + rot(mid, 1, 1))
        fzp[colour, here] = jnp.where(lane >= NL - zstep, F32(0.0), half * (plane + rot(mid, -zstep, 2)))
        fzm[colour, here] = jnp.where(lane < zstep, F32(0.0), half * (plane + rot(mid, zstep, 2)))


def lane_pairs(value, step):
    lane = iota(value.shape, value.ndim - 1)
    return value + jnp.where((lane // step) % 2 == 0, rot(value, -step, value.ndim - 1), rot(value, step, value.ndim - 1))


def fine_pre(pot, per, src, scr, fix, hpot, hper, hsrc, hscr, hfree, goty0, goty1, xm0, xm1, got0, got1,
             u, c, fin, fout, fyp, fym, fzp, fzm, esrc, escr, efree, csum, g1, m0, m1, n0, n1,
             ep, tr, tc, tp, p1):
    gots, mains, outs, nexts = (got0, got1), (xm0, xm1), (m0, m1), (n0, n1)
    first = colour_mask(1, 1)[0]

    def own(k, _):
        for ref, h, ext in ((pot, hpot, u), (per, hper, ep), (src, hsrc, esrc), (scr, hscr, escr), (fix, hfree, efree)):
            value = ref[pl.ds(pl.multiple_of(2 * k * BY, 8), 2 * BY), :]
            if ref is fix:
                value = jnp.where(value == 0, F32(1.0), F32(0.0))
            halo = h[pl.ds(pl.multiple_of(16 * k, 8), 16), :]
            for rows, one, two in (
                (slice(0, BY), value[:BY], value[BY:]),
                (slice(BY, YE), halo[:8], halo[8:]),
            ):
                ext[0, k + 2, rows, :] = jnp.where(first[rows], one, two)
                ext[1, k + 2, rows, :] = jnp.where(first[rows], two, one)
        return 0

    lax.fori_loop(0, X1, own, 0, unroll=2)

    def place(main, got, near, far, flip):
        k = 0
        for ext, depth in zip((u, ep, esrc, escr, efree), FIELDS, strict=True):
            planes = []
            for _ in range(depth):
                rows = main[BY * k : BY * (k + 1), :]
                planes.append(jnp.concatenate([rows, got[8 * k : 8 * (k + 1), :]], axis=0))
                k += 1
            one, two = (planes[1], planes[0]) if flip else (planes[0], planes[1])
            ext[0, near] = jnp.where(first, one, two)
            ext[1, near] = jnp.where(first, two, one)
            third = planes[2] if depth == 3 else jnp.zeros((YE, NL), F32)
            ext[0, far] = third
            ext[1, far] = third

    def action_x(hi, lo):
        place(mains[hi], gots[hi], X1 + 2, X1 + 3, False)
        place(mains[lo], gots[lo], 1, 0, True)

    by_parity("gx", action_x)
    refs = (c, fin, fout, fyp, fym, fzp, fzm, esrc, escr, efree)

    def begin(at):
        n = GF
        faces_of(ep, at, n, 1.0, 1, fin, fout, fyp, fym, fzp, fzm)
        here = pl.ds(at, n)
        lane = iota((n, YE, NL), 2)
        for colour in (0, 1):
            ends = jnp.where((lane == 0) | (lane == NL - 1), F32(0.5) * ep[colour, here], F32(0.0))
            c[colour, here] = (
                (fin[here] + fout[colour, here]) + (fyp[colour, here] + fym[colour, here])
                + (fzp[colour, here] + fzm[colour, here]) + ends
            )
        fine_half(u, at, n, 0, refs)

    groups(1, X1 + 2, GF, begin)
    groups(1, X1 + 2, GF, lambda at: fine_half(u, at, GF, 1, refs))

    def down(at):
        n = 4
        left, react = F32(0.0), F32(0.0)
        for colour in (0, 1):
            _, value, _, ch = pairs_of(u, at, n, colour, refs)
            left += jnp.where(efree[colour, pl.ds(at, n)] > 0.5, -value, F32(0.0))
            react += ch
        to = pl.multiple_of((at - 2) * BY, 8)
        tr[pl.ds(to, n * BY), :] = lane_pairs(left[:, 0:BY], 1).reshape(n * BY, NL)
        tc[pl.ds(to, n * BY), :] = lane_pairs(react[:, 0:BY], 1).reshape(n * BY, NL)

    groups(2, X1, 4, down)

    def coarse_p(k, _):
        at = pl.multiple_of(k * YE, 8)
        tp[pl.ds(at, YE), :] = lane_pairs(ep[0, k + 1] + ep[1, k + 1], 1)
        return 0

    lax.fori_loop(0, X1 + 2, coarse_p, 0, unroll=2)

    eighth = F32(0.125)
    sub = iota((8, NL), 0)
    lane = iota((8, NL), 1)

    def gather_p(k, _):
        p1[k] = eighth * (tp[pl.ds(k * YE, 8, stride=2), :] + tp[pl.ds(k * YE + 1, 8, stride=2), :])
        return 0

    lax.fori_loop(0, X1 + 2, gather_p, 0, unroll=2)

    first8 = (sub + lane // 2) % 2 == 0

    def coarse(x1):
        k = x1 + 1
        p = p1[k]
        base = k * YE
        high = eighth * (tp[pl.ds(base + 2, 8, stride=2), :] + tp[pl.ds(base + 3, 8, stride=2), :])
        edge = tp[pl.ds(pl.multiple_of(base + 16, 8), 8), :]
        edge = eighth * (edge + rot(edge, 1, 0))
        low = jnp.where(sub == 0, rot(edge, 1, 0), rot(p, 1, 0))
        front = jnp.where(lane >= NL - 2, F32(0.0), rot(p, -2, 1))
        back = jnp.where(lane < 2, F32(0.0), rot(p, 2, 1))
        near = (p1[k + 1] + p1[k - 1]) + (high + low) + (front + back)
        centre = F32(3.0) * p + F32(0.5) * near
        at = x1 * BY
        r = eighth * (tr[pl.ds(at, 8, stride=2), :] + tr[pl.ds(at + 1, 8, stride=2), :])
        react = eighth * (tc[pl.ds(at, 8, stride=2), :] + tc[pl.ds(at + 1, 8, stride=2), :])
        diag = F32(0.25) * centre + react
        message = jnp.where(lane % 2 == 0, r, F32(1.0) / diag)
        m0[pl.ds(pl.multiple_of(x1 * 8, 8), 8), :] = message
        m1[pl.ds(pl.multiple_of(x1 * 8, 8), 8), :] = message
        return diag, react

    def make(k, _):
        diag0, react0 = coarse(2 * k)
        diag1, react1 = coarse(2 * k + 1)
        csum[k] = react0 + react1
        g1[0, k] = jnp.where(first8, diag0, diag1)
        g1[1, k] = jnp.where(first8, diag1, diag0)
        return 0

    lax.fori_loop(0, X1 // 2, make, 0)

    for a in range(X1 // 2):
        message = jnp.where(lane % 2 == 0, p1[1 + 2 * a], p1[2 + 2 * a])
        for m in outs:
            m[X1 * 8 + 8 * a : X1 * 8 + 8 * a + 8, :] = message

    base = X1 * 8 + X1 * 4

    def odd_row(out, y):
        out[base : base + X1, :] = u[1, pl.ds(2, X1), y, :]

    def slab(out, at, x):
        out[0 : H1 * 8, :] = m0[8 * at : 8 * (at + H1), :]
        row = X1 * 8 + 4 * at
        out[H1 * 8 : H1 * 12, :] = m0[row : row + H1 * 4, :]
        out[XOWN:XMAIN, :] = u[1, x, 0:BY, :]

    def action_next(hi, lo):
        slab(nexts[hi], X1 - H1, X1 + 1)
        slab(nexts[lo], 0, 2)

    by_parity("gx", action_next)

    def action_y(hi, lo):
        odd_row(outs[hi], BY - 2)
        odd_row(outs[lo], 1)
        outs[hi][base + X1 : base + X1 + 8, :] = (goty0, goty1)[lo][YROWS : YROWS + 8, :]
        outs[lo][base + X1 : base + X1 + 8, :] = (goty0, goty1)[hi][YROWS : YROWS + 8, :]

    by_parity("gy", action_y)


def halo_rows(dx):
    return (16 * (dx - 1), 2) if dx < 5 else (64 + 8 * (dx - 5), 1)


def halo_pair(t):
    return (96 + 16 * t, 2) if t < 2 else (128 + 8 * (t - 2), 1)


P2AT = 144
YMSG = X1 * 8 + X1 * 4 + BX // 2 + 8
XOWN = H1 * 8 + (H1 // 2) * 8
XMAIN = XOWN + BY
XMSG = P2AT + 40


def pack_x1(got0, got1, fx0, fx1, _, __, out0, out1):
    gots, outs, fines = (got0, got1), (out0, out1), (fx0, fx1)
    odd_y = lax.axis_index("gy") % 2
    upper = iota((8, NL), 0) < 4

    def go(hi, lo):
        def put(out, at, count, row):
            above, below = gots[hi][row : row + 8, :], gots[lo][row : row + 8, :]
            if count == 2:
                out[at : at + 8, :] = above
                out[at + 8 : at + 16, :] = below
            else:
                out[at : at + 8, :] = jnp.where(upper, above, below)

        def slab(out, near, step, behind):
            for dx in range(1, H1 + 1):
                put(out, *halo_rows(dx), 8 * (near + step * (dx - 1)))
            for t in range(H1 // 2):
                put(out, *halo_pair(t), X1 * 8 + 8 * (near // 2 + step * t))
            out[P2AT : P2AT + 8, :] = gots[hi][YMSG - 8 : YMSG, :]
            out[P2AT + 8 : P2AT + 16, :] = gots[lo][YMSG - 8 : YMSG, :]
            out[P2AT + 16 : P2AT + 40, :] = behind[XROWS : XROWS + 24, :]

        def action(xhi, xlo):
            slab(outs[xhi], X1 - 1, -1, fines[xlo])
            slab(outs[xlo], 0, 1, fines[xhi])

        by_parity("gx", action)

    @pl.when(odd_y == 0)
    def _():
        go(0, 1)

    @pl.when(odd_y == 1)
    def _():
        go(1, 0)


def coarse_half(e, r, d, at, n, colour, faces, zstep):
    here = pl.ds(at, n)
    e[colour, here] = (r[colour, here] + beside_of(e, colour, faces, at, n, zstep)) * d[colour, here]


def dup_even(value):
    lane = iota(value.shape, value.ndim - 1)
    return jnp.where(lane % 2 == 0, value, rot(value, 1, value.ndim - 1))


def dup_odd(value):
    lane = iota(value.shape, value.ndim - 1)
    return jnp.where(lane % 2 == 1, value, rot(value, -1, value.ndim - 1))


def mid_pre(m0, gy0, gy1, xm0, xm1, gx0, gx1, csum, g1,
            e, r, d, fin, fout, fyp, fym, fzp, fzm, msg,
            p, t, tr, tc, pc, pk):
    gys, gxs, mains = (gy0, gy1), (gx0, gx1), (xm0, xm1)
    odd_y = lax.axis_index("gy") % 2
    first = colour_mask(1, 2)[0]

    def put(k, rows, one, two, both):
        mask = first[rows]
        for colour in (0, 1):
            a, b = (one, two) if colour == 0 else (two, one)
            value = jnp.where(mask, a, b)
            r[colour, k, rows, :] = dup_even(value)
            d[colour, k, rows, :] = dup_odd(value)
        a, b = dup_even(both), dup_odd(both)
        p[0, k, rows, :] = jnp.where(mask, a, b)
        p[1, k, rows, :] = jnp.where(mask, b, a)

    def own(hi, lo):
        def pairs(k, _):
            for j, ref in enumerate((m0, gys[hi], gys[lo])):
                two = ref[pl.ds(pl.multiple_of(16 * k, 8), 16), :]
                both = ref[pl.ds(pl.multiple_of(X1 * 8 + 8 * k, 8), 8), :]
                put(1 + H1 // 2 + k, slice(8 * j, 8 * j + 8), two[:8], two[8:], both)
            return 0

        lax.fori_loop(0, X1 // 2, pairs, 0, unroll=2)

    @pl.when(odd_y == 0)
    def _():
        own(0, 1)

    @pl.when(odd_y == 1)
    def _():
        own(1, 0)

    def beyond(main, ref, at, far):
        def whole(row, start, count):
            own_rows = main[row : row + 8, :]
            above = ref[start : start + 8, :]
            below = ref[start + 8 : start + 16, :] if count == 2 else above
            return jnp.concatenate([own_rows, above, below], axis=0)

        for k in range(H1 // 2):
            one, two = (whole(8 * a, *halo_rows(H1 - a if far else a + 1)) for a in (2 * k, 2 * k + 1))
            both = whole(H1 * 8 + 8 * k, *halo_pair(H1 // 2 - 1 - k if far else k))
            put(at + k, slice(0, YE), one, two, both)

    def action(hi, lo):
        beyond(mains[hi], gxs[hi], 1 + H1 // 2 + X1 // 2, False)
        beyond(mains[lo], gxs[lo], 1, True)

    by_parity("gx", action)
    for ref in (p, e):
        for colour in (0, 1):
            ref[colour, 0] = jnp.zeros((YE, NL), F32)
            ref[colour, NM - 1] = jnp.zeros((YE, NL), F32)
    faces = (fin, fout, fyp, fym, fzp, fzm)

    def begin(at):
        here = pl.ds(at, 2)
        faces_of(p, at, 2, 0.25, 2, *faces)
        e[0, here] = r[0, here] * d[0, here]

    groups(1, NM - 2, 2, begin)
    for colour in (1, 0, 1):
        groups(1, NM - 2, GM, lambda at, colour=colour: coarse_half(e, r, d, at, GM, colour, faces, 2))

    def down(at):
        n = 4
        here = pl.ds(at, n)
        k = pl.ds(at - 1 - H1 // 2, n)
        left = F32(0.0)
        for colour in (0, 1):
            part = r[colour, here] + beside_of(e, colour, faces, at, n, 2)
            left += part[:, 0:8] - g1[colour, k] * e[colour, here, 0:8, :]
        to = pl.multiple_of((at - 1 - H1 // 2) * 8, 8)
        tr[pl.ds(to, n * 8), :] = lane_pairs(left, 2).reshape(n * 8, NL)
        tc[pl.ds(to, n * 8), :] = lane_pairs(csum[k], 2).reshape(n * 8, NL)

    groups(1 + H1 // 2, X1 // 2, 4, down)

    def coarse_p(x2, _):
        t[pl.ds(pl.multiple_of(x2 * YE, 8), YE), :] = lane_pairs(p[0, x2 + 1] + p[1, x2 + 1], 2)
        return 0

    lax.fori_loop(0, G1 // 2, coarse_p, 0, unroll=2)

    eighth = F32(0.125)
    n2, m2 = X1 // 2, G1 // 2

    def compact(ref, first, rows, stride):
        lane = iota((rows, NL), 1)
        out = None
        for j in range(4):
            value = ref[pl.ds(first + 2 * j, rows, stride=stride), :] + ref[pl.ds(first + 2 * j + 1, rows, stride=stride), :]
            out = value if out is None else jnp.where(lane % 4 == j, value, out)
        return eighth * out

    r2 = compact(tr, 0, n2, 8)
    react2 = compact(tc, 0, n2, 8)
    for k in range(3):
        pc[k] = compact(t, 8 * k, m2, YE)
    h2 = H1 // 2
    centre_p = pc[0, h2 : h2 + n2, :]
    j4 = iota((n2, NL), 1) % 4
    lane = iota((n2, NL), 1)
    high = jnp.where(j4 < 3, rot(centre_p, -1, 1), rot(pc[1, h2 : h2 + n2, :], 3, 1))
    low = jnp.where(j4 > 0, rot(centre_p, 1, 1), rot(pc[2, h2 : h2 + n2, :], -3, 1))
    front = jnp.where(lane >= NL - 4, F32(0.0), rot(centre_p, -4, 1))
    back = jnp.where(lane < 4, F32(0.0), rot(centre_p, 4, 1))
    near = (pc[0, h2 + 1 : h2 + 1 + n2, :] + pc[0, h2 - 1 : h2 - 1 + n2, :]) + (high + low) + (front + back)
    diag2 = F32(0.0625) * (F32(3.0) * centre_p + F32(0.5) * near) + react2
    for k, value in enumerate((r2, F32(1.0) / diag2, centre_p)):
        pk[8 * k : 8 * k + 8, :] = value
    r2, inverse2, own_p = (split_rows(pk, 8 * k) for k in range(3))
    near_rows = iota((8, NL), 1) % 4 >= 2
    ahead = jnp.where(near_rows, r2, rot(own_p, -2, 1))
    behind = jnp.where(near_rows, rot(own_p, 2, 1), r2)
    count = lax.axis_size("gy")
    place = lax.axis_index("gy")

    def every(k, _):
        step = k % count - place
        msg[k, 0:8, :] = jnp.where(step == 3, ahead, jnp.where(step == -3, behind, r2))
        msg[k, 8:16, :] = inverse2
        return 0

    lax.fori_loop(0, msg.shape[0], every, 0, unroll=2)


def finish(at, got, p2own, yf0, yf1, xf0, xf1, e, r, d, fin1, fout1, fyp1, fym1, fzp1, fzm1,
           before, c, fin, fout, fyp, fym, fzp, fzm, src, scr, free, gy0, gy1, xm0, xm1, gx0, gx1,
           result,
           e2, p2, r2, d2, k2, blk, tx, eu, u, hal):
    wx, wy = got.shape[0], got.shape[1]
    rows = wx * 4
    ox, oy = at
    blk[...] = jnp.zeros_like(blk)
    e2[...] = jnp.zeros_like(e2)

    def keep(da, db, ref, first):
        blk[oy + db + 3, ox + da + 2] = ref[first : first + 8, :]

    keep(0, 0, p2own, 0)

    def blocks_y(hi, lo):
        for db, k in ((1, hi), (-1, lo)):
            keep(0, db, (yf0, yf1)[k], YROWS)
            keep(0, 2 * db, (gy0, gy1)[k], YMSG - 8)

    by_parity("gy", blocks_y)

    def blocks_x(hi, lo):
        for da, k in ((1, hi), (-1, lo)):
            fine, mid = (xf0, xf1)[k], (gx0, gx1)[k]
            for n, db in enumerate((0, 1, -1)):
                keep(da, db, fine, XROWS + 8 * n)
                keep(2 * da, db, mid, P2AT + 16 + 8 * n)
            keep(da, 2, mid, P2AT)
            keep(da, -2, mid, P2AT + 8)

    by_parity("gx", blocks_x)
    l4 = iota((8, NL), 1) % 4
    for db in (3, -3):

        @pl.when((oy + db >= 0) & (oy + db < wy))
        def _(db=db):
            for a in range(wx):
                value = got[a, oy + db, 0:8, :]
                value = jnp.where(l4 < 2, rot(value, -2, 1), F32(0.0)) if db > 0 else jnp.where(l4 >= 2, rot(value, 2, 1), F32(0.0))
                blk[oy + db + 3, a + 2] = value

    def spread(b, _):
        for a in range(wx):
            for colour in (0, 1):
                own, to = slice(4 * colour, 4 * colour + 4), slice(4 * a, 4 * a + 4)
                r2[colour, b, to, :] = got[a, b, own, :]
                d2[colour, b, to, :] = got[a, b, 8 + 4 * colour : 12 + 4 * colour, :]
                p2[colour, b + 1, to, :] = blk[b + 3, a + 2, own, :]
        return 0

    lax.fori_loop(0, wy, spread, 0, unroll=2)
    for b in (0, wy + 1):
        for colour in (0, 1):
            p2[colour, b] = jnp.zeros((rows, NL), F32)
    shape = (wy, rows, NL)
    sub, lane = iota(shape, 1), iota(shape, 2)
    j4 = lane % 4
    even = (j4 + lane // 4) % 2 == 0

    def around(ref, colour):
        v = ref[1 - colour]
        mid = v[1 : wy + 1]
        one, two = rot(mid, 1, 1), rot(mid, -1, 1)
        return (
            mid,
            jnp.where(even, one, two) if colour == 0 else jnp.where(even, two, one),
            jnp.where(j4 < 3, rot(mid, -1, 2), rot(v[2:], 3, 2)),
            jnp.where(j4 > 0, rot(mid, 1, 2), rot(v[:wy], -3, 2)),
            rot(mid, -4, 2), rot(mid, 4, 2),
        )

    for colour in (0, 1):
        at_first = even if colour == 0 else ~even
        outside = (at_first & (sub == 0)) | (~at_first & (sub == rows - 1))
        edges = (None, outside, None, None, lane >= NL - 4, lane < 4)
        mine = p2[colour, 1 : wy + 1]
        for k, (value, edge) in enumerate(zip(around(p2, colour), edges, strict=True)):
            face = F32(0.03125) * (mine + value)
            k2[colour, k] = face if edge is None else jnp.where(edge, F32(0.0), face)
    e2[0, 1 : wy + 1] = r2[0] * d2[0]

    def half2(colour):
        total = r2[colour]
        for k, value in enumerate(around(e2, colour)):
            total = total + k2[colour, k] * value
        e2[colour, 1 : wy + 1] = total * d2[colour]

    half2(1)

    def sweep2(_, carry):
        half2(0)
        half2(1)
        return carry

    lax.fori_loop(0, 3, sweep2, 0)

    s8, l8 = iota((8, NL), 0), iota((8, NL), 1)
    even8 = (l8 % 4 + l8 // 4) % 2 == 0
    start = 4 * ox - 2
    inside = (s8 + start >= 0) & (s8 + start < rows)
    for k, step in enumerate((0, 1, -1)):
        near = []
        for colour in (0, 1):
            block = pltpu.roll(e2[colour, oy + step + 1], (rows - start) % rows, 0)[0:8]
            near.append(jnp.where(inside, block, F32(0.0)))
        planes = (jnp.where(even8, near[0], near[1]), jnp.where(even8, near[1], near[0]))
        for second in (0, 1):
            for j in range(4):
                value = jnp.where(l8 % 4 == 0, rot(planes[second], -j, 1), F32(0.0))
                value = value + rot(value, 1, 1)
                value = value + rot(value, 2, 1)
                for y in (0, 1):
                    tx[pl.ds(second * YE + 8 * k + 2 * j + y, 8, stride=2 * YE), :] = value

    def correct(x2, _):
        value = tx[pl.ds(pl.multiple_of(x2 * YE, 8), YE), :]
        for colour in (0, 1):
            eu[colour, x2 + 1] = e[colour, x2 + 1] + value
        return 0

    lax.fori_loop(0, G1 // 2, correct, 0, unroll=2)
    faces1 = (fin1, fout1, fyp1, fym1, fzp1, fzm1)
    for at1, count, n, colour in ((3, 12, 4, 0), (3, 12, 4, 1), (4, 10, 5, 0), (4, 10, 5, 1)):
        groups(at1, count, n, lambda at, n=n, colour=colour: coarse_half(eu, r, d, at, n, colour, faces1, 2))

    base = X1 * 8 + X1 * 4

    def action_y(hi, lo):
        hal[pl.ds(1, X1, stride=8), :] = (gy0, gy1)[hi][base : base + X1, :]
        hal[pl.ds(6, X1, stride=8), :] = (gy0, gy1)[lo][base : base + X1, :]

    by_parity("gy", action_y)
    first = colour_mask(1, 1)[0]
    first1 = colour_mask(1, 2)[0]
    added = (s8 == 1) | (s8 == 6)
    own_rows = slice(0, BY)

    def widen(k, plane, now1, halo1):
        for y in (0, 1):
            tx[pl.ds(k * YE + y, 8, stride=2), :] = plane[0:8]
        wide = tx[pl.ds(pl.multiple_of(k * YE, 8), BY), :]
        hi, lo = plane[8:16], plane[16:24]
        halo = jnp.where(s8 < 2, jnp.where(s8 == 0, hi, rot(hi, 1, 0)), jnp.where(s8 == 7, lo, rot(lo, -1, 0)))
        now = ((before[0, k, own_rows, :], before[0, k, BY:YE, :]), (now1, halo1))
        for colour in (0, 1):
            one, two = now[colour]
            u[colour, k, own_rows, :] = jnp.where(free[colour, k, own_rows, :] > 0.5, one + wide, one)
            u[colour, k, BY:YE, :] = jnp.where(free[colour, k, BY:YE, :] > 0.5, two + halo, two)

    def level1_plane(m, second):
        one, two = (eu[1, m], eu[0, m]) if second else (eu[0, m], eu[1, m])
        return jnp.where(first1, one, two)

    def add(m, _):
        for second in (0, 1):
            k = 2 * m + second + 2
            halo = jnp.where(added, hal[pl.ds(pl.multiple_of(8 * (k - 2), 8), 8), :], before[1, k, BY:YE, :])
            widen(k, level1_plane(m + 1 + H1 // 2, second), before[1, k, own_rows, :], halo)
        return 0

    lax.fori_loop(0, X1 // 2, add, 0)

    def action_x(hi, lo):
        row = (xm0, xm1)[hi][XOWN:XMAIN, :]
        k = X1 + 2
        now = jnp.where(first[own_rows], row, before[1, k, own_rows, :])
        widen(k, level1_plane(1 + H1 // 2 + X1 // 2, 0), now, before[1, k, BY:YE, :])
        row = (xm0, xm1)[lo][XOWN:XMAIN, :]
        now = jnp.where(first[own_rows], before[1, 1, own_rows, :], row)
        widen(1, level1_plane(H1 // 2, 1), now, before[1, 1, BY:YE, :])

    by_parity("gx", action_x)
    for k in (0, NF - 1):
        u[1, k] = before[1, k]
    refs = (c, fin, fout, fyp, fym, fzp, fzm, src, scr, free)
    groups(1, X1 + 2, GF, lambda at: fine_half(u, at, GF, 0, refs))

    def last(at):
        n = 4
        new = fine_new(u, at, n, 1, refs)[:, own_rows]
        even = u[0, pl.ds(at, n), own_rows, :]
        mask = first[own_rows]
        for k in range(n):
            to = pl.multiple_of((at - 2 + k) * 2 * BY, 8)
            result[pl.ds(to, BY), :] = jnp.where(mask, even[k], new[k])
            result[pl.ds(to + BY, BY), :] = jnp.where(mask, new[k], even[k])

    groups(2, X1, 4, last)


def swap(pair, axis):
    count = lax.axis_size(axis)
    got = [None, None]
    for first in (1, 0):
        route = []
        for i in range(first, count - 1, 2):
            route += [(i, i + 1), (i + 1, i)]
        got[first] = lax.ppermute(pair[first], axis, route)
    return tuple(got)


def body(source, permittivity, screening, potential, fixed_cell):
    gx, gy = lax.axis_size("gx"), lax.axis_size("gy")
    args = [a.reshape(BX * BY, NL) for a in (potential, permittivity, source, screening, fixed_cell)]
    args = [pltpu.with_memory_space_constraint(a, pltpu.HBM) for a in args]

    whole = (sds(BX * BY, NL),) * 4 + (jax.ShapeDtypeStruct((BX * BY, NL), jnp.int32),)
    *args, p2, y0, y1, xm0, xm1 = call(
        pack_y,
        whole + (sds(8, NL),) + (sds(YROWS + 8, NL),) * 2 + (sds(12 * BY, NL),) * 2,
        [pltpu.SemaphoreType.DMA((5,)), pltpu.VMEM((BX // 4 * BY, NL), F32), pltpu.VMEM((8, NL), F32)],
        hbm=5,
    )(*args)
    y0 = (y0, y1)
    y0 = swap(y0, "gy")
    xm = swap((xm0, xm1), "gx")
    *halos, x0, x1 = call(pack_x, (sds(BX * 8, NL),) * 5 + (sds(XROWS + 24, NL),) * 2)(p2, *y0)
    gotx = swap((x0, x1), "gx")

    ext, one = (2, NF, YE, NL), (NF, YE, NL)
    fine = call(
        fine_pre,
        (sds(*ext),) * 2 + (sds(*one),) + (sds(*ext),) * 8
        + (sds(X1 // 2, 8, NL), sds(2, X1 // 2, 8, NL)) + (sds(YMSG, NL),) * 2 + (sds(XMAIN, NL),) * 2,
        [
            pltpu.VMEM(ext, F32),
            pltpu.VMEM((X1 * BY, NL), F32),
            pltpu.VMEM((X1 * BY, NL), F32),
            pltpu.VMEM(((X1 + 2) * YE, NL), F32),
            pltpu.VMEM((X1 + 2, 8, NL), F32),
        ],
    )(*args, *halos, *y0, *xm, *gotx)
    state, (c1, g1, m0, m1, *xm1) = fine[:11], fine[11:]
    goty1 = swap((m0, m1), "gy")
    xm1 = swap(xm1, "gx")
    x1msg = call(pack_x1, (sds(XMSG, NL),) * 2)(*goty1, *gotx, *xm1)
    gotx1 = swap(x1msg, "gx")

    mid, mid1 = (2, NM, YE, NL), (NM, YE, NL)
    *level1, message = call(
        mid_pre,
        (sds(*mid),) * 3 + (sds(*mid1),) + (sds(*mid),) * 5 + (sds(gx * gy, 16, NL),),
        [
            pltpu.VMEM(mid, F32),
            pltpu.VMEM((G1 // 2 * YE, NL), F32),
            pltpu.VMEM((X1 // 2 * 8, NL), F32),
            pltpu.VMEM((X1 // 2 * 8, NL), F32),
            pltpu.VMEM((3, G1 // 2, NL), F32),
            pltpu.VMEM((24, NL), F32),
        ],
    )(m0, *goty1, *xm1, *gotx1, c1, g1)

    gathered = lax.all_to_all(message, ("gx", "gy"), 0, 0).reshape(gx, gy, 16, NL)
    wx, wy = min(gx, 6), min(gy, 8)
    if (wx, wy) != (gx, gy):
        first = (*window(gx, gy, wx, wy)[:2], 0, 0)
        gathered = lax.dynamic_slice(gathered, first, (wx, wy, 16, NL))

    inputs = (gathered, p2, *y0, *gotx, *level1, *state, *goty1, *xm1, *gotx1)
    result = pl.pallas_call(
        finish_kernel(len(inputs), (gx, gy, wx, wy)),
        out_shape=sds(BX * BY, NL),
        scratch_shapes=[
            pltpu.VMEM((2, wy + 2, wx * 4, NL), F32),
            pltpu.VMEM((2, wy + 2, wx * 4, NL), F32),
            pltpu.VMEM((2, wy, wx * 4, NL), F32),
            pltpu.VMEM((2, wy, wx * 4, NL), F32),
            pltpu.VMEM((2, 6, wy, wx * 4, NL), F32),
            pltpu.VMEM((wy + 6, wx + 4, 8, NL), F32),
            pltpu.VMEM((NF * YE, NL), F32),
            pltpu.VMEM(mid, F32),
            pltpu.VMEM(ext, F32),
            pltpu.VMEM((BX // 2 * 8, NL), F32),
        ],
        compiler_params=pltpu.CompilerParams(vmem_limit_bytes=24 << 20),
        name="finish",
    )(*inputs)
    return result.reshape(BX, BY, NL)


def window(gx, gy, wx, wy):
    ix, iy = lax.axis_index("gx"), lax.axis_index("gy")
    fx = jnp.clip(ix - 2, 0, gx - wx)
    fy = jnp.clip(iy - 3, 0, gy - wy)
    return fx, fy, ix - fx, iy - fy


def finish_kernel(count, sizes):
    def kernel(*refs):
        ins, result, scratch = list(refs[:count]), refs[count], list(refs[1 + count :])
        finish(window(*sizes)[2:], *ins, result, *scratch)

    return kernel


def solution(mesh):
    placed = (P("gx", "gy", None),) * 5

    return jax.shard_map(body, mesh=mesh, in_specs=placed, out_specs=P("gx", "gy", None), check_vma=False)
```

```python
import jax
import jax.numpy as jnp
from jax import lax
from jax.experimental import pallas as pl
from jax.experimental.pallas import tpu as pltpu
from jax.sharding import PartitionSpec as P

F32 = jnp.float32
BX, BY, NL = 32, 16, 128
YE = 24
X1 = BX // 2
H1 = 8
G1 = X1 + 2 * H1
NF = X1 + 4
NM = G1 // 2 + 2
GF = 3
GM = 8
LN2 = 0.6931471805599453


def rot(value, shift, axis):
    return pltpu.roll(value, shift % value.shape[axis], axis)


def iota(shape, axis):
    return lax.broadcasted_iota(jnp.int32, shape, axis)


def sds(*shape):
    return jax.ShapeDtypeStruct(shape, F32)


def by_parity(axis, action):
    odd = lax.axis_index(axis) % 2

    @pl.when(odd == 0)
    def _():
        action(0, 1)

    @pl.when(odd == 1)
    def _():
        action(1, 0)


def call(kernel, out_shape, scratch=(), vmem=24, hbm=0):
    specs = {"in_specs": [pl.BlockSpec(memory_space=pltpu.HBM)] * hbm} if hbm else {}
    return pl.pallas_call(
        kernel,
        out_shape=out_shape,
        **specs,
        scratch_shapes=list(scratch),
        compiler_params=pltpu.CompilerParams(vmem_limit_bytes=vmem << 20),
    )


YROWS = 10 * BX
XROWS = 12 * 8
FIELDS = (3, 3, 2, 2, 2)


def split_rows(ref, at):
    one, two = ref[pl.ds(at, 4, stride=2), :], ref[pl.ds(at + 1, 4, stride=2), :]
    lane = iota((4, NL), 1)
    even = (lane % 4 + lane // 4) % 2 == 0
    return jnp.concatenate([jnp.where(even, one, two), jnp.where(even, two, one)], axis=0)


def pack_y(hpot, hper, hsrc, hscr, hfix, pot, per, src, scr, fix, p2, out0, out1, xm0, xm1, sems, t, pk):
    outs, mains = (out0, out1), (xm0, xm1)
    pairs = ((hpot, pot), (hper, per), (hsrc, src), (hscr, scr), (hfix, fix))
    copies = [pltpu.make_async_copy(a, b, sems.at[k]) for k, (a, b) in enumerate(pairs)]
    for k in (1, 0, 2, 3, 4):
        copies[k].start()
    copies[1].wait()
    zlane = iota((BX // 2, NL), 1)

    def free_of(value):
        return jnp.where(value == 0, F32(1.0), F32(0.0))

    def row(ref, r):
        return ref[pl.ds(r, BX, stride=BY), :]

    def half(ref, r, parity):
        even = ref[pl.ds(r, BX // 2, stride=2 * BY), :]
        odd = ref[pl.ds(BY + r, BX // 2, stride=2 * BY), :]
        return jnp.where((r + zlane) % 2 == parity, even, odd)

    def side(out, r1, r2, r3):
        rows = [
            row(pot, r1), row(per, r1), row(src, r1), row(scr, r1), free_of(row(fix, r1)),
            row(pot, r2), row(per, r2), free_of(row(fix, r2)),
        ]
        for k, value in enumerate(rows):
            out[BX * k : BX * (k + 1), :] = value
        base = BX * len(rows)
        for k, value in enumerate([half(pot, r3, 1), half(per, r3, 1), half(src, r2, 0), half(scr, r2, 0)]):
            out[base + k * BX // 2 : base + (k + 1) * BX // 2, :] = value

    v = per[...].reshape(BX // 4, 4, BY, NL)
    v = (v[:, 0] + v[:, 1]) + (v[:, 2] + v[:, 3])
    t[...] = lane_pairs(lane_pairs(v, 1), 2).reshape(BX // 4 * BY, NL)
    n2 = BX // 4
    lane = iota((n2, NL), 1)
    total = None
    for j in range(4):
        r = [t[pl.ds(4 * j + k, n2, stride=BY), :] for k in range(4)]
        value = (r[0] + r[1]) + (r[2] + r[3])
        total = value if total is None else jnp.where(lane % 4 == j, value, total)
    pk[...] = F32(1.0 / 64) * total
    p2[...] = split_rows(pk, 0)
    for k in (0, 2, 3, 4):
        copies[k].wait()

    def action(hi, lo):
        side(outs[hi], BY - 1, BY - 2, BY - 3)
        side(outs[lo], 0, 1, 2)
        for out in outs:
            out[YROWS : YROWS + 8, :] = p2[...]

    by_parity("gy", action)

    def slab(out, planes):
        k = 0
        for ref, depth in zip((pot, per, src, scr, fix), FIELDS, strict=True):
            for x in planes[:depth]:
                value = ref[BY * x : BY * (x + 1), :]
                out[BY * k : BY * (k + 1), :] = free_of(value) if ref is fix else value
                k += 1

    def action_x(hi, lo):
        slab(mains[hi], (BX - 1, BX - 2, BX - 3))
        slab(mains[lo], (0, 1, 2))

    by_parity("gx", action_x)


def pack_x(p2, got0, got1, hpot, hper, hsrc, hscr, hfree, out0, out1):
    gots, outs = (got0, got1), (out0, out1)
    halos = (hpot, hper, hsrc, hscr, hfree)
    for h in halos:
        h[...] = jnp.zeros_like(h)

    def place(got, slots):
        def whole(ref, k, slot):
            ref[pl.ds(slot, BX, stride=8), :] = got[BX * k : BX * (k + 1), :]

        def halved(ref, k, slot):
            value = got[BX * 8 + k * BX // 2 : BX * 8 + (k + 1) * BX // 2, :]
            ref[pl.ds(slot, BX // 2, stride=16), :] = value
            ref[pl.ds(8 + slot, BX // 2, stride=16), :] = value

        s1, s2, s3 = slots
        for k, ref in enumerate(halos):
            whole(ref, k, s1)
        whole(hpot, 5, s2)
        whole(hper, 6, s2)
        whole(hfree, 7, s2)
        halved(hpot, 0, s3)
        halved(hper, 1, s3)
        halved(hsrc, 2, s2)
        halved(hscr, 3, s2)

    def action_y(hi, lo):
        place(gots[hi], (0, 1, 2))
        place(gots[lo], (7, 6, 5))

    by_parity("gy", action_y)

    def slab(out, planes):
        k = 0
        for h, depth in zip(halos, FIELDS, strict=True):
            for x in planes[:depth]:
                out[8 * k : 8 * (k + 1), :] = h[8 * x : 8 * (x + 1), :]
                k += 1

    def action_p(hi, lo):
        for out in outs:
            out[XROWS : XROWS + 8, :] = p2[...]
            out[XROWS + 8 : XROWS + 16, :] = gots[hi][YROWS : YROWS + 8, :]
            out[XROWS + 16 : XROWS + 24, :] = gots[lo][YROWS : YROWS + 8, :]

    by_parity("gy", action_p)

    def action_x(hi, lo):
        slab(outs[hi], (BX - 1, BX - 2, BX - 3))
        slab(outs[lo], (0, 1, 2))

    by_parity("gx", action_x)


def nonlinear(u, scr):
    up = jnp.exp(u - F32(LN2))
    down = jnp.exp(-u - F32(LN2))
    return scr * (up - down), scr * (up + down)


def colour_mask(n, zstep):
    shape = (n, YE, NL)
    return (iota(shape, 1) + iota(shape, 2) // zstep) % 2 == 0


def beside_of(other, colour, faces, at, n, zstep):
    fin, fout, fyp, fym, fzp, fzm = faces
    here = pl.ds(at, n)
    v = other[1 - colour, pl.ds(at - 1, n + 2)]
    mid = v[1 : n + 1]
    first = colour_mask(n, zstep)
    across = jnp.where(first, v[:n], v[2:]) if colour == 0 else jnp.where(first, v[2:], v[:n])
    return (
        (fin[here] * mid + fout[colour, here] * across)
        + (fyp[colour, here] * rot(mid, -1, 1) + fym[colour, here] * rot(mid, 1, 1))
        + (fzp[colour, here] * rot(mid, -zstep, 2) + fzm[colour, here] * rot(mid, zstep, 2))
    )


def pairs_of(u, at, n, colour, refs):
    c, fin, fout, fyp, fym, fzp, fzm, src, scr, _ = refs
    here = pl.ds(at, n)
    plane = u[colour, here]
    sh, ch = nonlinear(plane, scr[colour, here])
    centre = c[colour, here]
    beside = beside_of(u, colour, (fin, fout, fyp, fym, fzp, fzm), at, n, 1)
    return plane, centre * plane - beside + sh - src[colour, here], centre, ch


def fine_new(u, at, n, colour, refs):
    plane, value, centre, ch = pairs_of(u, at, n, colour, refs)
    return jnp.where(refs[-1][colour, pl.ds(at, n)] > 0.5, plane - value / (centre + ch), plane)


def fine_half(u, at, n, colour, refs):
    u[colour, pl.ds(at, n)] = fine_new(u, at, n, colour, refs)


def groups(first, count, n, step):
    assert count % n == 0

    def one(g, _):
        step(first + g * n)
        return 0

    lax.fori_loop(0, count // n, one, 0, unroll=True)


def faces_of(p, at, n, scale, zstep, fin, fout, fyp, fym, fzp, fzm):
    here = pl.ds(at, n)
    lane = iota((n, YE, NL), 2)
    first = colour_mask(n, zstep)
    half = F32(0.5 * scale)
    for colour in (0, 1):
        plane = p[colour, here]
        v = p[1 - colour, pl.ds(at - 1, n + 2)]
        mid = v[1 : n + 1]
        across = jnp.where(first, v[:n], v[2:]) if colour == 0 else jnp.where(first, v[2:], v[:n])
        if colour == 0:
            fin[here] = half * (plane + mid)
        fout[colour, here] = half * (plane + across)
        fyp[colour, here] = half * (plane + rot(mid, -1, 1))
        fym[colour, here] = half * (plane + rot(mid, 1, 1))
        fzp[colour, here] = jnp.where(lane >= NL - zstep, F32(0.0), half * (plane + rot(mid, -zstep, 2)))
        fzm[colour, here] = jnp.where(lane < zstep, F32(0.0), half * (plane + rot(mid, zstep, 2)))


def lane_pairs(value, step):
    lane = iota(value.shape, value.ndim - 1)
    return value + jnp.where((lane // step) % 2 == 0, rot(value, -step, value.ndim - 1), rot(value, step, value.ndim - 1))


def fine_pre(pot, per, src, scr, fix, hpot, hper, hsrc, hscr, hfree, goty0, goty1, xm0, xm1, got0, got1,
             u, c, fin, fout, fyp, fym, fzp, fzm, esrc, escr, efree, csum, g1, m0, m1, n0, n1,
             ep, tr, tc, tp, p1):
    gots, mains, outs, nexts = (got0, got1), (xm0, xm1), (m0, m1), (n0, n1)
    first = colour_mask(1, 1)[0]

    def own(k, _):
        for ref, h, ext in ((pot, hpot, u), (per, hper, ep), (src, hsrc, esrc), (scr, hscr, escr), (fix, hfree, efree)):
            value = ref[pl.ds(pl.multiple_of(2 * k * BY, 8), 2 * BY), :]
            if ref is fix:
                value = jnp.where(value == 0, F32(1.0), F32(0.0))
            halo = h[pl.ds(pl.multiple_of(16 * k, 8), 16), :]
            for rows, one, two in (
                (slice(0, BY), value[:BY], value[BY:]),
                (slice(BY, YE), halo[:8], halo[8:]),
            ):
                ext[0, k + 2, rows, :] = jnp.where(first[rows], one, two)
                ext[1, k + 2, rows, :] = jnp.where(first[rows], two, one)
        return 0

    lax.fori_loop(0, X1, own, 0, unroll=4)

    def place(main, got, near, far, flip):
        k = 0
        for ext, depth in zip((u, ep, esrc, escr, efree), FIELDS, strict=True):
            planes = []
            for _ in range(depth):
                rows = main[BY * k : BY * (k + 1), :]
                planes.append(jnp.concatenate([rows, got[8 * k : 8 * (k + 1), :]], axis=0))
                k += 1
            one, two = (planes[1], planes[0]) if flip else (planes[0], planes[1])
            ext[0, near] = jnp.where(first, one, two)
            ext[1, near] = jnp.where(first, two, one)
            third = planes[2] if depth == 3 else jnp.zeros((YE, NL), F32)
            ext[0, far] = third
            ext[1, far] = third

    def action_x(hi, lo):
        place(mains[hi], gots[hi], X1 + 2, X1 + 3, False)
        place(mains[lo], gots[lo], 1, 0, True)

    by_parity("gx", action_x)
    refs = (c, fin, fout, fyp, fym, fzp, fzm, esrc, escr, efree)

    def begin(at):
        n = GF
        faces_of(ep, at, n, 1.0, 1, fin, fout, fyp, fym, fzp, fzm)
        here = pl.ds(at, n)
        lane = iota((n, YE, NL), 2)
        for colour in (0, 1):
            ends = jnp.where((lane == 0) | (lane == NL - 1), F32(0.5) * ep[colour, here], F32(0.0))
            c[colour, here] = (
                (fin[here] + fout[colour, here]) + (fyp[colour, here] + fym[colour, here])
                + (fzp[colour, here] + fzm[colour, here]) + ends
            )
        fine_half(u, at, n, 0, refs)

    groups(1, X1 + 2, GF, begin)
    groups(1, X1 + 2, GF, lambda at: fine_half(u, at, GF, 1, refs))

    def down(at):
        n = 4
        left, react = F32(0.0), F32(0.0)
        for colour in (0, 1):
            _, value, _, ch = pairs_of(u, at, n, colour, refs)
            left += jnp.where(efree[colour, pl.ds(at, n)] > 0.5, -value, F32(0.0))
            react += ch
        to = pl.multiple_of((at - 2) * BY, 8)
        tr[pl.ds(to, n * BY), :] = lane_pairs(left[:, 0:BY], 1).reshape(n * BY, NL)
        tc[pl.ds(to, n * BY), :] = lane_pairs(react[:, 0:BY], 1).reshape(n * BY, NL)

    groups(2, X1, 4, down)

    def coarse_p(k, _):
        at = pl.multiple_of(k * YE, 8)
        tp[pl.ds(at, YE), :] = lane_pairs(ep[0, k + 1] + ep[1, k + 1], 1)
        return 0

    lax.fori_loop(0, X1 + 2, coarse_p, 0, unroll=6)

    eighth = F32(0.125)
    sub = iota((8, NL), 0)
    lane = iota((8, NL), 1)

    def gather_p(k, _):
        p1[k] = eighth * (tp[pl.ds(k * YE, 8, stride=2), :] + tp[pl.ds(k * YE + 1, 8, stride=2), :])
        return 0

    lax.fori_loop(0, X1 + 2, gather_p, 0, unroll=6)

    first8 = (sub + lane // 2) % 2 == 0

    def coarse(x1):
        k = x1 + 1
        p = p1[k]
        base = k * YE
        high = eighth * (tp[pl.ds(base + 2, 8, stride=2), :] + tp[pl.ds(base + 3, 8, stride=2), :])
        edge = tp[pl.ds(pl.multiple_of(base + 16, 8), 8), :]
        edge = eighth * (edge + rot(edge, 1, 0))
        low = jnp.where(sub == 0, rot(edge, 1, 0), rot(p, 1, 0))
        front = jnp.where(lane >= NL - 2, F32(0.0), rot(p, -2, 1))
        back = jnp.where(lane < 2, F32(0.0), rot(p, 2, 1))
        near = (p1[k + 1] + p1[k - 1]) + (high + low) + (front + back)
        centre = F32(3.0) * p + F32(0.5) * near
        at = x1 * BY
        r = eighth * (tr[pl.ds(at, 8, stride=2), :] + tr[pl.ds(at + 1, 8, stride=2), :])
        react = eighth * (tc[pl.ds(at, 8, stride=2), :] + tc[pl.ds(at + 1, 8, stride=2), :])
        diag = F32(0.25) * centre + react
        message = jnp.where(lane % 2 == 0, r, F32(1.0) / diag)
        m0[pl.ds(pl.multiple_of(x1 * 8, 8), 8), :] = message
        m1[pl.ds(pl.multiple_of(x1 * 8, 8), 8), :] = message
        return diag, react

    def make(k, _):
        diag0, react0 = coarse(2 * k)
        diag1, react1 = coarse(2 * k + 1)
        csum[k] = react0 + react1
        g1[0, k] = jnp.where(first8, diag0, diag1)
        g1[1, k] = jnp.where(first8, diag1, diag0)
        return 0

    lax.fori_loop(0, X1 // 2, make, 0, unroll=4)

    for a in range(X1 // 2):
        message = jnp.where(lane % 2 == 0, p1[1 + 2 * a], p1[2 + 2 * a])
        for m in outs:
            m[X1 * 8 + 8 * a : X1 * 8 + 8 * a + 8, :] = message

    base = X1 * 8 + X1 * 4

    def odd_row(out, y):
        out[base : base + X1, :] = u[1, pl.ds(2, X1), y, :]

    def slab(out, at, x):
        out[0 : H1 * 8, :] = m0[8 * at : 8 * (at + H1), :]
        row = X1 * 8 + 4 * at
        out[H1 * 8 : H1 * 12, :] = m0[row : row + H1 * 4, :]
        out[XOWN:XMAIN, :] = u[1, x, 0:BY, :]

    def action_next(hi, lo):
        slab(nexts[hi], X1 - H1, X1 + 1)
        slab(nexts[lo], 0, 2)

    by_parity("gx", action_next)

    def action_y(hi, lo):
        odd_row(outs[hi], BY - 2)
        odd_row(outs[lo], 1)
        outs[hi][base + X1 : base + X1 + 8, :] = (goty0, goty1)[lo][YROWS : YROWS + 8, :]
        outs[lo][base + X1 : base + X1 + 8, :] = (goty0, goty1)[hi][YROWS : YROWS + 8, :]

    by_parity("gy", action_y)


def halo_rows(dx):
    return (16 * (dx - 1), 2) if dx < 5 else (64 + 8 * (dx - 5), 1)


def halo_pair(t):
    return (96 + 16 * t, 2) if t < 2 else (128 + 8 * (t - 2), 1)


P2AT = 144
YMSG = X1 * 8 + X1 * 4 + BX // 2 + 8
XOWN = H1 * 8 + (H1 // 2) * 8
XMAIN = XOWN + BY
XMSG = P2AT + 40


def pack_x1(got0, got1, fx0, fx1, _, __, out0, out1):
    gots, outs, fines = (got0, got1), (out0, out1), (fx0, fx1)
    odd_y = lax.axis_index("gy") % 2
    upper = iota((8, NL), 0) < 4

    def go(hi, lo):
        def put(out, at, count, row):
            above, below = gots[hi][row : row + 8, :], gots[lo][row : row + 8, :]
            if count == 2:
                out[at : at + 8, :] = above
                out[at + 8 : at + 16, :] = below
            else:
                out[at : at + 8, :] = jnp.where(upper, above, below)

        def slab(out, near, step, behind):
            for dx in range(1, H1 + 1):
                put(out, *halo_rows(dx), 8 * (near + step * (dx - 1)))
            for t in range(H1 // 2):
                put(out, *halo_pair(t), X1 * 8 + 8 * (near // 2 + step * t))
            out[P2AT : P2AT + 8, :] = gots[hi][YMSG - 8 : YMSG, :]
            out[P2AT + 8 : P2AT + 16, :] = gots[lo][YMSG - 8 : YMSG, :]
            out[P2AT + 16 : P2AT + 40, :] = behind[XROWS : XROWS + 24, :]

        def action(xhi, xlo):
            slab(outs[xhi], X1 - 1, -1, fines[xlo])
            slab(outs[xlo], 0, 1, fines[xhi])

        by_parity("gx", action)

    @pl.when(odd_y == 0)
    def _():
        go(0, 1)

    @pl.when(odd_y == 1)
    def _():
        go(1, 0)


def coarse_half(e, r, d, at, n, colour, faces, zstep):
    here = pl.ds(at, n)
    e[colour, here] = (r[colour, here] + beside_of(e, colour, faces, at, n, zstep)) * d[colour, here]


def dup_even(value):
    lane = iota(value.shape, value.ndim - 1)
    return jnp.where(lane % 2 == 0, value, rot(value, 1, value.ndim - 1))


def dup_odd(value):
    lane = iota(value.shape, value.ndim - 1)
    return jnp.where(lane % 2 == 1, value, rot(value, -1, value.ndim - 1))


def mid_pre(m0, gy0, gy1, xm0, xm1, gx0, gx1, csum, g1,
            e, r, d, fin, fout, fyp, fym, fzp, fzm, msg,
            p, t, tr, tc, pc, pk):
    gys, gxs, mains = (gy0, gy1), (gx0, gx1), (xm0, xm1)
    odd_y = lax.axis_index("gy") % 2
    first = colour_mask(1, 2)[0]

    def put(k, rows, one, two, both):
        mask = first[rows]
        for colour in (0, 1):
            a, b = (one, two) if colour == 0 else (two, one)
            value = jnp.where(mask, a, b)
            r[colour, k, rows, :] = dup_even(value)
            d[colour, k, rows, :] = dup_odd(value)
        a, b = dup_even(both), dup_odd(both)
        p[0, k, rows, :] = jnp.where(mask, a, b)
        p[1, k, rows, :] = jnp.where(mask, b, a)

    def own(hi, lo):
        def pairs(k, _):
            for j, ref in enumerate((m0, gys[hi], gys[lo])):
                two = ref[pl.ds(pl.multiple_of(16 * k, 8), 16), :]
                both = ref[pl.ds(pl.multiple_of(X1 * 8 + 8 * k, 8), 8), :]
                put(1 + H1 // 2 + k, slice(8 * j, 8 * j + 8), two[:8], two[8:], both)
            return 0

        lax.fori_loop(0, X1 // 2, pairs, 0, unroll=4)

    @pl.when(odd_y == 0)
    def _():
        own(0, 1)

    @pl.when(odd_y == 1)
    def _():
        own(1, 0)

    def beyond(main, ref, at, far):
        def whole(row, start, count):
            own_rows = main[row : row + 8, :]
            above = ref[start : start + 8, :]
            below = ref[start + 8 : start + 16, :] if count == 2 else above
            return jnp.concatenate([own_rows, above, below], axis=0)

        for k in range(H1 // 2):
            one, two = (whole(8 * a, *halo_rows(H1 - a if far else a + 1)) for a in (2 * k, 2 * k + 1))
            both = whole(H1 * 8 + 8 * k, *halo_pair(H1 // 2 - 1 - k if far else k))
            put(at + k, slice(0, YE), one, two, both)

    def action(hi, lo):
        beyond(mains[hi], gxs[hi], 1 + H1 // 2 + X1 // 2, False)
        beyond(mains[lo], gxs[lo], 1, True)

    by_parity("gx", action)
    for ref in (p, e):
        for colour in (0, 1):
            ref[colour, 0] = jnp.zeros((YE, NL), F32)
            ref[colour, NM - 1] = jnp.zeros((YE, NL), F32)
    faces = (fin, fout, fyp, fym, fzp, fzm)

    def begin(at):
        here = pl.ds(at, 2)
        faces_of(p, at, 2, 0.25, 2, *faces)
        e[0, here] = r[0, here] * d[0, here]

    groups(1, NM - 2, 2, begin)
    for colour in (1, 0, 1):
        groups(1, NM - 2, GM, lambda at, colour=colour: coarse_half(e, r, d, at, GM, colour, faces, 2))

    def down(at):
        n = 4
        here = pl.ds(at, n)
        k = pl.ds(at - 1 - H1 // 2, n)
        left = F32(0.0)
        for colour in (0, 1):
            part = r[colour, here] + beside_of(e, colour, faces, at, n, 2)
            left += part[:, 0:8] - g1[colour, k] * e[colour, here, 0:8, :]
        to = pl.multiple_of((at - 1 - H1 // 2) * 8, 8)
        tr[pl.ds(to, n * 8), :] = lane_pairs(left, 2).reshape(n * 8, NL)
        tc[pl.ds(to, n * 8), :] = lane_pairs(csum[k], 2).reshape(n * 8, NL)

    groups(1 + H1 // 2, X1 // 2, 4, down)

    def coarse_p(x2, _):
        t[pl.ds(pl.multiple_of(x2 * YE, 8), YE), :] = lane_pairs(p[0, x2 + 1] + p[1, x2 + 1], 2)
        return 0

    lax.fori_loop(0, G1 // 2, coarse_p, 0, unroll=4)

    eighth = F32(0.125)
    n2, m2 = X1 // 2, G1 // 2

    def compact(ref, first, rows, stride):
        lane = iota((rows, NL), 1)
        out = None
        for j in range(4):
            value = ref[pl.ds(first + 2 * j, rows, stride=stride), :] + ref[pl.ds(first + 2 * j + 1, rows, stride=stride), :]
            out = value if out is None else jnp.where(lane % 4 == j, value, out)
        return eighth * out

    r2 = compact(tr, 0, n2, 8)
    react2 = compact(tc, 0, n2, 8)
    for k in range(3):
        pc[k] = compact(t, 8 * k, m2, YE)
    h2 = H1 // 2
    centre_p = pc[0, h2 : h2 + n2, :]
    j4 = iota((n2, NL), 1) % 4
    lane = iota((n2, NL), 1)
    high = jnp.where(j4 < 3, rot(centre_p, -1, 1), rot(pc[1, h2 : h2 + n2, :], 3, 1))
    low = jnp.where(j4 > 0, rot(centre_p, 1, 1), rot(pc[2, h2 : h2 + n2, :], -3, 1))
    front = jnp.where(lane >= NL - 4, F32(0.0), rot(centre_p, -4, 1))
    back = jnp.where(lane < 4, F32(0.0), rot(centre_p, 4, 1))
    near = (pc[0, h2 + 1 : h2 + 1 + n2, :] + pc[0, h2 - 1 : h2 - 1 + n2, :]) + (high + low) + (front + back)
    diag2 = F32(0.0625) * (F32(3.0) * centre_p + F32(0.5) * near) + react2
    for k, value in enumerate((r2, F32(1.0) / diag2, centre_p)):
        pk[8 * k : 8 * k + 8, :] = value
    r2, inverse2, own_p = (split_rows(pk, 8 * k) for k in range(3))
    near_rows = iota((8, NL), 1) % 4 >= 2
    ahead = jnp.where(near_rows, r2, rot(own_p, -2, 1))
    behind = jnp.where(near_rows, rot(own_p, 2, 1), r2)
    count = lax.axis_size("gy")
    place = lax.axis_index("gy")

    def every(k, _):
        step = k % count - place
        msg[k, 0:8, :] = jnp.where(step == 3, ahead, jnp.where(step == -3, behind, r2))
        msg[k, 8:16, :] = inverse2
        return 0

    lax.fori_loop(0, msg.shape[0], every, 0, unroll=8)


def finish(at, got, p2own, yf0, yf1, xf0, xf1, e, r, d, fin1, fout1, fyp1, fym1, fzp1, fzm1,
           before, c, fin, fout, fyp, fym, fzp, fzm, src, scr, free, gy0, gy1, xm0, xm1, gx0, gx1,
           result,
           e2, p2, r2, d2, k2, blk, tx, eu, u, hal, res, sems):
    wx, wy = got.shape[0], got.shape[1]
    rows = wx * 4
    ox, oy = at
    blk[...] = jnp.zeros_like(blk)
    for b in (0, wy + 1):
        for colour in (0, 1):
            e2[colour, b] = jnp.zeros((rows, NL), F32)

    def keep(da, db, ref, first):
        blk[oy + db + 3, ox + da + 2] = ref[first : first + 8, :]

    keep(0, 0, p2own, 0)

    def blocks_y(hi, lo):
        for db, k in ((1, hi), (-1, lo)):
            keep(0, db, (yf0, yf1)[k], YROWS)
            keep(0, 2 * db, (gy0, gy1)[k], YMSG - 8)

    by_parity("gy", blocks_y)

    def blocks_x(hi, lo):
        for da, k in ((1, hi), (-1, lo)):
            fine, mid = (xf0, xf1)[k], (gx0, gx1)[k]
            for n, db in enumerate((0, 1, -1)):
                keep(da, db, fine, XROWS + 8 * n)
                keep(2 * da, db, mid, P2AT + 16 + 8 * n)
            keep(da, 2, mid, P2AT)
            keep(da, -2, mid, P2AT + 8)

    by_parity("gx", blocks_x)
    l4 = iota((8, NL), 1) % 4
    for db in (3, -3):

        @pl.when((oy + db >= 0) & (oy + db < wy))
        def _(db=db):
            for a in range(wx):
                value = got[a, oy + db, 0:8, :]
                value = jnp.where(l4 < 2, rot(value, -2, 1), F32(0.0)) if db > 0 else jnp.where(l4 >= 2, rot(value, 2, 1), F32(0.0))
                blk[oy + db + 3, a + 2] = value

    def spread(b, _):
        for a in range(wx):
            for colour in (0, 1):
                own, to = slice(4 * colour, 4 * colour + 4), slice(4 * a, 4 * a + 4)
                r2[colour, b, to, :] = got[a, b, own, :]
                d2[colour, b, to, :] = got[a, b, 8 + 4 * colour : 12 + 4 * colour, :]
                p2[colour, b + 1, to, :] = blk[b + 3, a + 2, own, :]
        return 0

    lax.fori_loop(0, wy, spread, 0, unroll=4)
    for b in (0, wy + 1):
        for colour in (0, 1):
            p2[colour, b] = jnp.zeros((rows, NL), F32)
    shape = (wy, rows, NL)
    sub, lane = iota(shape, 1), iota(shape, 2)
    j4 = lane % 4
    even = (j4 + lane // 4) % 2 == 0

    def around(ref, colour):
        v = ref[1 - colour]
        mid = v[1 : wy + 1]
        one, two = rot(mid, 1, 1), rot(mid, -1, 1)
        return (
            mid,
            jnp.where(even, one, two) if colour == 0 else jnp.where(even, two, one),
            jnp.where(j4 < 3, rot(mid, -1, 2), rot(v[2:], 3, 2)),
            jnp.where(j4 > 0, rot(mid, 1, 2), rot(v[:wy], -3, 2)),
            rot(mid, -4, 2), rot(mid, 4, 2),
        )

    for colour in (0, 1):
        at_first = even if colour == 0 else ~even
        outside = (at_first & (sub == 0)) | (~at_first & (sub == rows - 1))
        edges = (None, outside, None, None, lane >= NL - 4, lane < 4)
        mine = p2[colour, 1 : wy + 1]
        for k, (value, edge) in enumerate(zip(around(p2, colour), edges, strict=True)):
            face = F32(0.03125) * (mine + value)
            k2[colour, k] = face if edge is None else jnp.where(edge, F32(0.0), face)
    e2[0, 1 : wy + 1] = r2[0] * d2[0]

    def half2(colour):
        total = r2[colour]
        for k, value in enumerate(around(e2, colour)):
            total = total + k2[colour, k] * value
        e2[colour, 1 : wy + 1] = total * d2[colour]

    half2(1)

    def sweep2(_, carry):
        half2(0)
        half2(1)
        return carry

    lax.fori_loop(0, 3, sweep2, 0, unroll=True)

    s8, l8 = iota((8, NL), 0), iota((8, NL), 1)
    even8 = (l8 % 4 + l8 // 4) % 2 == 0
    start = 4 * ox - 2
    inside = (s8 + start >= 0) & (s8 + start < rows)
    for k, step in enumerate((0, 1, -1)):
        near = []
        for colour in (0, 1):
            block = pltpu.roll(e2[colour, oy + step + 1], (rows - start) % rows, 0)[0:8]
            near.append(jnp.where(inside, block, F32(0.0)))
        planes = (jnp.where(even8, near[0], near[1]), jnp.where(even8, near[1], near[0]))
        for second in (0, 1):
            for j in range(4):
                value = jnp.where(l8 % 4 == 0, rot(planes[second], -j, 1), F32(0.0))
                value = value + rot(value, 1, 1)
                value = value + rot(value, 2, 1)
                for y in (0, 1):
                    tx[pl.ds(second * YE + 8 * k + 2 * j + y, 8, stride=2 * YE), :] = value

    def correct(x2, _):
        value = tx[pl.ds(pl.multiple_of(x2 * YE, 8), YE), :]
        for colour in (0, 1):
            eu[colour, x2 + 1] = e[colour, x2 + 1] + value
        return 0

    lax.fori_loop(0, G1 // 2, correct, 0, unroll=4)
    faces1 = (fin1, fout1, fyp1, fym1, fzp1, fzm1)
    for at1, count, n, colour in ((3, 12, 4, 0), (3, 12, 4, 1), (4, 10, 5, 0), (4, 10, 5, 1)):
        groups(at1, count, n, lambda at, n=n, colour=colour: coarse_half(eu, r, d, at, n, colour, faces1, 2))

    base = X1 * 8 + X1 * 4

    def action_y(hi, lo):
        hal[pl.ds(1, X1, stride=8), :] = (gy0, gy1)[hi][base : base + X1, :]
        hal[pl.ds(6, X1, stride=8), :] = (gy0, gy1)[lo][base : base + X1, :]

    by_parity("gy", action_y)
    first = colour_mask(1, 1)[0]
    first1 = colour_mask(1, 2)[0]
    added = (s8 == 1) | (s8 == 6)
    own_rows = slice(0, BY)

    def widen(k, plane, now1, halo1):
        for y in (0, 1):
            tx[pl.ds(k * YE + y, 8, stride=2), :] = plane[0:8]
        wide = tx[pl.ds(pl.multiple_of(k * YE, 8), BY), :]
        hi, lo = plane[8:16], plane[16:24]
        halo = jnp.where(s8 < 2, jnp.where(s8 == 0, hi, rot(hi, 1, 0)), jnp.where(s8 == 7, lo, rot(lo, -1, 0)))
        now = ((before[0, k, own_rows, :], before[0, k, BY:YE, :]), (now1, halo1))
        for colour in (0, 1):
            one, two = now[colour]
            u[colour, k, own_rows, :] = jnp.where(free[colour, k, own_rows, :] > 0.5, one + wide, one)
            u[colour, k, BY:YE, :] = jnp.where(free[colour, k, BY:YE, :] > 0.5, two + halo, two)

    def level1_plane(m, second):
        one, two = (eu[1, m], eu[0, m]) if second else (eu[0, m], eu[1, m])
        return jnp.where(first1, one, two)

    def add(m, _):
        for second in (0, 1):
            k = 2 * m + second + 2
            halo = jnp.where(added, hal[pl.ds(pl.multiple_of(8 * (k - 2), 8), 8), :], before[1, k, BY:YE, :])
            widen(k, level1_plane(m + 1 + H1 // 2, second), before[1, k, own_rows, :], halo)
        return 0

    lax.fori_loop(0, X1 // 2, add, 0, unroll=4)

    def action_x(hi, lo):
        row = (xm0, xm1)[hi][XOWN:XMAIN, :]
        k = X1 + 2
        now = jnp.where(first[own_rows], row, before[1, k, own_rows, :])
        widen(k, level1_plane(1 + H1 // 2 + X1 // 2, 0), now, before[1, k, BY:YE, :])
        row = (xm0, xm1)[lo][XOWN:XMAIN, :]
        now = jnp.where(first[own_rows], before[1, 1, own_rows, :], row)
        widen(1, level1_plane(H1 // 2, 1), now, before[1, 1, BY:YE, :])

    by_parity("gx", action_x)
    for k in (0, NF - 1):
        u[1, k] = before[1, k]
    refs = (c, fin, fout, fyp, fym, fzp, fzm, src, scr, free)
    groups(1, X1 + 2, GF, lambda at: fine_half(u, at, GF, 0, refs))

    def last(at):
        n = 4
        new = fine_new(u, at, n, 1, refs)[:, own_rows]
        even = u[0, pl.ds(at, n), own_rows, :]
        mask = first[own_rows]
        for k in range(n):
            to = pl.multiple_of((at - 2 + k) * 2 * BY, 8)
            res[pl.ds(to, BY), :] = jnp.where(mask, even[k], new[k])
            res[pl.ds(to + BY, BY), :] = jnp.where(mask, new[k], even[k])

    copies = []
    for g in range(X1 // 4):
        last(2 + 4 * g)
        part = pl.ds(g * 8 * BY, 8 * BY)
        copies.append(pltpu.make_async_copy(res.at[part], result.at[part], sems.at[g]))
        copies[-1].start()
    for copy in copies:
        copy.wait()


def swap(pair, axis):
    count = lax.axis_size(axis)
    got = [None, None]
    for first in (1, 0):
        route = []
        for i in range(first, count - 1, 2):
            route += [(i, i + 1), (i + 1, i)]
        got[first] = lax.ppermute(pair[first], axis, route)
    return tuple(got)


def body(source, permittivity, screening, potential, fixed_cell):
    gx, gy = lax.axis_size("gx"), lax.axis_size("gy")
    args = [a.reshape(BX * BY, NL) for a in (potential, permittivity, source, screening, fixed_cell)]
    args = [pltpu.with_memory_space_constraint(a, pltpu.HBM) for a in args]

    whole = (sds(BX * BY, NL),) * 4 + (jax.ShapeDtypeStruct((BX * BY, NL), jnp.int32),)
    *args, p2, y0, y1, xm0, xm1 = call(
        pack_y,
        whole + (sds(8, NL),) + (sds(YROWS + 8, NL),) * 2 + (sds(12 * BY, NL),) * 2,
        [pltpu.SemaphoreType.DMA((5,)), pltpu.VMEM((BX // 4 * BY, NL), F32), pltpu.VMEM((8, NL), F32)],
        hbm=5,
    )(*args)
    y0 = (y0, y1)
    y0 = swap(y0, "gy")
    xm = swap((xm0, xm1), "gx")
    *halos, x0, x1 = call(pack_x, (sds(BX * 8, NL),) * 5 + (sds(XROWS + 24, NL),) * 2)(p2, *y0)
    gotx = swap((x0, x1), "gx")

    ext, one = (2, NF, YE, NL), (NF, YE, NL)
    fine = call(
        fine_pre,
        (sds(*ext),) * 2 + (sds(*one),) + (sds(*ext),) * 8
        + (sds(X1 // 2, 8, NL), sds(2, X1 // 2, 8, NL)) + (sds(YMSG, NL),) * 2 + (sds(XMAIN, NL),) * 2,
        [
            pltpu.VMEM(ext, F32),
            pltpu.VMEM((X1 * BY, NL), F32),
            pltpu.VMEM((X1 * BY, NL), F32),
            pltpu.VMEM(((X1 + 2) * YE, NL), F32),
            pltpu.VMEM((X1 + 2, 8, NL), F32),
        ],
    )(*args, *halos, *y0, *xm, *gotx)
    state, (c1, g1, m0, m1, *xm1) = fine[:11], fine[11:]
    goty1 = swap((m0, m1), "gy")
    xm1 = swap(xm1, "gx")
    x1msg = call(pack_x1, (sds(XMSG, NL),) * 2)(*goty1, *gotx, *xm1)
    gotx1 = swap(x1msg, "gx")

    mid, mid1 = (2, NM, YE, NL), (NM, YE, NL)
    *level1, message = call(
        mid_pre,
        (sds(*mid),) * 3 + (sds(*mid1),) + (sds(*mid),) * 5 + (sds(gx * gy, 16, NL),),
        [
            pltpu.VMEM(mid, F32),
            pltpu.VMEM((G1 // 2 * YE, NL), F32),
            pltpu.VMEM((X1 // 2 * 8, NL), F32),
            pltpu.VMEM((X1 // 2 * 8, NL), F32),
            pltpu.VMEM((3, G1 // 2, NL), F32),
            pltpu.VMEM((24, NL), F32),
        ],
    )(m0, *goty1, *xm1, *gotx1, c1, g1)

    gathered = lax.all_to_all(message, ("gx", "gy"), 0, 0).reshape(gx, gy, 16, NL)
    wx, wy = min(gx, 6), min(gy, 8)
    if (wx, wy) != (gx, gy):
        first = (*window(gx, gy, wx, wy)[:2], 0, 0)
        gathered = lax.dynamic_slice(gathered, first, (wx, wy, 16, NL))

    inputs = (gathered, p2, *y0, *gotx, *level1, *state, *goty1, *xm1, *gotx1)
    result = pl.pallas_call(
        finish_kernel(len(inputs), (gx, gy, wx, wy)),
        out_shape=sds(BX * BY, NL),
        scratch_shapes=[
            pltpu.VMEM((2, wy + 2, wx * 4, NL), F32),
            pltpu.VMEM((2, wy + 2, wx * 4, NL), F32),
            pltpu.VMEM((2, wy, wx * 4, NL), F32),
            pltpu.VMEM((2, wy, wx * 4, NL), F32),
            pltpu.VMEM((2, 6, wy, wx * 4, NL), F32),
            pltpu.VMEM((wy + 6, wx + 4, 8, NL), F32),
            pltpu.VMEM((NF * YE, NL), F32),
            pltpu.VMEM(mid, F32),
            pltpu.VMEM(ext, F32),
            pltpu.VMEM((BX // 2 * 8, NL), F32),
            pltpu.VMEM((BX * BY, NL), F32),
            pltpu.SemaphoreType.DMA((X1 // 4,)),
        ],
        out_specs=pl.BlockSpec(memory_space=pltpu.HBM),
        compiler_params=pltpu.CompilerParams(vmem_limit_bytes=24 << 20),
        name="finish",
    )(*inputs)
    return result.reshape(BX, BY, NL)


def window(gx, gy, wx, wy):
    ix, iy = lax.axis_index("gx"), lax.axis_index("gy")
    fx = jnp.clip(ix - 2, 0, gx - wx)
    fy = jnp.clip(iy - 3, 0, gy - wy)
    return fx, fy, ix - fx, iy - fy


def finish_kernel(count, sizes):
    def kernel(*refs):
        ins, result, scratch = list(refs[:count]), refs[count], list(refs[1 + count :])
        finish(window(*sizes)[2:], *ins, result, *scratch)

    return kernel


def solution(mesh):
    placed = (P("gx", "gy", None),) * 5

    return jax.shard_map(body, mesh=mesh, in_specs=placed, out_specs=P("gx", "gy", None), check_vma=False)
```

```python
import jax
import jax.numpy as jnp
from jax import lax
from jax.experimental import pallas as pl
from jax.experimental.pallas import tpu as pltpu
from jax.sharding import PartitionSpec as P

F32 = jnp.float32
BX, BY, NL = 32, 16, 128
YE = 24
X1 = BX // 2
H1 = 8
G1 = X1 + 2 * H1
NF = X1 + 4
NM = G1 // 2 + 2
STATE = 16
GF = 3
GM = 8
LN2 = 0.6931471805599453


def rot(value, shift, axis):
    return pltpu.roll(value, shift % value.shape[axis], axis)


def iota(shape, axis):
    return lax.broadcasted_iota(jnp.int32, shape, axis)


def sds(*shape):
    return jax.ShapeDtypeStruct(shape, F32)


def by_parity(axis, action):
    odd = lax.axis_index(axis) % 2

    @pl.when(odd == 0)
    def _():
        action(0, 1)

    @pl.when(odd == 1)
    def _():
        action(1, 0)


def call(kernel, out_shape, scratch=(), vmem=24, hbm=0, alias=None):
    specs = {"in_specs": [pl.BlockSpec(memory_space=pltpu.HBM)] * hbm} if hbm else {}
    return pl.pallas_call(
        kernel,
        out_shape=out_shape,
        **specs,
        input_output_aliases=alias or {},
        scratch_shapes=list(scratch),
        compiler_params=pltpu.CompilerParams(vmem_limit_bytes=vmem << 20),
    )


YROWS = 10 * BX
XROWS = 12 * 8
FIELDS = (3, 3, 2, 2, 2)


def split_rows(ref, at):
    one, two = ref[pl.ds(at, 4, stride=2), :], ref[pl.ds(at + 1, 4, stride=2), :]
    lane = iota((4, NL), 1)
    even = (lane % 4 + lane // 4) % 2 == 0
    return jnp.concatenate([jnp.where(even, one, two), jnp.where(even, two, one)], axis=0)


def pack_y(hpot, hper, hsrc, hscr, hfix, pot, per, src, scr, fix, p2, out0, out1, xm0, xm1, sems, t, pk):
    outs, mains = (out0, out1), (xm0, xm1)
    pairs = ((hpot, pot), (hper, per), (hsrc, src), (hscr, scr), (hfix, fix))
    copies = [pltpu.make_async_copy(a, b, sems.at[k]) for k, (a, b) in enumerate(pairs)]
    for k in (1, 0, 2, 3, 4):
        copies[k].start()
    copies[1].wait()
    zlane = iota((BX // 2, NL), 1)

    def free_of(value):
        return jnp.where(value == 0, F32(1.0), F32(0.0))

    def row(ref, r):
        return ref[pl.ds(r, BX, stride=BY), :]

    def half(ref, r, parity):
        even = ref[pl.ds(r, BX // 2, stride=2 * BY), :]
        odd = ref[pl.ds(BY + r, BX // 2, stride=2 * BY), :]
        return jnp.where((r + zlane) % 2 == parity, even, odd)

    def side(out, r1, r2, r3):
        rows = [
            row(pot, r1), row(per, r1), row(src, r1), row(scr, r1), free_of(row(fix, r1)),
            row(pot, r2), row(per, r2), free_of(row(fix, r2)),
        ]
        for k, value in enumerate(rows):
            out[BX * k : BX * (k + 1), :] = value
        base = BX * len(rows)
        for k, value in enumerate([half(pot, r3, 1), half(per, r3, 1), half(src, r2, 0), half(scr, r2, 0)]):
            out[base + k * BX // 2 : base + (k + 1) * BX // 2, :] = value

    v = per[...].reshape(BX // 4, 4, BY, NL)
    v = (v[:, 0] + v[:, 1]) + (v[:, 2] + v[:, 3])
    t[...] = lane_pairs(lane_pairs(v, 1), 2).reshape(BX // 4 * BY, NL)
    n2 = BX // 4
    lane = iota((n2, NL), 1)
    total = None
    for j in range(4):
        r = [t[pl.ds(4 * j + k, n2, stride=BY), :] for k in range(4)]
        value = (r[0] + r[1]) + (r[2] + r[3])
        total = value if total is None else jnp.where(lane % 4 == j, value, total)
    pk[...] = F32(1.0 / 64) * total
    p2[...] = split_rows(pk, 0)
    for k in (0, 2, 3, 4):
        copies[k].wait()

    def action(hi, lo):
        side(outs[hi], BY - 1, BY - 2, BY - 3)
        side(outs[lo], 0, 1, 2)
        for out in outs:
            out[YROWS : YROWS + 8, :] = p2[...]

    by_parity("gy", action)

    def slab(out, planes):
        k = 0
        for ref, depth in zip((pot, per, src, scr, fix), FIELDS, strict=True):
            for x in planes[:depth]:
                value = ref[BY * x : BY * (x + 1), :]
                out[BY * k : BY * (k + 1), :] = free_of(value) if ref is fix else value
                k += 1

    def action_x(hi, lo):
        slab(mains[hi], (BX - 1, BX - 2, BX - 3))
        slab(mains[lo], (0, 1, 2))

    by_parity("gx", action_x)


def pack_x(p2, got0, got1, hpot, hper, hsrc, hscr, hfree, out0, out1):
    gots, outs = (got0, got1), (out0, out1)
    halos = (hpot, hper, hsrc, hscr, hfree)
    for h in halos:
        h[...] = jnp.zeros_like(h)

    def place(got, slots):
        def whole(ref, k, slot):
            ref[pl.ds(slot, BX, stride=8), :] = got[BX * k : BX * (k + 1), :]

        def halved(ref, k, slot):
            value = got[BX * 8 + k * BX // 2 : BX * 8 + (k + 1) * BX // 2, :]
            ref[pl.ds(slot, BX // 2, stride=16), :] = value
            ref[pl.ds(8 + slot, BX // 2, stride=16), :] = value

        s1, s2, s3 = slots
        for k, ref in enumerate(halos):
            whole(ref, k, s1)
        whole(hpot, 5, s2)
        whole(hper, 6, s2)
        whole(hfree, 7, s2)
        halved(hpot, 0, s3)
        halved(hper, 1, s3)
        halved(hsrc, 2, s2)
        halved(hscr, 3, s2)

    def action_y(hi, lo):
        place(gots[hi], (0, 1, 2))
        place(gots[lo], (7, 6, 5))

    by_parity("gy", action_y)

    def slab(out, planes):
        k = 0
        for h, depth in zip(halos, FIELDS, strict=True):
            for x in planes[:depth]:
                out[8 * k : 8 * (k + 1), :] = h[8 * x : 8 * (x + 1), :]
                k += 1

    def action_p(hi, lo):
        for out in outs:
            out[XROWS : XROWS + 8, :] = p2[...]
            out[XROWS + 8 : XROWS + 16, :] = gots[hi][YROWS : YROWS + 8, :]
            out[XROWS + 16 : XROWS + 24, :] = gots[lo][YROWS : YROWS + 8, :]

    by_parity("gy", action_p)

    def action_x(hi, lo):
        slab(outs[hi], (BX - 1, BX - 2, BX - 3))
        slab(outs[lo], (0, 1, 2))

    by_parity("gx", action_x)


def nonlinear(u, scr):
    up = jnp.exp(u - F32(LN2))
    down = jnp.exp(-u - F32(LN2))
    return scr * (up - down), scr * (up + down)


def colour_mask(n, zstep):
    shape = (n, YE, NL)
    return (iota(shape, 1) + iota(shape, 2) // zstep) % 2 == 0


def beside_of(other, colour, faces, at, n, zstep):
    fin, fout, fyp, fym, fzp, fzm = faces
    here = pl.ds(at, n)
    v = other[1 - colour, pl.ds(at - 1, n + 2)]
    mid = v[1 : n + 1]
    first = colour_mask(n, zstep)
    across = jnp.where(first, v[:n], v[2:]) if colour == 0 else jnp.where(first, v[2:], v[:n])
    return (
        (fin[here] * mid + fout[colour, here] * across)
        + (fyp[colour, here] * rot(mid, -1, 1) + fym[colour, here] * rot(mid, 1, 1))
        + (fzp[colour, here] * rot(mid, -zstep, 2) + fzm[colour, here] * rot(mid, zstep, 2))
    )


def pairs_of(u, at, n, colour, refs):
    c, fin, fout, fyp, fym, fzp, fzm, src, scr, _ = refs
    here = pl.ds(at, n)
    plane = u[colour, here]
    sh, ch = nonlinear(plane, scr[colour, here])
    centre = c[colour, here]
    beside = beside_of(u, colour, (fin, fout, fyp, fym, fzp, fzm), at, n, 1)
    return plane, centre * plane - beside + sh - src[colour, here], centre, ch


def fine_new(u, at, n, colour, refs):
    plane, value, centre, ch = pairs_of(u, at, n, colour, refs)
    return jnp.where(refs[-1][colour, pl.ds(at, n)] > 0.5, plane - value / (centre + ch), plane)


def fine_half(u, at, n, colour, refs):
    u[colour, pl.ds(at, n)] = fine_new(u, at, n, colour, refs)


def groups(first, count, n, step):
    assert count % n == 0

    def one(g, _):
        step(first + g * n)
        return 0

    lax.fori_loop(0, count // n, one, 0, unroll=True)


def faces_of(p, at, n, scale, zstep, fin, fout, fyp, fym, fzp, fzm):
    here = pl.ds(at, n)
    lane = iota((n, YE, NL), 2)
    first = colour_mask(n, zstep)
    half = F32(0.5 * scale)
    for colour in (0, 1):
        plane = p[colour, here]
        v = p[1 - colour, pl.ds(at - 1, n + 2)]
        mid = v[1 : n + 1]
        across = jnp.where(first, v[:n], v[2:]) if colour == 0 else jnp.where(first, v[2:], v[:n])
        if colour == 0:
            fin[here] = half * (plane + mid)
        fout[colour, here] = half * (plane + across)
        fyp[colour, here] = half * (plane + rot(mid, -1, 1))
        fym[colour, here] = half * (plane + rot(mid, 1, 1))
        fzp[colour, here] = jnp.where(lane >= NL - zstep, F32(0.0), half * (plane + rot(mid, -zstep, 2)))
        fzm[colour, here] = jnp.where(lane < zstep, F32(0.0), half * (plane + rot(mid, zstep, 2)))


def lane_pairs(value, step):
    lane = iota(value.shape, value.ndim - 1)
    return value + jnp.where((lane // step) % 2 == 0, rot(value, -step, value.ndim - 1), rot(value, step, value.ndim - 1))


def fine_begin(state, at, n):
    u, ep, c, fin, fout, fyp, fym, fzp, fzm, esrc, escr, efree = state[:12]
    faces_of(ep, at, n, 1.0, 1, fin, fout, fyp, fym, fzp, fzm)
    here = pl.ds(at, n)
    lane = iota((n, YE, NL), 2)
    for colour in (0, 1):
        ends = jnp.where((lane == 0) | (lane == NL - 1), F32(0.5) * ep[colour, here], F32(0.0))
        c[colour, here] = (
            (fin[here] + fout[colour, here]) + (fyp[colour, here] + fym[colour, here])
            + (fzp[colour, here] + fzm[colour, here]) + ends
        )
    fine_half(u, at, n, 0, (c, fin, fout, fyp, fym, fzp, fzm, esrc, escr, efree))


def fine_own(pot, per, src, scr, fix, hpot, hper, hsrc, hscr, hfree, *state):
    u, ep, c, fin, fout, fyp, fym, fzp, fzm, esrc, escr, efree = state[:12]
    first = colour_mask(1, 1)[0]

    def own(k, _):
        for ref, h, ext in ((pot, hpot, u), (per, hper, ep), (src, hsrc, esrc), (scr, hscr, escr), (fix, hfree, efree)):
            value = ref[pl.ds(pl.multiple_of(2 * k * BY, 8), 2 * BY), :]
            if ref is fix:
                value = jnp.where(value == 0, F32(1.0), F32(0.0))
            halo = h[pl.ds(pl.multiple_of(16 * k, 8), 16), :]
            for rows, one, two in (
                (slice(0, BY), value[:BY], value[BY:]),
                (slice(BY, YE), halo[:8], halo[8:]),
            ):
                ext[0, k + 2, rows, :] = jnp.where(first[rows], one, two)
                ext[1, k + 2, rows, :] = jnp.where(first[rows], two, one)
        return 0

    lax.fori_loop(0, X1, own, 0, unroll=4)
    groups(3, X1 - 2, 2, lambda at: fine_begin(state, at, 2))
    refs = (c, fin, fout, fyp, fym, fzp, fzm, esrc, escr, efree)
    groups(4, X1 - 4, 3, lambda at: fine_half(u, at, 3, 1, refs))
    groups(6, X1 - 8, 4, lambda at: fine_down(state, at, 4))
    for k in range(1, X1 + 1):
        fine_coarse_p(state, k)


def fine_down(state, at, n):
    u, _, c, fin, fout, fyp, fym, fzp, fzm, esrc, escr, efree, tr, tc = state[:14]
    refs = (c, fin, fout, fyp, fym, fzp, fzm, esrc, escr, efree)
    left, react = F32(0.0), F32(0.0)
    for colour in (0, 1):
        _, value, _, ch = pairs_of(u, at, n, colour, refs)
        left += jnp.where(efree[colour, pl.ds(at, n)] > 0.5, -value, F32(0.0))
        react += ch
    to = pl.multiple_of((at - 2) * BY, 8)
    tr[pl.ds(to, n * BY), :] = lane_pairs(left[:, 0:BY], 1).reshape(n * BY, NL)
    tc[pl.ds(to, n * BY), :] = lane_pairs(react[:, 0:BY], 1).reshape(n * BY, NL)


def fine_coarse_p(state, k):
    ep, tp, p1 = state[1], state[14], state[15]
    at = k * YE
    tp[at : at + YE, :] = lane_pairs(ep[0, k + 1] + ep[1, k + 1], 1)
    p1[k] = F32(0.125) * (tp[pl.ds(at, 8, stride=2), :] + tp[pl.ds(at + 1, 8, stride=2), :])


def fine_pre(goty0, goty1, xm0, xm1, got0, got1, *refs_):
    state, refs_ = refs_[STATE : 2 * STATE], refs_[2 * STATE :]
    u, ep, c, fin, fout, fyp, fym, fzp, fzm, esrc, escr, efree, tr, tc, tp, p1 = state
    csum, g1, m0, m1, n0, n1 = refs_
    gots, mains, outs, nexts = (got0, got1), (xm0, xm1), (m0, m1), (n0, n1)
    first = colour_mask(1, 1)[0]

    def place(main, got, near, far, flip):
        k = 0
        for ext, depth in zip((u, ep, esrc, escr, efree), FIELDS, strict=True):
            planes = []
            for _ in range(depth):
                rows = main[BY * k : BY * (k + 1), :]
                planes.append(jnp.concatenate([rows, got[8 * k : 8 * (k + 1), :]], axis=0))
                k += 1
            one, two = (planes[1], planes[0]) if flip else (planes[0], planes[1])
            ext[0, near] = jnp.where(first, one, two)
            ext[1, near] = jnp.where(first, two, one)
            third = planes[2] if depth == 3 else jnp.zeros((YE, NL), F32)
            ext[0, far] = third
            ext[1, far] = third

    def action_x(hi, lo):
        place(mains[hi], gots[hi], X1 + 2, X1 + 3, False)
        place(mains[lo], gots[lo], 1, 0, True)

    by_parity("gx", action_x)
    refs = (c, fin, fout, fyp, fym, fzp, fzm, esrc, escr, efree)

    for at in (1, X1 + 1):
        fine_begin(state, at, 2)
    for at in (1, X1):
        fine_half(u, at, 3, 1, refs)
    for at in (2, X1 - 2):
        fine_down(state, at, 4)
    for k in (0, X1 + 1):
        fine_coarse_p(state, k)

    eighth = F32(0.125)
    sub = iota((8, NL), 0)
    lane = iota((8, NL), 1)

    first8 = (sub + lane // 2) % 2 == 0

    def coarse(x1):
        k = x1 + 1
        p = p1[k]
        base = k * YE
        high = eighth * (tp[pl.ds(base + 2, 8, stride=2), :] + tp[pl.ds(base + 3, 8, stride=2), :])
        edge = tp[pl.ds(pl.multiple_of(base + 16, 8), 8), :]
        edge = eighth * (edge + rot(edge, 1, 0))
        low = jnp.where(sub == 0, rot(edge, 1, 0), rot(p, 1, 0))
        front = jnp.where(lane >= NL - 2, F32(0.0), rot(p, -2, 1))
        back = jnp.where(lane < 2, F32(0.0), rot(p, 2, 1))
        near = (p1[k + 1] + p1[k - 1]) + (high + low) + (front + back)
        centre = F32(3.0) * p + F32(0.5) * near
        at = x1 * BY
        r = eighth * (tr[pl.ds(at, 8, stride=2), :] + tr[pl.ds(at + 1, 8, stride=2), :])
        react = eighth * (tc[pl.ds(at, 8, stride=2), :] + tc[pl.ds(at + 1, 8, stride=2), :])
        diag = F32(0.25) * centre + react
        message = jnp.where(lane % 2 == 0, r, F32(1.0) / diag)
        m0[pl.ds(pl.multiple_of(x1 * 8, 8), 8), :] = message
        m1[pl.ds(pl.multiple_of(x1 * 8, 8), 8), :] = message
        return diag, react

    def make(k, _):
        diag0, react0 = coarse(2 * k)
        diag1, react1 = coarse(2 * k + 1)
        csum[k] = react0 + react1
        g1[0, k] = jnp.where(first8, diag0, diag1)
        g1[1, k] = jnp.where(first8, diag1, diag0)
        return 0

    lax.fori_loop(0, X1 // 2, make, 0, unroll=4)

    for a in range(X1 // 2):
        message = jnp.where(lane % 2 == 0, p1[1 + 2 * a], p1[2 + 2 * a])
        for m in outs:
            m[X1 * 8 + 8 * a : X1 * 8 + 8 * a + 8, :] = message

    base = X1 * 8 + X1 * 4

    def odd_row(out, y):
        out[base : base + X1, :] = u[1, pl.ds(2, X1), y, :]

    def slab(out, at, x):
        out[0 : H1 * 8, :] = m0[8 * at : 8 * (at + H1), :]
        row = X1 * 8 + 4 * at
        out[H1 * 8 : H1 * 12, :] = m0[row : row + H1 * 4, :]
        out[XOWN:XMAIN, :] = u[1, x, 0:BY, :]

    def action_next(hi, lo):
        slab(nexts[hi], X1 - H1, X1 + 1)
        slab(nexts[lo], 0, 2)

    by_parity("gx", action_next)

    def action_y(hi, lo):
        odd_row(outs[hi], BY - 2)
        odd_row(outs[lo], 1)
        outs[hi][base + X1 : base + X1 + 8, :] = (goty0, goty1)[lo][YROWS : YROWS + 8, :]
        outs[lo][base + X1 : base + X1 + 8, :] = (goty0, goty1)[hi][YROWS : YROWS + 8, :]

    by_parity("gy", action_y)


def halo_rows(dx):
    return (16 * (dx - 1), 2) if dx < 5 else (64 + 8 * (dx - 5), 1)


def halo_pair(t):
    return (96 + 16 * t, 2) if t < 2 else (128 + 8 * (t - 2), 1)


P2AT = 144
YMSG = X1 * 8 + X1 * 4 + BX // 2 + 8
XOWN = H1 * 8 + (H1 // 2) * 8
XMAIN = XOWN + BY
XMSG = P2AT + 40


def pack_x1(got0, got1, fx0, fx1, out0, out1):
    gots, outs, fines = (got0, got1), (out0, out1), (fx0, fx1)
    odd_y = lax.axis_index("gy") % 2
    upper = iota((8, NL), 0) < 4

    def go(hi, lo):
        def put(out, at, count, row):
            above, below = gots[hi][row : row + 8, :], gots[lo][row : row + 8, :]
            if count == 2:
                out[at : at + 8, :] = above
                out[at + 8 : at + 16, :] = below
            else:
                out[at : at + 8, :] = jnp.where(upper, above, below)

        def slab(out, near, step, behind):
            for dx in range(1, H1 + 1):
                put(out, *halo_rows(dx), 8 * (near + step * (dx - 1)))
            for t in range(H1 // 2):
                put(out, *halo_pair(t), X1 * 8 + 8 * (near // 2 + step * t))
            out[P2AT : P2AT + 8, :] = gots[hi][YMSG - 8 : YMSG, :]
            out[P2AT + 8 : P2AT + 16, :] = gots[lo][YMSG - 8 : YMSG, :]
            out[P2AT + 16 : P2AT + 40, :] = behind[XROWS : XROWS + 24, :]

        def action(xhi, xlo):
            slab(outs[xhi], X1 - 1, -1, fines[xlo])
            slab(outs[xlo], 0, 1, fines[xhi])

        by_parity("gx", action)

    @pl.when(odd_y == 0)
    def _():
        go(0, 1)

    @pl.when(odd_y == 1)
    def _():
        go(1, 0)


def coarse_half(e, r, d, at, n, colour, faces, zstep):
    here = pl.ds(at, n)
    e[colour, here] = (r[colour, here] + beside_of(e, colour, faces, at, n, zstep)) * d[colour, here]


def dup_even(value):
    lane = iota(value.shape, value.ndim - 1)
    return jnp.where(lane % 2 == 0, value, rot(value, 1, value.ndim - 1))


def dup_odd(value):
    lane = iota(value.shape, value.ndim - 1)
    return jnp.where(lane % 2 == 1, value, rot(value, -1, value.ndim - 1))


MIDS = 10


def mid_put(state, k, rows, one, two, both):
    _, r, d, p = state[:4]
    mask = colour_mask(1, 2)[0][rows]
    for colour in (0, 1):
        a, b = (one, two) if colour == 0 else (two, one)
        value = jnp.where(mask, a, b)
        r[colour, k, rows, :] = dup_even(value)
        d[colour, k, rows, :] = dup_odd(value)
    a, b = dup_even(both), dup_odd(both)
    p[0, k, rows, :] = jnp.where(mask, a, b)
    p[1, k, rows, :] = jnp.where(mask, b, a)


def mid_begin(state, at, n):
    e, r, d, p, *faces = state
    here = pl.ds(at, n)
    faces_of(p, at, n, 0.25, 2, *faces)
    e[0, here] = r[0, here] * d[0, here]


def mid_own(m0, gy0, gy1, *state):
    gys = (gy0, gy1)
    e, r, d, p, *faces = state

    def own(hi, lo):
        for k in range(X1 // 2):
            for j, ref in enumerate((m0, gys[hi], gys[lo])):
                two = ref[16 * k : 16 * k + 16, :]
                both = ref[X1 * 8 + 8 * k : X1 * 8 + 8 * k + 8, :]
                mid_put(state, 1 + H1 // 2 + k, slice(8 * j, 8 * j + 8), two[:8], two[8:], both)

    by_parity("gy", own)
    first = 2 + H1 // 2
    groups(first, X1 // 2 - 2, 2, lambda at: mid_begin(state, at, 2))
    groups(first + 1, X1 // 2 - 4, 2, lambda at: coarse_half(e, r, d, at, 2, 1, faces, 2))


def mid_pre(xm0, xm1, gx0, gx1, csum, g1, *refs_):
    gxs, mains = (gx0, gx1), (xm0, xm1)
    state, refs_ = refs_[MIDS : 2 * MIDS], refs_[2 * MIDS :]
    e, r, d, p, *faces = state
    fin, fout, fyp, fym, fzp, fzm = faces
    msg, t, tr, tc, pc, pk = refs_

    def beyond(main, ref, at, far):
        def whole(row, start, count):
            own_rows = main[row : row + 8, :]
            above = ref[start : start + 8, :]
            below = ref[start + 8 : start + 16, :] if count == 2 else above
            return jnp.concatenate([own_rows, above, below], axis=0)

        for k in range(H1 // 2):
            one, two = (whole(8 * a, *halo_rows(H1 - a if far else a + 1)) for a in (2 * k, 2 * k + 1))
            both = whole(H1 * 8 + 8 * k, *halo_pair(H1 // 2 - 1 - k if far else k))
            mid_put(state, at + k, slice(0, YE), one, two, both)

    def action(hi, lo):
        beyond(mains[hi], gxs[hi], 1 + H1 // 2 + X1 // 2, False)
        beyond(mains[lo], gxs[lo], 1, True)

    by_parity("gx", action)
    for ref in (p, e):
        for colour in (0, 1):
            ref[colour, 0] = jnp.zeros((YE, NL), F32)
            ref[colour, NM - 1] = jnp.zeros((YE, NL), F32)
    inner = 1 + H1 // 2
    for at in (*range(1, inner + 1), *range(inner + X1 // 2 - 1, NM - 1)):
        mid_begin(state, at, 1)
    for at in (1, inner + X1 // 2 - 2):
        coarse_half(e, r, d, at, inner + 1, 1, faces, 2)
    for colour in (0, 1):
        groups(1, NM - 2, GM, lambda at, colour=colour: coarse_half(e, r, d, at, GM, colour, faces, 2))

    def down(at):
        n = 4
        here = pl.ds(at, n)
        k = pl.ds(at - 1 - H1 // 2, n)
        left = F32(0.0)
        for colour in (0, 1):
            part = r[colour, here] + beside_of(e, colour, faces, at, n, 2)
            left += part[:, 0:8] - g1[colour, k] * e[colour, here, 0:8, :]
        to = pl.multiple_of((at - 1 - H1 // 2) * 8, 8)
        tr[pl.ds(to, n * 8), :] = lane_pairs(left, 2).reshape(n * 8, NL)
        tc[pl.ds(to, n * 8), :] = lane_pairs(csum[k], 2).reshape(n * 8, NL)

    groups(1 + H1 // 2, X1 // 2, 4, down)

    def coarse_p(x2, _):
        t[pl.ds(pl.multiple_of(x2 * YE, 8), YE), :] = lane_pairs(p[0, x2 + 1] + p[1, x2 + 1], 2)
        return 0

    lax.fori_loop(0, G1 // 2, coarse_p, 0, unroll=4)

    eighth = F32(0.125)
    n2, m2 = X1 // 2, G1 // 2

    def compact(ref, first, rows, stride):
        lane = iota((rows, NL), 1)
        out = None
        for j in range(4):
            value = ref[pl.ds(first + 2 * j, rows, stride=stride), :] + ref[pl.ds(first + 2 * j + 1, rows, stride=stride), :]
            out = value if out is None else jnp.where(lane % 4 == j, value, out)
        return eighth * out

    r2 = compact(tr, 0, n2, 8)
    react2 = compact(tc, 0, n2, 8)
    for k in range(3):
        pc[k] = compact(t, 8 * k, m2, YE)
    h2 = H1 // 2
    centre_p = pc[0, h2 : h2 + n2, :]
    j4 = iota((n2, NL), 1) % 4
    lane = iota((n2, NL), 1)
    high = jnp.where(j4 < 3, rot(centre_p, -1, 1), rot(pc[1, h2 : h2 + n2, :], 3, 1))
    low = jnp.where(j4 > 0, rot(centre_p, 1, 1), rot(pc[2, h2 : h2 + n2, :], -3, 1))
    front = jnp.where(lane >= NL - 4, F32(0.0), rot(centre_p, -4, 1))
    back = jnp.where(lane < 4, F32(0.0), rot(centre_p, 4, 1))
    near = (pc[0, h2 + 1 : h2 + 1 + n2, :] + pc[0, h2 - 1 : h2 - 1 + n2, :]) + (high + low) + (front + back)
    diag2 = F32(0.0625) * (F32(3.0) * centre_p + F32(0.5) * near) + react2
    for k, value in enumerate((r2, F32(1.0) / diag2, centre_p)):
        pk[8 * k : 8 * k + 8, :] = value
    r2, inverse2, own_p = (split_rows(pk, 8 * k) for k in range(3))
    near_rows = iota((8, NL), 1) % 4 >= 2
    ahead = jnp.where(near_rows, r2, rot(own_p, -2, 1))
    behind = jnp.where(near_rows, rot(own_p, 2, 1), r2)
    count = lax.axis_size("gy")
    place = lax.axis_index("gy")

    def every(k, _):
        step = k % count - place
        msg[k, 0:8, :] = jnp.where(step == 3, ahead, jnp.where(step == -3, behind, r2))
        msg[k, 8:16, :] = inverse2
        return 0

    lax.fori_loop(0, msg.shape[0], every, 0, unroll=8)


def finish(at, got, p2own, yf0, yf1, xf0, xf1, e, r, d, fin1, fout1, fyp1, fym1, fzp1, fzm1,
           before, c, fin, fout, fyp, fym, fzp, fzm, src, scr, free, gy0, gy1, xm0, xm1, gx0, gx1,
           result,
           e2, p2, r2, d2, k2, blk, tx, eu, u, hal, res, sems):
    wx, wy = got.shape[0], got.shape[1]
    rows = wx * 4
    ox, oy = at
    blk[...] = jnp.zeros_like(blk)
    for b in (0, wy + 1):
        for colour in (0, 1):
            e2[colour, b] = jnp.zeros((rows, NL), F32)

    def keep(da, db, ref, first):
        blk[oy + db + 3, ox + da + 2] = ref[first : first + 8, :]

    keep(0, 0, p2own, 0)

    def blocks_y(hi, lo):
        for db, k in ((1, hi), (-1, lo)):
            keep(0, db, (yf0, yf1)[k], YROWS)
            keep(0, 2 * db, (gy0, gy1)[k], YMSG - 8)

    by_parity("gy", blocks_y)

    def blocks_x(hi, lo):
        for da, k in ((1, hi), (-1, lo)):
            fine, mid = (xf0, xf1)[k], (gx0, gx1)[k]
            for n, db in enumerate((0, 1, -1)):
                keep(da, db, fine, XROWS + 8 * n)
                keep(2 * da, db, mid, P2AT + 16 + 8 * n)
            keep(da, 2, mid, P2AT)
            keep(da, -2, mid, P2AT + 8)

    by_parity("gx", blocks_x)
    l4 = iota((8, NL), 1) % 4
    for db in (3, -3):

        @pl.when((oy + db >= 0) & (oy + db < wy))
        def _(db=db):
            for a in range(wx):
                value = got[a, oy + db, 0:8, :]
                value = jnp.where(l4 < 2, rot(value, -2, 1), F32(0.0)) if db > 0 else jnp.where(l4 >= 2, rot(value, 2, 1), F32(0.0))
                blk[oy + db + 3, a + 2] = value

    def spread(b, _):
        for a in range(wx):
            for colour in (0, 1):
                own, to = slice(4 * colour, 4 * colour + 4), slice(4 * a, 4 * a + 4)
                r2[colour, b, to, :] = got[a, b, own, :]
                d2[colour, b, to, :] = got[a, b, 8 + 4 * colour : 12 + 4 * colour, :]
                p2[colour, b + 1, to, :] = blk[b + 3, a + 2, own, :]
        return 0

    lax.fori_loop(0, wy, spread, 0, unroll=4)
    for b in (0, wy + 1):
        for colour in (0, 1):
            p2[colour, b] = jnp.zeros((rows, NL), F32)
    shape = (wy, rows, NL)
    sub, lane = iota(shape, 1), iota(shape, 2)
    j4 = lane % 4
    even = (j4 + lane // 4) % 2 == 0

    def around(ref, colour):
        v = ref[1 - colour]
        mid = v[1 : wy + 1]
        one, two = rot(mid, 1, 1), rot(mid, -1, 1)
        return (
            mid,
            jnp.where(even, one, two) if colour == 0 else jnp.where(even, two, one),
            jnp.where(j4 < 3, rot(mid, -1, 2), rot(v[2:], 3, 2)),
            jnp.where(j4 > 0, rot(mid, 1, 2), rot(v[:wy], -3, 2)),
            rot(mid, -4, 2), rot(mid, 4, 2),
        )

    for colour in (0, 1):
        at_first = even if colour == 0 else ~even
        outside = (at_first & (sub == 0)) | (~at_first & (sub == rows - 1))
        edges = (None, outside, None, None, lane >= NL - 4, lane < 4)
        mine = p2[colour, 1 : wy + 1]
        for k, (value, edge) in enumerate(zip(around(p2, colour), edges, strict=True)):
            face = F32(0.03125) * (mine + value)
            k2[colour, k] = face if edge is None else jnp.where(edge, F32(0.0), face)
    e2[0, 1 : wy + 1] = r2[0] * d2[0]

    def half2(colour):
        total = r2[colour]
        for k, value in enumerate(around(e2, colour)):
            total = total + k2[colour, k] * value
        e2[colour, 1 : wy + 1] = total * d2[colour]

    half2(1)

    def sweep2(_, carry):
        half2(0)
        half2(1)
        return carry

    lax.fori_loop(0, 3, sweep2, 0, unroll=True)

    s8, l8 = iota((8, NL), 0), iota((8, NL), 1)
    even8 = (l8 % 4 + l8 // 4) % 2 == 0
    start = 4 * ox - 2
    inside = (s8 + start >= 0) & (s8 + start < rows)
    for k, step in enumerate((0, 1, -1)):
        near = []
        for colour in (0, 1):
            block = pltpu.roll(e2[colour, oy + step + 1], (rows - start) % rows, 0)[0:8]
            near.append(jnp.where(inside, block, F32(0.0)))
        planes = (jnp.where(even8, near[0], near[1]), jnp.where(even8, near[1], near[0]))
        for second in (0, 1):
            for j in range(4):
                value = jnp.where(l8 % 4 == 0, rot(planes[second], -j, 1), F32(0.0))
                value = value + rot(value, 1, 1)
                value = value + rot(value, 2, 1)
                for y in (0, 1):
                    tx[pl.ds(second * YE + 8 * k + 2 * j + y, 8, stride=2 * YE), :] = value

    def correct(x2, _):
        value = tx[pl.ds(pl.multiple_of(x2 * YE, 8), YE), :]
        for colour in (0, 1):
            eu[colour, x2 + 1] = e[colour, x2 + 1] + value
        return 0

    lax.fori_loop(0, G1 // 2, correct, 0, unroll=4)
    faces1 = (fin1, fout1, fyp1, fym1, fzp1, fzm1)
    for at1, count, n, colour in ((3, 12, 4, 0), (3, 12, 4, 1), (4, 10, 5, 0), (4, 10, 5, 1)):
        groups(at1, count, n, lambda at, n=n, colour=colour: coarse_half(eu, r, d, at, n, colour, faces1, 2))

    base = X1 * 8 + X1 * 4

    def action_y(hi, lo):
        hal[pl.ds(1, X1, stride=8), :] = (gy0, gy1)[hi][base : base + X1, :]
        hal[pl.ds(6, X1, stride=8), :] = (gy0, gy1)[lo][base : base + X1, :]

    by_parity("gy", action_y)
    first = colour_mask(1, 1)[0]
    first1 = colour_mask(1, 2)[0]
    added = (s8 == 1) | (s8 == 6)
    own_rows = slice(0, BY)

    def widen(k, plane, now1, halo1):
        for y in (0, 1):
            tx[pl.ds(k * YE + y, 8, stride=2), :] = plane[0:8]
        wide = tx[pl.ds(pl.multiple_of(k * YE, 8), BY), :]
        hi, lo = plane[8:16], plane[16:24]
        halo = jnp.where(s8 < 2, jnp.where(s8 == 0, hi, rot(hi, 1, 0)), jnp.where(s8 == 7, lo, rot(lo, -1, 0)))
        now = ((before[0, k, own_rows, :], before[0, k, BY:YE, :]), (now1, halo1))
        for colour in (0, 1):
            one, two = now[colour]
            u[colour, k, own_rows, :] = jnp.where(free[colour, k, own_rows, :] > 0.5, one + wide, one)
            u[colour, k, BY:YE, :] = jnp.where(free[colour, k, BY:YE, :] > 0.5, two + halo, two)

    def level1_plane(m, second):
        one, two = (eu[1, m], eu[0, m]) if second else (eu[0, m], eu[1, m])
        return jnp.where(first1, one, two)

    def add(m, _):
        for second in (0, 1):
            k = 2 * m + second + 2
            halo = jnp.where(added, hal[pl.ds(pl.multiple_of(8 * (k - 2), 8), 8), :], before[1, k, BY:YE, :])
            widen(k, level1_plane(m + 1 + H1 // 2, second), before[1, k, own_rows, :], halo)
        return 0

    lax.fori_loop(0, X1 // 2, add, 0, unroll=4)

    def action_x(hi, lo):
        row = (xm0, xm1)[hi][XOWN:XMAIN, :]
        k = X1 + 2
        now = jnp.where(first[own_rows], row, before[1, k, own_rows, :])
        widen(k, level1_plane(1 + H1 // 2 + X1 // 2, 0), now, before[1, k, BY:YE, :])
        row = (xm0, xm1)[lo][XOWN:XMAIN, :]
        now = jnp.where(first[own_rows], before[1, 1, own_rows, :], row)
        widen(1, level1_plane(H1 // 2, 1), now, before[1, 1, BY:YE, :])

    by_parity("gx", action_x)
    for k in (0, NF - 1):
        u[1, k] = before[1, k]
    refs = (c, fin, fout, fyp, fym, fzp, fzm, src, scr, free)
    groups(1, X1 + 2, GF, lambda at: fine_half(u, at, GF, 0, refs))

    def last(at):
        n = 4
        new = fine_new(u, at, n, 1, refs)[:, own_rows]
        even = u[0, pl.ds(at, n), own_rows, :]
        mask = first[own_rows]
        for k in range(n):
            to = pl.multiple_of((at - 2 + k) * 2 * BY, 8)
            res[pl.ds(to, BY), :] = jnp.where(mask, even[k], new[k])
            res[pl.ds(to + BY, BY), :] = jnp.where(mask, new[k], even[k])

    copies = []
    for g in range(X1 // 4):
        last(2 + 4 * g)
        part = pl.ds(g * 8 * BY, 8 * BY)
        copies.append(pltpu.make_async_copy(res.at[part], result.at[part], sems.at[g]))
        copies[-1].start()
    for copy in copies:
        copy.wait()


def swap(pair, axis):
    count = lax.axis_size(axis)
    got = [None, None]
    for first in (1, 0):
        route = []
        for i in range(first, count - 1, 2):
            route += [(i, i + 1), (i + 1, i)]
        got[first] = lax.ppermute(pair[first], axis, route)
    return tuple(got)


def body(source, permittivity, screening, potential, fixed_cell):
    gx, gy = lax.axis_size("gx"), lax.axis_size("gy")
    args = [a.reshape(BX * BY, NL) for a in (potential, permittivity, source, screening, fixed_cell)]
    args = [pltpu.with_memory_space_constraint(a, pltpu.HBM) for a in args]

    whole = (sds(BX * BY, NL),) * 4 + (jax.ShapeDtypeStruct((BX * BY, NL), jnp.int32),)
    *args, p2, y0, y1, xm0, xm1 = call(
        pack_y,
        whole + (sds(8, NL),) + (sds(YROWS + 8, NL),) * 2 + (sds(12 * BY, NL),) * 2,
        [pltpu.SemaphoreType.DMA((5,)), pltpu.VMEM((BX // 4 * BY, NL), F32), pltpu.VMEM((8, NL), F32)],
        hbm=5,
    )(*args)
    y0 = (y0, y1)
    y0 = swap(y0, "gy")
    xm = swap((xm0, xm1), "gx")
    *halos, x0, x1 = call(pack_x, (sds(BX * 8, NL),) * 5 + (sds(XROWS + 24, NL),) * 2)(p2, *y0)
    gotx = swap((x0, x1), "gx")

    ext, one = (2, NF, YE, NL), (NF, YE, NL)
    fields = (sds(*ext),) * 3 + (sds(*one),) + (sds(*ext),) * 8
    fields += (sds(X1 * BY, NL),) * 2 + (sds((X1 + 2) * YE, NL), sds(X1 + 2, 8, NL))
    state = call(fine_own, fields)(*args, *halos)
    fine = call(
        fine_pre,
        fields + (sds(X1 // 2, 8, NL), sds(2, X1 // 2, 8, NL)) + (sds(YMSG, NL),) * 2 + (sds(XMAIN, NL),) * 2,
        alias={6 + k: k for k in range(STATE)},
    )(*y0, *xm, *gotx, *state)
    state, (c1, g1, m0, m1, *xm1) = (fine[0], *fine[2:12]), fine[STATE:]
    goty1 = swap((m0, m1), "gy")
    xm1 = swap(xm1, "gx")
    x1msg = call(pack_x1, (sds(XMSG, NL),) * 2)(*goty1, *gotx)
    gotx1 = swap(x1msg, "gx")

    mid, mid1 = (2, NM, YE, NL), (NM, YE, NL)
    fields1 = (sds(*mid),) * 4 + (sds(*mid1),) + (sds(*mid),) * 5
    level1 = call(mid_own, fields1)(m0, *goty1)
    *level1, message = call(
        mid_pre,
        fields1 + (sds(gx * gy, 16, NL),),
        [
            pltpu.VMEM((G1 // 2 * YE, NL), F32),
            pltpu.VMEM((X1 // 2 * 8, NL), F32),
            pltpu.VMEM((X1 // 2 * 8, NL), F32),
            pltpu.VMEM((3, G1 // 2, NL), F32),
            pltpu.VMEM((24, NL), F32),
        ],
        alias={6 + k: k for k in range(MIDS)},
    )(*xm1, *gotx1, c1, g1, *level1)
    level1 = (*level1[:3], *level1[4:])

    gathered = lax.all_to_all(message, ("gx", "gy"), 0, 0).reshape(gx, gy, 16, NL)
    wx, wy = min(gx, 6), min(gy, 8)
    if (wx, wy) != (gx, gy):
        first = (*window(gx, gy, wx, wy)[:2], 0, 0)
        gathered = lax.dynamic_slice(gathered, first, (wx, wy, 16, NL))

    inputs = (gathered, p2, *y0, *gotx, *level1, *state, *goty1, *xm1, *gotx1)
    result = pl.pallas_call(
        finish_kernel(len(inputs), (gx, gy, wx, wy)),
        out_shape=sds(BX * BY, NL),
        scratch_shapes=[
            pltpu.VMEM((2, wy + 2, wx * 4, NL), F32),
            pltpu.VMEM((2, wy + 2, wx * 4, NL), F32),
            pltpu.VMEM((2, wy, wx * 4, NL), F32),
            pltpu.VMEM((2, wy, wx * 4, NL), F32),
            pltpu.VMEM((2, 6, wy, wx * 4, NL), F32),
            pltpu.VMEM((wy + 6, wx + 4, 8, NL), F32),
            pltpu.VMEM((NF * YE, NL), F32),
            pltpu.VMEM(mid, F32),
            pltpu.VMEM(ext, F32),
            pltpu.VMEM((BX // 2 * 8, NL), F32),
            pltpu.VMEM((BX * BY, NL), F32),
            pltpu.SemaphoreType.DMA((X1 // 4,)),
        ],
        out_specs=pl.BlockSpec(memory_space=pltpu.HBM),
        compiler_params=pltpu.CompilerParams(vmem_limit_bytes=24 << 20),
        name="finish",
    )(*inputs)
    return result.reshape(BX, BY, NL)


def window(gx, gy, wx, wy):
    ix, iy = lax.axis_index("gx"), lax.axis_index("gy")
    fx = jnp.clip(ix - 2, 0, gx - wx)
    fy = jnp.clip(iy - 3, 0, gy - wy)
    return fx, fy, ix - fx, iy - fy


def finish_kernel(count, sizes):
    def kernel(*refs):
        ins, result, scratch = list(refs[:count]), refs[count], list(refs[1 + count :])
        finish(window(*sizes)[2:], *ins, result, *scratch)

    return kernel


def solution(mesh):
    placed = (P("gx", "gy", None),) * 5

    return jax.shard_map(body, mesh=mesh, in_specs=placed, out_specs=P("gx", "gy", None), check_vma=False)
```

```python
import jax
import jax.numpy as jnp
from jax import lax
from jax.experimental import pallas as pl
from jax.experimental.pallas import tpu as pltpu
from jax.sharding import PartitionSpec as P

F32 = jnp.float32
BX, BY, NL = 32, 16, 128
YE = 24
X1 = BX // 2
H1 = 8
G1 = X1 + 2 * H1
NF = X1 + 4
NM = G1 // 2 + 2
STATE = 16
GF = 3
GM = 8
LN2 = 0.6931471805599453


def rot(value, shift, axis):
    return pltpu.roll(value, shift % value.shape[axis], axis)


def iota(shape, axis):
    return lax.broadcasted_iota(jnp.int32, shape, axis)


def sds(*shape):
    return jax.ShapeDtypeStruct(shape, F32)


def by_parity(axis, action):
    odd = lax.axis_index(axis) % 2

    @pl.when(odd == 0)
    def _():
        action(0, 1)

    @pl.when(odd == 1)
    def _():
        action(1, 0)


def call(kernel, out_shape, scratch=(), vmem=24, hbm=0, alias=None):
    specs = {"in_specs": [pl.BlockSpec(memory_space=pltpu.HBM)] * hbm} if hbm else {}
    return pl.pallas_call(
        kernel,
        out_shape=out_shape,
        **specs,
        input_output_aliases=alias or {},
        scratch_shapes=list(scratch),
        compiler_params=pltpu.CompilerParams(vmem_limit_bytes=vmem << 20),
    )


YROWS = 10 * BX
XROWS = 12 * 8
FIELDS = (3, 3, 2, 2, 2)


def split_rows(ref, at):
    one, two = ref[pl.ds(at, 4, stride=2), :], ref[pl.ds(at + 1, 4, stride=2), :]
    lane = iota((4, NL), 1)
    even = (lane % 4 + lane // 4) % 2 == 0
    return jnp.concatenate([jnp.where(even, one, two), jnp.where(even, two, one)], axis=0)


def pack_y(hpot, hper, hsrc, hscr, hfix, pot, per, src, scr, fix, p2, out0, out1, xm0, xm1, sems, t, pk):
    outs, mains = (out0, out1), (xm0, xm1)
    pairs = ((hpot, pot), (hper, per), (hsrc, src), (hscr, scr), (hfix, fix))
    copies = [pltpu.make_async_copy(a, b, sems.at[k]) for k, (a, b) in enumerate(pairs)]
    for k in (1, 0, 2, 3, 4):
        copies[k].start()
    copies[1].wait()
    zlane = iota((BX // 2, NL), 1)

    def free_of(value):
        return jnp.where(value == 0, F32(1.0), F32(0.0))

    def row(ref, r):
        return ref[pl.ds(r, BX, stride=BY), :]

    def half(ref, r, parity):
        even = ref[pl.ds(r, BX // 2, stride=2 * BY), :]
        odd = ref[pl.ds(BY + r, BX // 2, stride=2 * BY), :]
        return jnp.where((r + zlane) % 2 == parity, even, odd)

    def side(out, r1, r2, r3):
        rows = [
            row(pot, r1), row(per, r1), row(src, r1), row(scr, r1), free_of(row(fix, r1)),
            row(pot, r2), row(per, r2), free_of(row(fix, r2)),
        ]
        for k, value in enumerate(rows):
            out[BX * k : BX * (k + 1), :] = value
        base = BX * len(rows)
        for k, value in enumerate([half(pot, r3, 1), half(per, r3, 1), half(src, r2, 0), half(scr, r2, 0)]):
            out[base + k * BX // 2 : base + (k + 1) * BX // 2, :] = value

    v = per[...].reshape(BX // 4, 4, BY, NL)
    v = (v[:, 0] + v[:, 1]) + (v[:, 2] + v[:, 3])
    t[...] = lane_pairs(lane_pairs(v, 1), 2).reshape(BX // 4 * BY, NL)
    n2 = BX // 4
    lane = iota((n2, NL), 1)
    total = None
    for j in range(4):
        r = [t[pl.ds(4 * j + k, n2, stride=BY), :] for k in range(4)]
        value = (r[0] + r[1]) + (r[2] + r[3])
        total = value if total is None else jnp.where(lane % 4 == j, value, total)
    pk[...] = F32(1.0 / 64) * total
    p2[...] = split_rows(pk, 0)
    for k in (0, 2, 3, 4):
        copies[k].wait()

    def action(hi, lo):
        side(outs[hi], BY - 1, BY - 2, BY - 3)
        side(outs[lo], 0, 1, 2)
        for out in outs:
            out[YROWS : YROWS + 8, :] = p2[...]

    by_parity("gy", action)

    def slab(out, planes):
        k = 0
        for ref, depth in zip((pot, per, src, scr, fix), FIELDS, strict=True):
            for x in planes[:depth]:
                value = ref[BY * x : BY * (x + 1), :]
                out[BY * k : BY * (k + 1), :] = free_of(value) if ref is fix else value
                k += 1

    def action_x(hi, lo):
        slab(mains[hi], (BX - 1, BX - 2, BX - 3))
        slab(mains[lo], (0, 1, 2))

    by_parity("gx", action_x)


def pack_x(p2, got0, got1, hpot, hper, hsrc, hscr, hfree, out0, out1):
    gots, outs = (got0, got1), (out0, out1)
    halos = (hpot, hper, hsrc, hscr, hfree)
    for h in halos:
        h[...] = jnp.zeros_like(h)

    def place(got, slots):
        def whole(ref, k, slot):
            ref[pl.ds(slot, BX, stride=8), :] = got[BX * k : BX * (k + 1), :]

        def halved(ref, k, slot):
            value = got[BX * 8 + k * BX // 2 : BX * 8 + (k + 1) * BX // 2, :]
            ref[pl.ds(slot, BX // 2, stride=16), :] = value
            ref[pl.ds(8 + slot, BX // 2, stride=16), :] = value

        s1, s2, s3 = slots
        for k, ref in enumerate(halos):
            whole(ref, k, s1)
        whole(hpot, 5, s2)
        whole(hper, 6, s2)
        whole(hfree, 7, s2)
        halved(hpot, 0, s3)
        halved(hper, 1, s3)
        halved(hsrc, 2, s2)
        halved(hscr, 3, s2)

    def action_y(hi, lo):
        place(gots[hi], (0, 1, 2))
        place(gots[lo], (7, 6, 5))

    by_parity("gy", action_y)

    def slab(out, planes):
        k = 0
        for h, depth in zip(halos, FIELDS, strict=True):
            for x in planes[:depth]:
                out[8 * k : 8 * (k + 1), :] = h[8 * x : 8 * (x + 1), :]
                k += 1

    def action_p(hi, lo):
        for out in outs:
            out[XROWS : XROWS + 8, :] = p2[...]
            out[XROWS + 8 : XROWS + 16, :] = gots[hi][YROWS : YROWS + 8, :]
            out[XROWS + 16 : XROWS + 24, :] = gots[lo][YROWS : YROWS + 8, :]

    by_parity("gy", action_p)

    def action_x(hi, lo):
        slab(outs[hi], (BX - 1, BX - 2, BX - 3))
        slab(outs[lo], (0, 1, 2))

    by_parity("gx", action_x)


def nonlinear(u, scr):
    up = jnp.exp(u - F32(LN2))
    down = jnp.exp(-u - F32(LN2))
    return scr * (up - down), scr * (up + down)


def colour_mask(n, zstep):
    shape = (n, YE, NL)
    return (iota(shape, 1) + iota(shape, 2) // zstep) % 2 == 0


def beside_of(other, colour, faces, at, n, zstep):
    fin, fout, fyp, fym, fzp, fzm = faces
    here = pl.ds(at, n)
    v = other[1 - colour, pl.ds(at - 1, n + 2)]
    mid = v[1 : n + 1]
    first = colour_mask(n, zstep)
    across = jnp.where(first, v[:n], v[2:]) if colour == 0 else jnp.where(first, v[2:], v[:n])
    return (
        (fin[here] * mid + fout[colour, here] * across)
        + (fyp[colour, here] * rot(mid, -1, 1) + fym[colour, here] * rot(mid, 1, 1))
        + (fzp[colour, here] * rot(mid, -zstep, 2) + fzm[colour, here] * rot(mid, zstep, 2))
    )


def pairs_of(u, at, n, colour, refs):
    c, fin, fout, fyp, fym, fzp, fzm, src, scr, _ = refs
    here = pl.ds(at, n)
    plane = u[colour, here]
    sh, ch = nonlinear(plane, scr[colour, here])
    centre = c[colour, here]
    beside = beside_of(u, colour, (fin, fout, fyp, fym, fzp, fzm), at, n, 1)
    return plane, centre * plane - beside + sh - src[colour, here], centre, ch


def fine_new(u, at, n, colour, refs):
    plane, value, centre, ch = pairs_of(u, at, n, colour, refs)
    return jnp.where(refs[-1][colour, pl.ds(at, n)] > 0.5, plane - value / (centre + ch), plane)


def fine_half(u, at, n, colour, refs):
    u[colour, pl.ds(at, n)] = fine_new(u, at, n, colour, refs)


def groups(first, count, n, step):
    assert count % n == 0

    def one(g, _):
        step(first + g * n)
        return 0

    lax.fori_loop(0, count // n, one, 0, unroll=True)


def faces_of(p, at, n, scale, zstep, fin, fout, fyp, fym, fzp, fzm):
    here = pl.ds(at, n)
    lane = iota((n, YE, NL), 2)
    first = colour_mask(n, zstep)
    half = F32(0.5 * scale)
    for colour in (0, 1):
        plane = p[colour, here]
        v = p[1 - colour, pl.ds(at - 1, n + 2)]
        mid = v[1 : n + 1]
        across = jnp.where(first, v[:n], v[2:]) if colour == 0 else jnp.where(first, v[2:], v[:n])
        if colour == 0:
            fin[here] = half * (plane + mid)
        fout[colour, here] = half * (plane + across)
        fyp[colour, here] = half * (plane + rot(mid, -1, 1))
        fym[colour, here] = half * (plane + rot(mid, 1, 1))
        fzp[colour, here] = jnp.where(lane >= NL - zstep, F32(0.0), half * (plane + rot(mid, -zstep, 2)))
        fzm[colour, here] = jnp.where(lane < zstep, F32(0.0), half * (plane + rot(mid, zstep, 2)))


def lane_pairs(value, step):
    lane = iota(value.shape, value.ndim - 1)
    return value + jnp.where((lane // step) % 2 == 0, rot(value, -step, value.ndim - 1), rot(value, step, value.ndim - 1))


def fine_begin(state, at, n):
    u, ep, c, fin, fout, fyp, fym, fzp, fzm, esrc, escr, efree = state[:12]
    faces_of(ep, at, n, 1.0, 1, fin, fout, fyp, fym, fzp, fzm)
    here = pl.ds(at, n)
    lane = iota((n, YE, NL), 2)
    for colour in (0, 1):
        ends = jnp.where((lane == 0) | (lane == NL - 1), F32(0.5) * ep[colour, here], F32(0.0))
        c[colour, here] = (
            (fin[here] + fout[colour, here]) + (fyp[colour, here] + fym[colour, here])
            + (fzp[colour, here] + fzm[colour, here]) + ends
        )
    fine_half(u, at, n, 0, (c, fin, fout, fyp, fym, fzp, fzm, esrc, escr, efree))


def fine_own(pot, per, src, scr, fix, hpot, hper, hsrc, hscr, hfree, *state):
    u, ep, c, fin, fout, fyp, fym, fzp, fzm, esrc, escr, efree = state[:12]
    first = colour_mask(1, 1)[0]

    def own(k, _):
        for ref, h, ext in ((pot, hpot, u), (per, hper, ep), (src, hsrc, esrc), (scr, hscr, escr), (fix, hfree, efree)):
            value = ref[pl.ds(pl.multiple_of(2 * k * BY, 8), 2 * BY), :]
            if ref is fix:
                value = jnp.where(value == 0, F32(1.0), F32(0.0))
            halo = h[pl.ds(pl.multiple_of(16 * k, 8), 16), :]
            for rows, one, two in (
                (slice(0, BY), value[:BY], value[BY:]),
                (slice(BY, YE), halo[:8], halo[8:]),
            ):
                ext[0, k + 2, rows, :] = jnp.where(first[rows], one, two)
                ext[1, k + 2, rows, :] = jnp.where(first[rows], two, one)
        return 0

    lax.fori_loop(0, X1, own, 0, unroll=4)
    groups(3, X1 - 2, 2, lambda at: fine_begin(state, at, 2))
    refs = (c, fin, fout, fyp, fym, fzp, fzm, esrc, escr, efree)
    groups(4, X1 - 4, 3, lambda at: fine_half(u, at, 3, 1, refs))
    groups(6, X1 - 8, 4, lambda at: fine_down(state, at, 4))
    for k in range(1, X1 + 1):
        fine_coarse_p(state, k)


def fine_down(state, at, n):
    u, _, c, fin, fout, fyp, fym, fzp, fzm, esrc, escr, efree, tr, tc = state[:14]
    refs = (c, fin, fout, fyp, fym, fzp, fzm, esrc, escr, efree)
    left, react = F32(0.0), F32(0.0)
    for colour in (0, 1):
        _, value, _, ch = pairs_of(u, at, n, colour, refs)
        left += jnp.where(efree[colour, pl.ds(at, n)] > 0.5, -value, F32(0.0))
        react += ch
    to = pl.multiple_of((at - 2) * BY, 8)
    tr[pl.ds(to, n * BY), :] = lane_pairs(left[:, 0:BY], 1).reshape(n * BY, NL)
    tc[pl.ds(to, n * BY), :] = lane_pairs(react[:, 0:BY], 1).reshape(n * BY, NL)


def fine_coarse_p(state, k):
    ep, tp, p1 = state[1], state[14], state[15]
    at = k * YE
    tp[at : at + YE, :] = lane_pairs(ep[0, k + 1] + ep[1, k + 1], 1)
    p1[k] = F32(0.125) * (tp[pl.ds(at, 8, stride=2), :] + tp[pl.ds(at + 1, 8, stride=2), :])


def fine_pre(goty0, goty1, xm0, xm1, got0, got1, *refs_):
    state, refs_ = refs_[STATE : 2 * STATE], refs_[2 * STATE :]
    u, ep, c, fin, fout, fyp, fym, fzp, fzm, esrc, escr, efree, tr, tc, tp, p1 = state
    csum, g1, m0, m1, n0, n1 = refs_
    gots, mains, outs, nexts = (got0, got1), (xm0, xm1), (m0, m1), (n0, n1)
    first = colour_mask(1, 1)[0]

    def place(main, got, near, far, flip):
        k = 0
        for ext, depth in zip((u, ep, esrc, escr, efree), FIELDS, strict=True):
            planes = []
            for _ in range(depth):
                rows = main[BY * k : BY * (k + 1), :]
                planes.append(jnp.concatenate([rows, got[8 * k : 8 * (k + 1), :]], axis=0))
                k += 1
            one, two = (planes[1], planes[0]) if flip else (planes[0], planes[1])
            ext[0, near] = jnp.where(first, one, two)
            ext[1, near] = jnp.where(first, two, one)
            third = planes[2] if depth == 3 else jnp.zeros((YE, NL), F32)
            ext[0, far] = third
            ext[1, far] = third

    def action_x(hi, lo):
        place(mains[hi], gots[hi], X1 + 2, X1 + 3, False)
        place(mains[lo], gots[lo], 1, 0, True)

    by_parity("gx", action_x)
    refs = (c, fin, fout, fyp, fym, fzp, fzm, esrc, escr, efree)

    for at in (1, X1 + 1):
        fine_begin(state, at, 2)
    for at in (1, X1):
        fine_half(u, at, 3, 1, refs)
    for at in (2, X1 - 2):
        fine_down(state, at, 4)
    for k in (0, X1 + 1):
        fine_coarse_p(state, k)

    eighth = F32(0.125)
    sub = iota((8, NL), 0)
    lane = iota((8, NL), 1)

    first8 = (sub + lane // 2) % 2 == 0

    def coarse(x1):
        k = x1 + 1
        p = p1[k]
        base = k * YE
        high = eighth * (tp[pl.ds(base + 2, 8, stride=2), :] + tp[pl.ds(base + 3, 8, stride=2), :])
        edge = tp[pl.ds(pl.multiple_of(base + 16, 8), 8), :]
        edge = eighth * (edge + rot(edge, 1, 0))
        low = jnp.where(sub == 0, rot(edge, 1, 0), rot(p, 1, 0))
        front = jnp.where(lane >= NL - 2, F32(0.0), rot(p, -2, 1))
        back = jnp.where(lane < 2, F32(0.0), rot(p, 2, 1))
        near = (p1[k + 1] + p1[k - 1]) + (high + low) + (front + back)
        centre = F32(3.0) * p + F32(0.5) * near
        at = x1 * BY
        r = eighth * (tr[pl.ds(at, 8, stride=2), :] + tr[pl.ds(at + 1, 8, stride=2), :])
        react = eighth * (tc[pl.ds(at, 8, stride=2), :] + tc[pl.ds(at + 1, 8, stride=2), :])
        diag = F32(0.25) * centre + react
        message = jnp.where(lane % 2 == 0, r, F32(1.0) / diag)
        m0[pl.ds(pl.multiple_of(x1 * 8, 8), 8), :] = message
        m1[pl.ds(pl.multiple_of(x1 * 8, 8), 8), :] = message
        return diag, react

    def make(k, _):
        diag0, react0 = coarse(2 * k)
        diag1, react1 = coarse(2 * k + 1)
        csum[k] = react0 + react1
        g1[0, k] = jnp.where(first8, diag0, diag1)
        g1[1, k] = jnp.where(first8, diag1, diag0)
        return 0

    lax.fori_loop(0, X1 // 2, make, 0, unroll=4)

    for a in range(X1 // 2):
        message = jnp.where(lane % 2 == 0, p1[1 + 2 * a], p1[2 + 2 * a])
        for m in outs:
            m[X1 * 8 + 8 * a : X1 * 8 + 8 * a + 8, :] = message

    base = X1 * 8 + X1 * 4

    def odd_row(out, y):
        out[base : base + X1, :] = u[1, pl.ds(2, X1), y, :]

    def slab(out, at, x):
        out[0 : H1 * 8, :] = m0[8 * at : 8 * (at + H1), :]
        row = X1 * 8 + 4 * at
        out[H1 * 8 : H1 * 12, :] = m0[row : row + H1 * 4, :]
        out[XOWN:XMAIN, :] = u[1, x, 0:BY, :]

    def action_next(hi, lo):
        slab(nexts[hi], X1 - H1, X1 + 1)
        slab(nexts[lo], 0, 2)

    by_parity("gx", action_next)

    def action_y(hi, lo):
        odd_row(outs[hi], BY - 2)
        odd_row(outs[lo], 1)
        outs[hi][base + X1 : base + X1 + 8, :] = (goty0, goty1)[lo][YROWS : YROWS + 8, :]
        outs[lo][base + X1 : base + X1 + 8, :] = (goty0, goty1)[hi][YROWS : YROWS + 8, :]

    by_parity("gy", action_y)


def halo_rows(dx):
    return (16 * (dx - 1), 2) if dx < 5 else (64 + 8 * (dx - 5), 1)


def halo_pair(t):
    return (96 + 16 * t, 2) if t < 2 else (128 + 8 * (t - 2), 1)


P2AT = 144
YMSG = X1 * 8 + X1 * 4 + BX // 2 + 8
XOWN = H1 * 8 + (H1 // 2) * 8
XMAIN = XOWN + BY
XMSG = P2AT + 40


def pack_x1(got0, got1, fx0, fx1, out0, out1):
    gots, outs, fines = (got0, got1), (out0, out1), (fx0, fx1)
    odd_y = lax.axis_index("gy") % 2
    upper = iota((8, NL), 0) < 4

    def go(hi, lo):
        def put(out, at, count, row):
            above, below = gots[hi][row : row + 8, :], gots[lo][row : row + 8, :]
            if count == 2:
                out[at : at + 8, :] = above
                out[at + 8 : at + 16, :] = below
            else:
                out[at : at + 8, :] = jnp.where(upper, above, below)

        def slab(out, near, step, behind):
            for dx in range(1, H1 + 1):
                put(out, *halo_rows(dx), 8 * (near + step * (dx - 1)))
            for t in range(H1 // 2):
                put(out, *halo_pair(t), X1 * 8 + 8 * (near // 2 + step * t))
            out[P2AT : P2AT + 8, :] = gots[hi][YMSG - 8 : YMSG, :]
            out[P2AT + 8 : P2AT + 16, :] = gots[lo][YMSG - 8 : YMSG, :]
            out[P2AT + 16 : P2AT + 40, :] = behind[XROWS : XROWS + 24, :]

        def action(xhi, xlo):
            slab(outs[xhi], X1 - 1, -1, fines[xlo])
            slab(outs[xlo], 0, 1, fines[xhi])

        by_parity("gx", action)

    @pl.when(odd_y == 0)
    def _():
        go(0, 1)

    @pl.when(odd_y == 1)
    def _():
        go(1, 0)


def coarse_half(e, r, d, at, n, colour, faces, zstep):
    here = pl.ds(at, n)
    e[colour, here] = (r[colour, here] + beside_of(e, colour, faces, at, n, zstep)) * d[colour, here]


def dup_even(value):
    lane = iota(value.shape, value.ndim - 1)
    return jnp.where(lane % 2 == 0, value, rot(value, 1, value.ndim - 1))


def dup_odd(value):
    lane = iota(value.shape, value.ndim - 1)
    return jnp.where(lane % 2 == 1, value, rot(value, -1, value.ndim - 1))


MIDS = 10


def mid_put(state, k, rows, one, two, both):
    _, r, d, p = state[:4]
    mask = colour_mask(1, 2)[0][rows]
    for colour in (0, 1):
        a, b = (one, two) if colour == 0 else (two, one)
        value = jnp.where(mask, a, b)
        r[colour, k, rows, :] = dup_even(value)
        d[colour, k, rows, :] = dup_odd(value)
    a, b = dup_even(both), dup_odd(both)
    p[0, k, rows, :] = jnp.where(mask, a, b)
    p[1, k, rows, :] = jnp.where(mask, b, a)


def mid_begin(state, at, n):
    e, r, d, p, *faces = state
    here = pl.ds(at, n)
    faces_of(p, at, n, 0.25, 2, *faces)
    e[0, here] = r[0, here] * d[0, here]


def mid_own(m0, gy0, gy1, *state):
    gys = (gy0, gy1)
    e, r, d, p, *faces = state

    def own(hi, lo):
        for k in range(X1 // 2):
            for j, ref in enumerate((m0, gys[hi], gys[lo])):
                two = ref[16 * k : 16 * k + 16, :]
                both = ref[X1 * 8 + 8 * k : X1 * 8 + 8 * k + 8, :]
                mid_put(state, 1 + H1 // 2 + k, slice(8 * j, 8 * j + 8), two[:8], two[8:], both)

    by_parity("gy", own)
    first = 2 + H1 // 2
    groups(first, X1 // 2 - 2, 2, lambda at: mid_begin(state, at, 2))
    groups(first + 1, X1 // 2 - 4, 2, lambda at: coarse_half(e, r, d, at, 2, 1, faces, 2))


def mid_pre(xm0, xm1, gx0, gx1, csum, g1, *refs_):
    gxs, mains = (gx0, gx1), (xm0, xm1)
    state, refs_ = refs_[MIDS : 2 * MIDS], refs_[2 * MIDS :]
    e, r, d, p, *faces = state
    fin, fout, fyp, fym, fzp, fzm = faces
    msg, t, tr, tc, pc, pk = refs_

    def beyond(main, ref, at, far):
        def whole(row, start, count):
            own_rows = main[row : row + 8, :]
            above = ref[start : start + 8, :]
            below = ref[start + 8 : start + 16, :] if count == 2 else above
            return jnp.concatenate([own_rows, above, below], axis=0)

        for k in range(H1 // 2):
            one, two = (whole(8 * a, *halo_rows(H1 - a if far else a + 1)) for a in (2 * k, 2 * k + 1))
            both = whole(H1 * 8 + 8 * k, *halo_pair(H1 // 2 - 1 - k if far else k))
            mid_put(state, at + k, slice(0, YE), one, two, both)

    def action(hi, lo):
        beyond(mains[hi], gxs[hi], 1 + H1 // 2 + X1 // 2, False)
        beyond(mains[lo], gxs[lo], 1, True)

    by_parity("gx", action)
    for ref in (p, e):
        for colour in (0, 1):
            ref[colour, 0] = jnp.zeros((YE, NL), F32)
            ref[colour, NM - 1] = jnp.zeros((YE, NL), F32)
    inner = 1 + H1 // 2
    for at in (*range(1, inner + 1), *range(inner + X1 // 2 - 1, NM - 1)):
        mid_begin(state, at, 1)
    for at in (1, inner + X1 // 2 - 2):
        coarse_half(e, r, d, at, inner + 1, 1, faces, 2)
    for colour in (0, 1):
        groups(1, NM - 2, GM, lambda at, colour=colour: coarse_half(e, r, d, at, GM, colour, faces, 2))

    def down(at):
        n = 4
        here = pl.ds(at, n)
        k = pl.ds(at - 1 - H1 // 2, n)
        left = F32(0.0)
        for colour in (0, 1):
            part = r[colour, here] + beside_of(e, colour, faces, at, n, 2)
            left += part[:, 0:8] - g1[colour, k] * e[colour, here, 0:8, :]
        to = pl.multiple_of((at - 1 - H1 // 2) * 8, 8)
        tr[pl.ds(to, n * 8), :] = lane_pairs(left, 2).reshape(n * 8, NL)
        tc[pl.ds(to, n * 8), :] = lane_pairs(csum[k], 2).reshape(n * 8, NL)

    groups(1 + H1 // 2, X1 // 2, 4, down)

    def coarse_p(x2, _):
        t[pl.ds(pl.multiple_of(x2 * YE, 8), YE), :] = lane_pairs(p[0, x2 + 1] + p[1, x2 + 1], 2)
        return 0

    lax.fori_loop(0, G1 // 2, coarse_p, 0, unroll=4)

    eighth = F32(0.125)
    n2, m2 = X1 // 2, G1 // 2

    def compact(ref, first, rows, stride):
        lane = iota((rows, NL), 1)
        out = None
        for j in range(4):
            value = ref[pl.ds(first + 2 * j, rows, stride=stride), :] + ref[pl.ds(first + 2 * j + 1, rows, stride=stride), :]
            out = value if out is None else jnp.where(lane % 4 == j, value, out)
        return eighth * out

    r2 = compact(tr, 0, n2, 8)
    react2 = compact(tc, 0, n2, 8)
    for k in range(3):
        pc[k] = compact(t, 8 * k, m2, YE)
    h2 = H1 // 2
    centre_p = pc[0, h2 : h2 + n2, :]
    j4 = iota((n2, NL), 1) % 4
    lane = iota((n2, NL), 1)
    high = jnp.where(j4 < 3, rot(centre_p, -1, 1), rot(pc[1, h2 : h2 + n2, :], 3, 1))
    low = jnp.where(j4 > 0, rot(centre_p, 1, 1), rot(pc[2, h2 : h2 + n2, :], -3, 1))
    front = jnp.where(lane >= NL - 4, F32(0.0), rot(centre_p, -4, 1))
    back = jnp.where(lane < 4, F32(0.0), rot(centre_p, 4, 1))
    near = (pc[0, h2 + 1 : h2 + 1 + n2, :] + pc[0, h2 - 1 : h2 - 1 + n2, :]) + (high + low) + (front + back)
    diag2 = F32(0.0625) * (F32(3.0) * centre_p + F32(0.5) * near) + react2
    for k, value in enumerate((r2, F32(1.0) / diag2, centre_p)):
        pk[8 * k : 8 * k + 8, :] = value
    r2, inverse2, own_p = (split_rows(pk, 8 * k) for k in range(3))
    near_rows = iota((8, NL), 1) % 4 >= 2
    ahead = jnp.where(near_rows, r2, rot(own_p, -2, 1))
    behind = jnp.where(near_rows, rot(own_p, 2, 1), r2)
    count = lax.axis_size("gy")
    place = lax.axis_index("gy")

    def every(k, _):
        step = k % count - place
        msg[k, 0:8, :] = jnp.where(step == 3, ahead, jnp.where(step == -3, behind, r2))
        msg[k, 8:16, :] = inverse2
        return 0

    lax.fori_loop(0, msg.shape[0], every, 0, unroll=8)


def finish(at, got, p2own, yf0, yf1, xf0, xf1, e, r, d, fin1, fout1, fyp1, fym1, fzp1, fzm1,
           before, c, fin, fout, fyp, fym, fzp, fzm, src, scr, free, gy0, gy1, xm0, xm1, gx0, gx1,
           result,
           e2, p2, r2, d2, k2, blk, tx, eu, u, hal, res, sems):
    wx, wy = got.shape[0], got.shape[1]
    rows = wx * 4
    ox, oy = at
    blk[...] = jnp.zeros_like(blk)
    for b in (0, wy + 1):
        for colour in (0, 1):
            e2[colour, b] = jnp.zeros((rows, NL), F32)

    def keep(da, db, ref, first):
        blk[oy + db + 3, ox + da + 2] = ref[first : first + 8, :]

    keep(0, 0, p2own, 0)

    def blocks_y(hi, lo):
        for db, k in ((1, hi), (-1, lo)):
            keep(0, db, (yf0, yf1)[k], YROWS)
            keep(0, 2 * db, (gy0, gy1)[k], YMSG - 8)

    by_parity("gy", blocks_y)

    def blocks_x(hi, lo):
        for da, k in ((1, hi), (-1, lo)):
            fine, mid = (xf0, xf1)[k], (gx0, gx1)[k]
            for n, db in enumerate((0, 1, -1)):
                keep(da, db, fine, XROWS + 8 * n)
                keep(2 * da, db, mid, P2AT + 16 + 8 * n)
            keep(da, 2, mid, P2AT)
            keep(da, -2, mid, P2AT + 8)

    by_parity("gx", blocks_x)
    l4 = iota((8, NL), 1) % 4
    for db in (3, -3):

        @pl.when((oy + db >= 0) & (oy + db < wy))
        def _(db=db):
            for a in range(wx):
                value = got[a, oy + db, 0:8, :]
                value = jnp.where(l4 < 2, rot(value, -2, 1), F32(0.0)) if db > 0 else jnp.where(l4 >= 2, rot(value, 2, 1), F32(0.0))
                blk[oy + db + 3, a + 2] = value

    def spread(b, _):
        for a in range(wx):
            for colour in (0, 1):
                own, to = slice(4 * colour, 4 * colour + 4), slice(4 * a, 4 * a + 4)
                r2[colour, b, to, :] = got[a, b, own, :]
                d2[colour, b, to, :] = got[a, b, 8 + 4 * colour : 12 + 4 * colour, :]
                p2[colour, b + 1, to, :] = blk[b + 3, a + 2, own, :]
        return 0

    lax.fori_loop(0, wy, spread, 0, unroll=4)
    for b in (0, wy + 1):
        for colour in (0, 1):
            p2[colour, b] = jnp.zeros((rows, NL), F32)
    shape = (wy, rows, NL)
    sub, lane = iota(shape, 1), iota(shape, 2)
    j4 = lane % 4
    even = (j4 + lane // 4) % 2 == 0

    def around(ref, colour, b, n):
        v = ref[1 - colour, pl.ds(b, n + 2)]
        mid = v[1 : n + 1]
        one, two = rot(mid, 1, 1), rot(mid, -1, 1)
        mask, j = even[:n], j4[:n]
        return (
            mid,
            jnp.where(mask, one, two) if colour == 0 else jnp.where(mask, two, one),
            jnp.where(j < 3, rot(mid, -1, 2), rot(v[2:], 3, 2)),
            jnp.where(j > 0, rot(mid, 1, 2), rot(v[:n], -3, 2)),
            rot(mid, -4, 2), rot(mid, 4, 2),
        )

    for colour in (0, 1):
        at_first = even if colour == 0 else ~even
        outside = (at_first & (sub == 0)) | (~at_first & (sub == rows - 1))
        edges = (None, outside, None, None, lane >= NL - 4, lane < 4)
        mine = p2[colour, 1 : wy + 1]
        for k, (value, edge) in enumerate(zip(around(p2, colour, 0, wy), edges, strict=True)):
            face = F32(0.03125) * (mine + value)
            k2[colour, k] = face if edge is None else jnp.where(edge, F32(0.0), face)
    e2[0, 1 : wy + 1] = r2[0] * d2[0]

    def half2(colour, b, n):
        here = pl.ds(b, n)
        total = r2[colour, here]
        for k, value in enumerate(around(e2, colour, b, n)):
            total = total + k2[colour, k, here] * value
        e2[colour, pl.ds(b + 1, n)] = total * d2[colour, here]

    half2(1, 0, wy)
    for reach, colours in ((2, (0, 1, 0, 1)), (1, (0, 1))):
        n = min(2 * reach + 1, wy)
        start_b = jnp.clip(oy - reach, 0, wy - n)
        for colour in colours:
            half2(colour, start_b, n)

    s8, l8 = iota((8, NL), 0), iota((8, NL), 1)
    even8 = (l8 % 4 + l8 // 4) % 2 == 0
    start = 4 * ox - 2
    inside = (s8 + start >= 0) & (s8 + start < rows)
    for k, step in enumerate((0, 1, -1)):
        near = []
        for colour in (0, 1):
            block = pltpu.roll(e2[colour, oy + step + 1], (rows - start) % rows, 0)[0:8]
            near.append(jnp.where(inside, block, F32(0.0)))
        planes = (jnp.where(even8, near[0], near[1]), jnp.where(even8, near[1], near[0]))
        for second in (0, 1):
            for j in range(4):
                value = jnp.where(l8 % 4 == 0, rot(planes[second], -j, 1), F32(0.0))
                value = value + rot(value, 1, 1)
                value = value + rot(value, 2, 1)
                for y in (0, 1):
                    tx[pl.ds(second * YE + 8 * k + 2 * j + y, 8, stride=2 * YE), :] = value

    def correct(x2, _):
        value = tx[pl.ds(pl.multiple_of(x2 * YE, 8), YE), :]
        for colour in (0, 1):
            eu[colour, x2 + 1] = e[colour, x2 + 1] + value
        return 0

    lax.fori_loop(0, G1 // 2, correct, 0, unroll=4)
    faces1 = (fin1, fout1, fyp1, fym1, fzp1, fzm1)
    for at1, count, n, colour in ((3, 12, 4, 0), (3, 12, 4, 1), (4, 10, 5, 0), (4, 10, 5, 1)):
        groups(at1, count, n, lambda at, n=n, colour=colour: coarse_half(eu, r, d, at, n, colour, faces1, 2))

    base = X1 * 8 + X1 * 4

    def action_y(hi, lo):
        hal[pl.ds(1, X1, stride=8), :] = (gy0, gy1)[hi][base : base + X1, :]
        hal[pl.ds(6, X1, stride=8), :] = (gy0, gy1)[lo][base : base + X1, :]

    by_parity("gy", action_y)
    first = colour_mask(1, 1)[0]
    first1 = colour_mask(1, 2)[0]
    added = (s8 == 1) | (s8 == 6)
    own_rows = slice(0, BY)

    def widen(k, plane, now1, halo1):
        for y in (0, 1):
            tx[pl.ds(k * YE + y, 8, stride=2), :] = plane[0:8]
        wide = tx[pl.ds(pl.multiple_of(k * YE, 8), BY), :]
        hi, lo = plane[8:16], plane[16:24]
        halo = jnp.where(s8 < 2, jnp.where(s8 == 0, hi, rot(hi, 1, 0)), jnp.where(s8 == 7, lo, rot(lo, -1, 0)))
        now = ((before[0, k, own_rows, :], before[0, k, BY:YE, :]), (now1, halo1))
        for colour in (0, 1):
            one, two = now[colour]
            u[colour, k, own_rows, :] = jnp.where(free[colour, k, own_rows, :] > 0.5, one + wide, one)
            u[colour, k, BY:YE, :] = jnp.where(free[colour, k, BY:YE, :] > 0.5, two + halo, two)

    def level1_plane(m, second):
        one, two = (eu[1, m], eu[0, m]) if second else (eu[0, m], eu[1, m])
        return jnp.where(first1, one, two)

    def add(m, _):
        for second in (0, 1):
            k = 2 * m + second + 2
            halo = jnp.where(added, hal[pl.ds(pl.multiple_of(8 * (k - 2), 8), 8), :], before[1, k, BY:YE, :])
            widen(k, level1_plane(m + 1 + H1 // 2, second), before[1, k, own_rows, :], halo)
        return 0

    lax.fori_loop(0, X1 // 2, add, 0, unroll=4)

    def action_x(hi, lo):
        row = (xm0, xm1)[hi][XOWN:XMAIN, :]
        k = X1 + 2
        now = jnp.where(first[own_rows], row, before[1, k, own_rows, :])
        widen(k, level1_plane(1 + H1 // 2 + X1 // 2, 0), now, before[1, k, BY:YE, :])
        row = (xm0, xm1)[lo][XOWN:XMAIN, :]
        now = jnp.where(first[own_rows], before[1, 1, own_rows, :], row)
        widen(1, level1_plane(H1 // 2, 1), now, before[1, 1, BY:YE, :])

    by_parity("gx", action_x)
    for k in (0, NF - 1):
        u[1, k] = before[1, k]
    refs = (c, fin, fout, fyp, fym, fzp, fzm, src, scr, free)
    groups(1, X1 + 2, GF, lambda at: fine_half(u, at, GF, 0, refs))

    def last(at):
        n = 4
        new = fine_new(u, at, n, 1, refs)[:, own_rows]
        even = u[0, pl.ds(at, n), own_rows, :]
        mask = first[own_rows]
        for k in range(n):
            to = pl.multiple_of((at - 2 + k) * 2 * BY, 8)
            res[pl.ds(to, BY), :] = jnp.where(mask, even[k], new[k])
            res[pl.ds(to + BY, BY), :] = jnp.where(mask, new[k], even[k])

    copies = []
    for g in range(X1 // 4):
        last(2 + 4 * g)
        part = pl.ds(g * 8 * BY, 8 * BY)
        copies.append(pltpu.make_async_copy(res.at[part], result.at[part], sems.at[g]))
        copies[-1].start()
    for copy in copies:
        copy.wait()


def swap(pair, axis):
    count = lax.axis_size(axis)
    got = [None, None]
    for first in (1, 0):
        route = []
        for i in range(first, count - 1, 2):
            route += [(i, i + 1), (i + 1, i)]
        got[first] = lax.ppermute(pair[first], axis, route)
    return tuple(got)


def body(source, permittivity, screening, potential, fixed_cell):
    gx, gy = lax.axis_size("gx"), lax.axis_size("gy")
    args = [a.reshape(BX * BY, NL) for a in (potential, permittivity, source, screening, fixed_cell)]
    args = [pltpu.with_memory_space_constraint(a, pltpu.HBM) for a in args]

    whole = (sds(BX * BY, NL),) * 4 + (jax.ShapeDtypeStruct((BX * BY, NL), jnp.int32),)
    *args, p2, y0, y1, xm0, xm1 = call(
        pack_y,
        whole + (sds(8, NL),) + (sds(YROWS + 8, NL),) * 2 + (sds(12 * BY, NL),) * 2,
        [pltpu.SemaphoreType.DMA((5,)), pltpu.VMEM((BX // 4 * BY, NL), F32), pltpu.VMEM((8, NL), F32)],
        hbm=5,
    )(*args)
    y0 = (y0, y1)
    y0 = swap(y0, "gy")
    xm = swap((xm0, xm1), "gx")
    *halos, x0, x1 = call(pack_x, (sds(BX * 8, NL),) * 5 + (sds(XROWS + 24, NL),) * 2)(p2, *y0)
    gotx = swap((x0, x1), "gx")

    ext, one = (2, NF, YE, NL), (NF, YE, NL)
    fields = (sds(*ext),) * 3 + (sds(*one),) + (sds(*ext),) * 8
    fields += (sds(X1 * BY, NL),) * 2 + (sds((X1 + 2) * YE, NL), sds(X1 + 2, 8, NL))
    state = call(fine_own, fields)(*args, *halos)
    fine = call(
        fine_pre,
        fields + (sds(X1 // 2, 8, NL), sds(2, X1 // 2, 8, NL)) + (sds(YMSG, NL),) * 2 + (sds(XMAIN, NL),) * 2,
        alias={6 + k: k for k in range(STATE)},
    )(*y0, *xm, *gotx, *state)
    state, (c1, g1, m0, m1, *xm1) = (fine[0], *fine[2:12]), fine[STATE:]
    goty1 = swap((m0, m1), "gy")
    xm1 = swap(xm1, "gx")
    x1msg = call(pack_x1, (sds(XMSG, NL),) * 2)(*goty1, *gotx)
    gotx1 = swap(x1msg, "gx")

    mid, mid1 = (2, NM, YE, NL), (NM, YE, NL)
    fields1 = (sds(*mid),) * 4 + (sds(*mid1),) + (sds(*mid),) * 5
    level1 = call(mid_own, fields1)(m0, *goty1)
    *level1, message = call(
        mid_pre,
        fields1 + (sds(gx * gy, 16, NL),),
        [
            pltpu.VMEM((G1 // 2 * YE, NL), F32),
            pltpu.VMEM((X1 // 2 * 8, NL), F32),
            pltpu.VMEM((X1 // 2 * 8, NL), F32),
            pltpu.VMEM((3, G1 // 2, NL), F32),
            pltpu.VMEM((24, NL), F32),
        ],
        alias={6 + k: k for k in range(MIDS)},
    )(*xm1, *gotx1, c1, g1, *level1)
    level1 = (*level1[:3], *level1[4:])

    gathered = lax.all_to_all(message, ("gx", "gy"), 0, 0).reshape(gx, gy, 16, NL)
    wx, wy = min(gx, 6), min(gy, 8)
    if (wx, wy) != (gx, gy):
        first = (*window(gx, gy, wx, wy)[:2], 0, 0)
        gathered = lax.dynamic_slice(gathered, first, (wx, wy, 16, NL))

    inputs = (gathered, p2, *y0, *gotx, *level1, *state, *goty1, *xm1, *gotx1)
    result = pl.pallas_call(
        finish_kernel(len(inputs), (gx, gy, wx, wy)),
        out_shape=sds(BX * BY, NL),
        scratch_shapes=[
            pltpu.VMEM((2, wy + 2, wx * 4, NL), F32),
            pltpu.VMEM((2, wy + 2, wx * 4, NL), F32),
            pltpu.VMEM((2, wy, wx * 4, NL), F32),
            pltpu.VMEM((2, wy, wx * 4, NL), F32),
            pltpu.VMEM((2, 6, wy, wx * 4, NL), F32),
            pltpu.VMEM((wy + 6, wx + 4, 8, NL), F32),
            pltpu.VMEM((NF * YE, NL), F32),
            pltpu.VMEM(mid, F32),
            pltpu.VMEM(ext, F32),
            pltpu.VMEM((BX // 2 * 8, NL), F32),
            pltpu.VMEM((BX * BY, NL), F32),
            pltpu.SemaphoreType.DMA((X1 // 4,)),
        ],
        out_specs=pl.BlockSpec(memory_space=pltpu.HBM),
        compiler_params=pltpu.CompilerParams(vmem_limit_bytes=24 << 20),
        name="finish",
    )(*inputs)
    return result.reshape(BX, BY, NL)


def window(gx, gy, wx, wy):
    ix, iy = lax.axis_index("gx"), lax.axis_index("gy")
    fx = jnp.clip(ix - 2, 0, gx - wx)
    fy = jnp.clip(iy - 3, 0, gy - wy)
    return fx, fy, ix - fx, iy - fy


def finish_kernel(count, sizes):
    def kernel(*refs):
        ins, result, scratch = list(refs[:count]), refs[count], list(refs[1 + count :])
        finish(window(*sizes)[2:], *ins, result, *scratch)

    return kernel


def solution(mesh):
    placed = (P("gx", "gy", None),) * 5

    return jax.shard_map(body, mesh=mesh, in_specs=placed, out_specs=P("gx", "gy", None), check_vma=False)
```

```python
import jax
import jax.numpy as jnp
from jax import lax
from jax.experimental import pallas as pl
from jax.experimental.pallas import tpu as pltpu
from jax.sharding import PartitionSpec as P

F32 = jnp.float32
BX, BY, NL = 32, 16, 128
YE = 24
X1 = BX // 2
H1 = 8
G1 = X1 + 2 * H1
NF = X1 + 4
NM = G1 // 2 + 2
STATE = 16
GF = 3
LN2 = 0.6931471805599453


def rot(value, shift, axis):
    return pltpu.roll(value, shift % value.shape[axis], axis)


def iota(shape, axis):
    return lax.broadcasted_iota(jnp.int32, shape, axis)


def sds(*shape):
    return jax.ShapeDtypeStruct(shape, F32)


def by_parity(axis, action):
    odd = lax.axis_index(axis) % 2

    @pl.when(odd == 0)
    def _():
        action(0, 1)

    @pl.when(odd == 1)
    def _():
        action(1, 0)


def call(kernel, out_shape, scratch=(), vmem=24, hbm=0, alias=None):
    specs = {"in_specs": [pl.BlockSpec(memory_space=pltpu.HBM)] * hbm} if hbm else {}
    return pl.pallas_call(
        kernel,
        out_shape=out_shape,
        **specs,
        input_output_aliases=alias or {},
        scratch_shapes=list(scratch),
        compiler_params=pltpu.CompilerParams(vmem_limit_bytes=vmem << 20),
    )


YROWS = 10 * BX
XROWS = 12 * 8
FIELDS = (3, 3, 2, 2, 2)


def split_rows(ref, at):
    one, two = ref[pl.ds(at, 4, stride=2), :], ref[pl.ds(at + 1, 4, stride=2), :]
    lane = iota((4, NL), 1)
    even = (lane % 4 + lane // 4) % 2 == 0
    return jnp.concatenate([jnp.where(even, one, two), jnp.where(even, two, one)], axis=0)


def pack_y(hpot, hper, hsrc, hscr, hfix, pot, per, src, scr, fix, p2, out0, out1, xm0, xm1, sems, t, pk):
    outs, mains = (out0, out1), (xm0, xm1)
    pairs = ((hpot, pot), (hper, per), (hsrc, src), (hscr, scr), (hfix, fix))
    copies = [pltpu.make_async_copy(a, b, sems.at[k]) for k, (a, b) in enumerate(pairs)]
    for k in (1, 0, 2, 3, 4):
        copies[k].start()
    copies[1].wait()
    zlane = iota((BX // 2, NL), 1)

    def free_of(value):
        return jnp.where(value == 0, F32(1.0), F32(0.0))

    def row(ref, r):
        return ref[pl.ds(r, BX, stride=BY), :]

    def half(ref, r, parity):
        even = ref[pl.ds(r, BX // 2, stride=2 * BY), :]
        odd = ref[pl.ds(BY + r, BX // 2, stride=2 * BY), :]
        return jnp.where((r + zlane) % 2 == parity, even, odd)

    def side(out, r1, r2, r3):
        rows = [
            row(pot, r1), row(per, r1), row(src, r1), row(scr, r1), free_of(row(fix, r1)),
            row(pot, r2), row(per, r2), free_of(row(fix, r2)),
        ]
        for k, value in enumerate(rows):
            out[BX * k : BX * (k + 1), :] = value
        base = BX * len(rows)
        for k, value in enumerate([half(pot, r3, 1), half(per, r3, 1), half(src, r2, 0), half(scr, r2, 0)]):
            out[base + k * BX // 2 : base + (k + 1) * BX // 2, :] = value

    v = per[...].reshape(BX // 4, 4, BY, NL)
    v = (v[:, 0] + v[:, 1]) + (v[:, 2] + v[:, 3])
    t[...] = lane_pairs(lane_pairs(v, 1), 2).reshape(BX // 4 * BY, NL)
    n2 = BX // 4
    lane = iota((n2, NL), 1)
    total = None
    for j in range(4):
        r = [t[pl.ds(4 * j + k, n2, stride=BY), :] for k in range(4)]
        value = (r[0] + r[1]) + (r[2] + r[3])
        total = value if total is None else jnp.where(lane % 4 == j, value, total)
    pk[...] = F32(1.0 / 64) * total
    p2[...] = split_rows(pk, 0)
    for k in (0, 2, 3, 4):
        copies[k].wait()

    def action(hi, lo):
        side(outs[hi], BY - 1, BY - 2, BY - 3)
        side(outs[lo], 0, 1, 2)
        for out in outs:
            out[YROWS : YROWS + 8, :] = p2[...]

    by_parity("gy", action)

    def slab(out, planes):
        k = 0
        for ref, depth in zip((pot, per, src, scr, fix), FIELDS, strict=True):
            for x in planes[:depth]:
                value = ref[BY * x : BY * (x + 1), :]
                out[BY * k : BY * (k + 1), :] = free_of(value) if ref is fix else value
                k += 1

    def action_x(hi, lo):
        slab(mains[hi], (BX - 1, BX - 2, BX - 3))
        slab(mains[lo], (0, 1, 2))

    by_parity("gx", action_x)


def pack_x(p2, got0, got1, hpot, hper, hsrc, hscr, hfree, out0, out1):
    gots, outs = (got0, got1), (out0, out1)
    halos = (hpot, hper, hsrc, hscr, hfree)
    for h in halos:
        h[...] = jnp.zeros_like(h)

    def place(got, slots):
        def whole(ref, k, slot):
            ref[pl.ds(slot, BX, stride=8), :] = got[BX * k : BX * (k + 1), :]

        def halved(ref, k, slot):
            value = got[BX * 8 + k * BX // 2 : BX * 8 + (k + 1) * BX // 2, :]
            ref[pl.ds(slot, BX // 2, stride=16), :] = value
            ref[pl.ds(8 + slot, BX // 2, stride=16), :] = value

        s1, s2, s3 = slots
        for k, ref in enumerate(halos):
            whole(ref, k, s1)
        whole(hpot, 5, s2)
        whole(hper, 6, s2)
        whole(hfree, 7, s2)
        halved(hpot, 0, s3)
        halved(hper, 1, s3)
        halved(hsrc, 2, s2)
        halved(hscr, 3, s2)

    def action_y(hi, lo):
        place(gots[hi], (0, 1, 2))
        place(gots[lo], (7, 6, 5))

    by_parity("gy", action_y)

    def slab(out, planes):
        k = 0
        for h, depth in zip(halos, FIELDS, strict=True):
            for x in planes[:depth]:
                out[8 * k : 8 * (k + 1), :] = h[8 * x : 8 * (x + 1), :]
                k += 1

    def action_p(hi, lo):
        for out in outs:
            out[XROWS : XROWS + 8, :] = p2[...]
            out[XROWS + 8 : XROWS + 16, :] = gots[hi][YROWS : YROWS + 8, :]
            out[XROWS + 16 : XROWS + 24, :] = gots[lo][YROWS : YROWS + 8, :]

    by_parity("gy", action_p)

    def action_x(hi, lo):
        slab(outs[hi], (BX - 1, BX - 2, BX - 3))
        slab(outs[lo], (0, 1, 2))

    by_parity("gx", action_x)


def nonlinear(u, scr):
    up = jnp.exp(u - F32(LN2))
    down = jnp.exp(-u - F32(LN2))
    return scr * (up - down), scr * (up + down)


def colour_mask(n, zstep):
    shape = (n, YE, NL)
    return (iota(shape, 1) + iota(shape, 2) // zstep) % 2 == 0


def beside_of(other, colour, faces, at, n, zstep):
    fin, fout, fyp, fym, fzp, fzm = faces
    here = pl.ds(at, n)
    v = other[1 - colour, pl.ds(at - 1, n + 2)]
    mid = v[1 : n + 1]
    first = colour_mask(n, zstep)
    across = jnp.where(first, v[:n], v[2:]) if colour == 0 else jnp.where(first, v[2:], v[:n])
    return (
        (fin[here] * mid + fout[colour, here] * across)
        + (fyp[colour, here] * rot(mid, -1, 1) + fym[colour, here] * rot(mid, 1, 1))
        + (fzp[colour, here] * rot(mid, -zstep, 2) + fzm[colour, here] * rot(mid, zstep, 2))
    )


def pairs_of(u, at, n, colour, refs):
    c, fin, fout, fyp, fym, fzp, fzm, src, scr, _ = refs
    here = pl.ds(at, n)
    plane = u[colour, here]
    sh, ch = nonlinear(plane, scr[colour, here])
    centre = c[colour, here]
    beside = beside_of(u, colour, (fin, fout, fyp, fym, fzp, fzm), at, n, 1)
    return plane, centre * plane - beside + sh - src[colour, here], centre, ch


def fine_new(u, at, n, colour, refs):
    plane, value, centre, ch = pairs_of(u, at, n, colour, refs)
    return jnp.where(refs[-1][colour, pl.ds(at, n)] > 0.5, plane - value / (centre + ch), plane)


def fine_half(u, at, n, colour, refs):
    u[colour, pl.ds(at, n)] = fine_new(u, at, n, colour, refs)


def groups(first, count, n, step):
    assert count % n == 0

    def one(g, _):
        step(first + g * n)
        return 0

    lax.fori_loop(0, count // n, one, 0, unroll=True)


def faces_of(p, at, n, scale, zstep, fin, fout, fyp, fym, fzp, fzm):
    here = pl.ds(at, n)
    lane = iota((n, YE, NL), 2)
    first = colour_mask(n, zstep)
    half = F32(0.5 * scale)
    for colour in (0, 1):
        plane = p[colour, here]
        v = p[1 - colour, pl.ds(at - 1, n + 2)]
        mid = v[1 : n + 1]
        across = jnp.where(first, v[:n], v[2:]) if colour == 0 else jnp.where(first, v[2:], v[:n])
        if colour == 0:
            fin[here] = half * (plane + mid)
        fout[colour, here] = half * (plane + across)
        fyp[colour, here] = half * (plane + rot(mid, -1, 1))
        fym[colour, here] = half * (plane + rot(mid, 1, 1))
        fzp[colour, here] = jnp.where(lane >= NL - zstep, F32(0.0), half * (plane + rot(mid, -zstep, 2)))
        fzm[colour, here] = jnp.where(lane < zstep, F32(0.0), half * (plane + rot(mid, zstep, 2)))


def lane_pairs(value, step):
    lane = iota(value.shape, value.ndim - 1)
    return value + jnp.where((lane // step) % 2 == 0, rot(value, -step, value.ndim - 1), rot(value, step, value.ndim - 1))


def fine_begin(state, at, n):
    u, ep, c, fin, fout, fyp, fym, fzp, fzm, esrc, escr, efree = state[:12]
    faces_of(ep, at, n, 1.0, 1, fin, fout, fyp, fym, fzp, fzm)
    here = pl.ds(at, n)
    lane = iota((n, YE, NL), 2)
    for colour in (0, 1):
        ends = jnp.where((lane == 0) | (lane == NL - 1), F32(0.5) * ep[colour, here], F32(0.0))
        c[colour, here] = (
            (fin[here] + fout[colour, here]) + (fyp[colour, here] + fym[colour, here])
            + (fzp[colour, here] + fzm[colour, here]) + ends
        )
    fine_half(u, at, n, 0, (c, fin, fout, fyp, fym, fzp, fzm, esrc, escr, efree))


def fine_own(pot, per, src, scr, fix, hpot, hper, hsrc, hscr, hfree, *state):
    u, ep, c, fin, fout, fyp, fym, fzp, fzm, esrc, escr, efree = state[:12]
    first = colour_mask(1, 1)[0]

    def own(k, _):
        for ref, h, ext in ((pot, hpot, u), (per, hper, ep), (src, hsrc, esrc), (scr, hscr, escr), (fix, hfree, efree)):
            value = ref[pl.ds(pl.multiple_of(2 * k * BY, 8), 2 * BY), :]
            if ref is fix:
                value = jnp.where(value == 0, F32(1.0), F32(0.0))
            halo = h[pl.ds(pl.multiple_of(16 * k, 8), 16), :]
            for rows, one, two in (
                (slice(0, BY), value[:BY], value[BY:]),
                (slice(BY, YE), halo[:8], halo[8:]),
            ):
                ext[0, k + 2, rows, :] = jnp.where(first[rows], one, two)
                ext[1, k + 2, rows, :] = jnp.where(first[rows], two, one)
        return 0

    lax.fori_loop(0, X1, own, 0, unroll=4)
    groups(3, X1 - 2, 2, lambda at: fine_begin(state, at, 2))
    refs = (c, fin, fout, fyp, fym, fzp, fzm, esrc, escr, efree)
    groups(4, X1 - 4, 3, lambda at: fine_half(u, at, 3, 1, refs))
    groups(6, X1 - 8, 4, lambda at: fine_down(state, at, 4))
    for k in range(1, X1 + 1):
        fine_coarse_p(state, k)


def fine_down(state, at, n):
    u, _, c, fin, fout, fyp, fym, fzp, fzm, esrc, escr, efree, tr, tc = state[:14]
    refs = (c, fin, fout, fyp, fym, fzp, fzm, esrc, escr, efree)
    left, react = F32(0.0), F32(0.0)
    for colour in (0, 1):
        _, value, _, ch = pairs_of(u, at, n, colour, refs)
        left += jnp.where(efree[colour, pl.ds(at, n)] > 0.5, -value, F32(0.0))
        react += ch
    to = pl.multiple_of((at - 2) * BY, 8)
    tr[pl.ds(to, n * BY), :] = lane_pairs(left[:, 0:BY], 1).reshape(n * BY, NL)
    tc[pl.ds(to, n * BY), :] = lane_pairs(react[:, 0:BY], 1).reshape(n * BY, NL)


def fine_coarse_p(state, k):
    ep, tp, p1 = state[1], state[14], state[15]
    at = k * YE
    tp[at : at + YE, :] = lane_pairs(ep[0, k + 1] + ep[1, k + 1], 1)
    p1[k] = F32(0.125) * (tp[pl.ds(at, 8, stride=2), :] + tp[pl.ds(at + 1, 8, stride=2), :])


def fine_pre(goty0, goty1, xm0, xm1, got0, got1, *refs_):
    state, refs_ = refs_[STATE : 2 * STATE], refs_[2 * STATE :]
    u, ep, c, fin, fout, fyp, fym, fzp, fzm, esrc, escr, efree, tr, tc, tp, p1 = state
    csum, g1, m0, m1, n0, n1 = refs_
    gots, mains, outs, nexts = (got0, got1), (xm0, xm1), (m0, m1), (n0, n1)
    first = colour_mask(1, 1)[0]

    def place(main, got, near, far, flip):
        k = 0
        for ext, depth in zip((u, ep, esrc, escr, efree), FIELDS, strict=True):
            planes = []
            for _ in range(depth):
                rows = main[BY * k : BY * (k + 1), :]
                planes.append(jnp.concatenate([rows, got[8 * k : 8 * (k + 1), :]], axis=0))
                k += 1
            one, two = (planes[1], planes[0]) if flip else (planes[0], planes[1])
            ext[0, near] = jnp.where(first, one, two)
            ext[1, near] = jnp.where(first, two, one)
            third = planes[2] if depth == 3 else jnp.zeros((YE, NL), F32)
            ext[0, far] = third
            ext[1, far] = third

    def action_x(hi, lo):
        place(mains[hi], gots[hi], X1 + 2, X1 + 3, False)
        place(mains[lo], gots[lo], 1, 0, True)

    by_parity("gx", action_x)
    refs = (c, fin, fout, fyp, fym, fzp, fzm, esrc, escr, efree)

    for at in (1, X1 + 1):
        fine_begin(state, at, 2)
    for at in (1, X1):
        fine_half(u, at, 3, 1, refs)
    for at in (2, X1 - 2):
        fine_down(state, at, 4)
    for k in (0, X1 + 1):
        fine_coarse_p(state, k)

    eighth = F32(0.125)
    sub = iota((8, NL), 0)
    lane = iota((8, NL), 1)

    first8 = (sub + lane // 2) % 2 == 0

    def coarse(x1):
        k = x1 + 1
        p = p1[k]
        base = k * YE
        high = eighth * (tp[pl.ds(base + 2, 8, stride=2), :] + tp[pl.ds(base + 3, 8, stride=2), :])
        edge = tp[pl.ds(pl.multiple_of(base + 16, 8), 8), :]
        edge = eighth * (edge + rot(edge, 1, 0))
        low = jnp.where(sub == 0, rot(edge, 1, 0), rot(p, 1, 0))
        front = jnp.where(lane >= NL - 2, F32(0.0), rot(p, -2, 1))
        back = jnp.where(lane < 2, F32(0.0), rot(p, 2, 1))
        near = (p1[k + 1] + p1[k - 1]) + (high + low) + (front + back)
        centre = F32(3.0) * p + F32(0.5) * near
        at = x1 * BY
        r = eighth * (tr[pl.ds(at, 8, stride=2), :] + tr[pl.ds(at + 1, 8, stride=2), :])
        react = eighth * (tc[pl.ds(at, 8, stride=2), :] + tc[pl.ds(at + 1, 8, stride=2), :])
        diag = F32(0.25) * centre + react
        message = jnp.where(lane % 2 == 0, r, F32(1.0) / diag)
        m0[pl.ds(pl.multiple_of(x1 * 8, 8), 8), :] = message
        m1[pl.ds(pl.multiple_of(x1 * 8, 8), 8), :] = message
        return diag, react

    def make(k, _):
        diag0, react0 = coarse(2 * k)
        diag1, react1 = coarse(2 * k + 1)
        csum[k] = react0 + react1
        g1[0, k] = jnp.where(first8, diag0, diag1)
        g1[1, k] = jnp.where(first8, diag1, diag0)
        return 0

    lax.fori_loop(0, X1 // 2, make, 0, unroll=4)

    for a in range(X1 // 2):
        message = jnp.where(lane % 2 == 0, p1[1 + 2 * a], p1[2 + 2 * a])
        for m in outs:
            m[X1 * 8 + 8 * a : X1 * 8 + 8 * a + 8, :] = message

    base = X1 * 8 + X1 * 4

    def odd_row(out, y):
        out[base : base + X1, :] = u[1, pl.ds(2, X1), y, :]

    def slab(out, at, x):
        out[0 : H1 * 8, :] = m0[8 * at : 8 * (at + H1), :]
        row = X1 * 8 + 4 * at
        out[H1 * 8 : H1 * 12, :] = m0[row : row + H1 * 4, :]
        out[XOWN:XMAIN, :] = u[1, x, 0:BY, :]

    def action_next(hi, lo):
        slab(nexts[hi], X1 - H1, X1 + 1)
        slab(nexts[lo], 0, 2)

    by_parity("gx", action_next)

    def action_y(hi, lo):
        odd_row(outs[hi], BY - 2)
        odd_row(outs[lo], 1)
        outs[hi][base + X1 : base + X1 + 8, :] = (goty0, goty1)[lo][YROWS : YROWS + 8, :]
        outs[lo][base + X1 : base + X1 + 8, :] = (goty0, goty1)[hi][YROWS : YROWS + 8, :]

    by_parity("gy", action_y)


def halo_rows(dx):
    return (16 * (dx - 1), 2) if dx < 5 else (64 + 8 * (dx - 5), 1)


def halo_pair(t):
    return (96 + 16 * t, 2) if t < 2 else (128 + 8 * (t - 2), 1)


P2AT = 144
YMSG = X1 * 8 + X1 * 4 + BX // 2 + 8
XOWN = H1 * 8 + (H1 // 2) * 8
XMAIN = XOWN + BY
XMSG = P2AT + 40


def pack_x1(got0, got1, fx0, fx1, out0, out1):
    gots, outs, fines = (got0, got1), (out0, out1), (fx0, fx1)
    odd_y = lax.axis_index("gy") % 2
    upper = iota((8, NL), 0) < 4

    def go(hi, lo):
        def put(out, at, count, row):
            above, below = gots[hi][row : row + 8, :], gots[lo][row : row + 8, :]
            if count == 2:
                out[at : at + 8, :] = above
                out[at + 8 : at + 16, :] = below
            else:
                out[at : at + 8, :] = jnp.where(upper, above, below)

        def slab(out, near, step, behind):
            for dx in range(1, H1 + 1):
                put(out, *halo_rows(dx), 8 * (near + step * (dx - 1)))
            for t in range(H1 // 2):
                put(out, *halo_pair(t), X1 * 8 + 8 * (near // 2 + step * t))
            out[P2AT : P2AT + 8, :] = gots[hi][YMSG - 8 : YMSG, :]
            out[P2AT + 8 : P2AT + 16, :] = gots[lo][YMSG - 8 : YMSG, :]
            out[P2AT + 16 : P2AT + 40, :] = behind[XROWS : XROWS + 24, :]

        def action(xhi, xlo):
            slab(outs[xhi], X1 - 1, -1, fines[xlo])
            slab(outs[xlo], 0, 1, fines[xhi])

        by_parity("gx", action)

    @pl.when(odd_y == 0)
    def _():
        go(0, 1)

    @pl.when(odd_y == 1)
    def _():
        go(1, 0)


def coarse_half(e, r, d, at, n, colour, faces, zstep):
    here = pl.ds(at, n)
    e[colour, here] = (r[colour, here] + beside_of(e, colour, faces, at, n, zstep)) * d[colour, here]


def dup_even(value):
    lane = iota(value.shape, value.ndim - 1)
    return jnp.where(lane % 2 == 0, value, rot(value, 1, value.ndim - 1))


def dup_odd(value):
    lane = iota(value.shape, value.ndim - 1)
    return jnp.where(lane % 2 == 1, value, rot(value, -1, value.ndim - 1))


MIDS = 12


def mid_put(state, k, rows, one, two, both):
    _, r, d, p = state[:4]
    mask = colour_mask(1, 2)[0][rows]
    for colour in (0, 1):
        a, b = (one, two) if colour == 0 else (two, one)
        value = jnp.where(mask, a, b)
        r[colour, k, rows, :] = dup_even(value)
        d[colour, k, rows, :] = dup_odd(value)
    a, b = dup_even(both), dup_odd(both)
    p[0, k, rows, :] = jnp.where(mask, a, b)
    p[1, k, rows, :] = jnp.where(mask, b, a)


def mid_begin(state, at, n):
    e, r, d, p, *faces = state[:10]
    here = pl.ds(at, n)
    faces_of(p, at, n, 0.25, 2, *faces)
    e[0, here] = r[0, here] * d[0, here]


def mid_own(m0, gy0, gy1, csum, *state):
    gys = (gy0, gy1)
    e, r, d, p, *faces, t, tc = state

    def own(hi, lo):
        for k in range(X1 // 2):
            for j, ref in enumerate((m0, gys[hi], gys[lo])):
                two = ref[16 * k : 16 * k + 16, :]
                both = ref[X1 * 8 + 8 * k : X1 * 8 + 8 * k + 8, :]
                mid_put(state, 1 + H1 // 2 + k, slice(8 * j, 8 * j + 8), two[:8], two[8:], both)

    by_parity("gy", own)
    first = 2 + H1 // 2
    groups(first, X1 // 2 - 2, 2, lambda at: mid_begin(state, at, 2))
    groups(first + 1, X1 // 2 - 4, 2, lambda at: coarse_half(e, r, d, at, 2, 1, faces, 2))
    for x2 in range(H1 // 2, H1 // 2 + X1 // 2):
        mid_coarse_p(p, t, x2)
    tc[...] = lane_pairs(csum[...], 2).reshape(X1 // 2 * 8, NL)


def mid_coarse_p(p, t, x2):
    t[x2 * YE : (x2 + 1) * YE, :] = lane_pairs(p[0, x2 + 1] + p[1, x2 + 1], 2)


def mid_pre(xm0, xm1, gx0, gx1, csum, g1, *refs_):
    gxs, mains = (gx0, gx1), (xm0, xm1)
    state, refs_ = refs_[MIDS : 2 * MIDS], refs_[2 * MIDS :]
    e, r, d, p, *faces, t, tc = state
    msg, tr, pc, pk = refs_

    def beyond(main, ref, at, far):
        def whole(row, start, count):
            own_rows = main[row : row + 8, :]
            above = ref[start : start + 8, :]
            below = ref[start + 8 : start + 16, :] if count == 2 else above
            return jnp.concatenate([own_rows, above, below], axis=0)

        for k in range(H1 // 2):
            one, two = (whole(8 * a, *halo_rows(H1 - a if far else a + 1)) for a in (2 * k, 2 * k + 1))
            both = whole(H1 * 8 + 8 * k, *halo_pair(H1 // 2 - 1 - k if far else k))
            mid_put(state, at + k, slice(0, YE), one, two, both)

    def action(hi, lo):
        beyond(mains[hi], gxs[hi], 1 + H1 // 2 + X1 // 2, False)
        beyond(mains[lo], gxs[lo], 1, True)

    by_parity("gx", action)
    for ref in (p, e):
        for colour in (0, 1):
            ref[colour, 0] = jnp.zeros((YE, NL), F32)
            ref[colour, NM - 1] = jnp.zeros((YE, NL), F32)
    inner = 1 + H1 // 2
    for at in (*range(1, inner + 1), *range(inner + X1 // 2 - 1, NM - 1)):
        mid_begin(state, at, 1)
    for at in (1, inner + X1 // 2 - 2):
        coarse_half(e, r, d, at, inner + 1, 1, faces, 2)
    for colour in (0, 1):
        groups(2, NM - 4, 7, lambda at, colour=colour: coarse_half(e, r, d, at, 7, colour, faces, 2))

    def down(at):
        n = 4
        here = pl.ds(at, n)
        k = pl.ds(at - 1 - H1 // 2, n)
        left = F32(0.0)
        for colour in (0, 1):
            part = r[colour, here] + beside_of(e, colour, faces, at, n, 2)
            left += part[:, 0:8] - g1[colour, k] * e[colour, here, 0:8, :]
        to = pl.multiple_of((at - 1 - H1 // 2) * 8, 8)
        tr[pl.ds(to, n * 8), :] = lane_pairs(left, 2).reshape(n * 8, NL)

    groups(1 + H1 // 2, X1 // 2, 4, down)

    for x2 in (*range(H1 // 2), *range(H1 // 2 + X1 // 2, G1 // 2)):
        mid_coarse_p(p, t, x2)

    eighth = F32(0.125)
    n2, m2 = X1 // 2, G1 // 2

    def compact(ref, first, rows, stride):
        lane = iota((rows, NL), 1)
        out = None
        for j in range(4):
            value = ref[pl.ds(first + 2 * j, rows, stride=stride), :] + ref[pl.ds(first + 2 * j + 1, rows, stride=stride), :]
            out = value if out is None else jnp.where(lane % 4 == j, value, out)
        return eighth * out

    r2 = compact(tr, 0, n2, 8)
    react2 = compact(tc, 0, n2, 8)
    for k in range(3):
        pc[k] = compact(t, 8 * k, m2, YE)
    h2 = H1 // 2
    centre_p = pc[0, h2 : h2 + n2, :]
    j4 = iota((n2, NL), 1) % 4
    lane = iota((n2, NL), 1)
    high = jnp.where(j4 < 3, rot(centre_p, -1, 1), rot(pc[1, h2 : h2 + n2, :], 3, 1))
    low = jnp.where(j4 > 0, rot(centre_p, 1, 1), rot(pc[2, h2 : h2 + n2, :], -3, 1))
    front = jnp.where(lane >= NL - 4, F32(0.0), rot(centre_p, -4, 1))
    back = jnp.where(lane < 4, F32(0.0), rot(centre_p, 4, 1))
    near = (pc[0, h2 + 1 : h2 + 1 + n2, :] + pc[0, h2 - 1 : h2 - 1 + n2, :]) + (high + low) + (front + back)
    diag2 = F32(0.0625) * (F32(3.0) * centre_p + F32(0.5) * near) + react2
    for k, value in enumerate((r2, F32(1.0) / diag2, centre_p)):
        pk[8 * k : 8 * k + 8, :] = value
    r2, inverse2, own_p = (split_rows(pk, 8 * k) for k in range(3))
    near_rows = iota((8, NL), 1) % 4 >= 2
    ahead = jnp.where(near_rows, r2, rot(own_p, -2, 1))
    behind = jnp.where(near_rows, rot(own_p, 2, 1), r2)
    count = lax.axis_size("gy")
    place = lax.axis_index("gy")

    def every(k, _):
        step = k % count - place
        msg[k, 0:8, :] = jnp.where(step == 3, ahead, jnp.where(step == -3, behind, r2))
        msg[k, 8:16, :] = inverse2
        return 0

    lax.fori_loop(0, msg.shape[0], every, 0, unroll=8)


def finish(at, got, p2own, yf0, yf1, xf0, xf1, e, r, d, fin1, fout1, fyp1, fym1, fzp1, fzm1,
           before, c, fin, fout, fyp, fym, fzp, fzm, src, scr, free, gy0, gy1, xm0, xm1, gx0, gx1,
           result,
           e2, p2, r2, d2, k2, blk, tx, eu, u, hal, res, sems):
    wx, wy = got.shape[0], got.shape[1]
    rows = wx * 4
    ox, oy = at
    blk[...] = jnp.zeros_like(blk)
    for b in (0, wy + 1):
        for colour in (0, 1):
            e2[colour, b] = jnp.zeros((rows, NL), F32)

    def keep(da, db, ref, first):
        blk[oy + db + 3, ox + da + 2] = ref[first : first + 8, :]

    keep(0, 0, p2own, 0)

    def blocks_y(hi, lo):
        for db, k in ((1, hi), (-1, lo)):
            keep(0, db, (yf0, yf1)[k], YROWS)
            keep(0, 2 * db, (gy0, gy1)[k], YMSG - 8)

    by_parity("gy", blocks_y)

    def blocks_x(hi, lo):
        for da, k in ((1, hi), (-1, lo)):
            fine, mid = (xf0, xf1)[k], (gx0, gx1)[k]
            for n, db in enumerate((0, 1, -1)):
                keep(da, db, fine, XROWS + 8 * n)
                keep(2 * da, db, mid, P2AT + 16 + 8 * n)
            keep(da, 2, mid, P2AT)
            keep(da, -2, mid, P2AT + 8)

    by_parity("gx", blocks_x)
    l4 = iota((8, NL), 1) % 4
    for db in (3, -3):

        @pl.when((oy + db >= 0) & (oy + db < wy))
        def _(db=db):
            for a in range(wx):
                value = got[a, oy + db, 0:8, :]
                value = jnp.where(l4 < 2, rot(value, -2, 1), F32(0.0)) if db > 0 else jnp.where(l4 >= 2, rot(value, 2, 1), F32(0.0))
                blk[oy + db + 3, a + 2] = value

    def spread(b, _):
        for a in range(wx):
            for colour in (0, 1):
                own, to = slice(4 * colour, 4 * colour + 4), slice(4 * a, 4 * a + 4)
                r2[colour, b, to, :] = got[a, b, own, :]
                d2[colour, b, to, :] = got[a, b, 8 + 4 * colour : 12 + 4 * colour, :]
                p2[colour, b + 1, to, :] = blk[b + 3, a + 2, own, :]
        return 0

    lax.fori_loop(0, wy, spread, 0, unroll=4)
    for b in (0, wy + 1):
        for colour in (0, 1):
            p2[colour, b] = jnp.zeros((rows, NL), F32)
    shape = (wy, rows, NL)
    sub, lane = iota(shape, 1), iota(shape, 2)
    j4 = lane % 4
    even = (j4 + lane // 4) % 2 == 0

    def around(ref, colour, b, n):
        v = ref[1 - colour, pl.ds(b, n + 2)]
        mid = v[1 : n + 1]
        one, two = rot(mid, 1, 1), rot(mid, -1, 1)
        mask, j = even[:n], j4[:n]
        return (
            mid,
            jnp.where(mask, one, two) if colour == 0 else jnp.where(mask, two, one),
            jnp.where(j < 3, rot(mid, -1, 2), rot(v[2:], 3, 2)),
            jnp.where(j > 0, rot(mid, 1, 2), rot(v[:n], -3, 2)),
            rot(mid, -4, 2), rot(mid, 4, 2),
        )

    for colour in (0, 1):
        at_first = even if colour == 0 else ~even
        outside = (at_first & (sub == 0)) | (~at_first & (sub == rows - 1))
        edges = (None, outside, None, None, lane >= NL - 4, lane < 4)
        mine = p2[colour, 1 : wy + 1]
        for k, (value, edge) in enumerate(zip(around(p2, colour, 0, wy), edges, strict=True)):
            face = F32(0.03125) * (mine + value)
            k2[colour, k] = face if edge is None else jnp.where(edge, F32(0.0), face)
    e2[0, 1 : wy + 1] = r2[0] * d2[0]

    def half2(colour, b, n):
        here = pl.ds(b, n)
        total = r2[colour, here]
        for k, value in enumerate(around(e2, colour, b, n)):
            total = total + k2[colour, k, here] * value
        e2[colour, pl.ds(b + 1, n)] = total * d2[colour, here]

    half2(1, 0, wy)
    for reach, colours in ((2, (0, 1, 0, 1)), (1, (0, 1))):
        n = min(2 * reach + 1, wy)
        start_b = jnp.clip(oy - reach, 0, wy - n)
        for colour in colours:
            half2(colour, start_b, n)

    s8, l8 = iota((8, NL), 0), iota((8, NL), 1)
    even8 = (l8 % 4 + l8 // 4) % 2 == 0
    start = 4 * ox - 2
    inside = (s8 + start >= 0) & (s8 + start < rows)
    for k, step in enumerate((0, 1, -1)):
        near = []
        for colour in (0, 1):
            block = pltpu.roll(e2[colour, oy + step + 1], (rows - start) % rows, 0)[0:8]
            near.append(jnp.where(inside, block, F32(0.0)))
        planes = (jnp.where(even8, near[0], near[1]), jnp.where(even8, near[1], near[0]))
        for second in (0, 1):
            for j in range(4):
                value = jnp.where(l8 % 4 == 0, rot(planes[second], -j, 1), F32(0.0))
                value = value + rot(value, 1, 1)
                value = value + rot(value, 2, 1)
                for y in (0, 1):
                    tx[pl.ds(second * YE + 8 * k + 2 * j + y, 8, stride=2 * YE), :] = value

    def correct(x2, _):
        value = tx[pl.ds(pl.multiple_of(x2 * YE, 8), YE), :]
        for colour in (0, 1):
            eu[colour, x2 + 1] = e[colour, x2 + 1] + value
        return 0

    lax.fori_loop(0, G1 // 2, correct, 0, unroll=4)
    faces1 = (fin1, fout1, fyp1, fym1, fzp1, fzm1)
    for at1, count, n, colour in ((3, 12, 4, 0), (3, 12, 4, 1), (4, 10, 5, 0), (4, 10, 5, 1)):
        groups(at1, count, n, lambda at, n=n, colour=colour: coarse_half(eu, r, d, at, n, colour, faces1, 2))

    base = X1 * 8 + X1 * 4

    def action_y(hi, lo):
        hal[pl.ds(1, X1, stride=8), :] = (gy0, gy1)[hi][base : base + X1, :]
        hal[pl.ds(6, X1, stride=8), :] = (gy0, gy1)[lo][base : base + X1, :]

    by_parity("gy", action_y)
    first = colour_mask(1, 1)[0]
    first1 = colour_mask(1, 2)[0]
    added = (s8 == 1) | (s8 == 6)
    own_rows = slice(0, BY)

    def widen(k, plane, now1, halo1):
        for y in (0, 1):
            tx[pl.ds(k * YE + y, 8, stride=2), :] = plane[0:8]
        wide = tx[pl.ds(pl.multiple_of(k * YE, 8), BY), :]
        hi, lo = plane[8:16], plane[16:24]
        halo = jnp.where(s8 < 2, jnp.where(s8 == 0, hi, rot(hi, 1, 0)), jnp.where(s8 == 7, lo, rot(lo, -1, 0)))
        now = ((before[0, k, own_rows, :], before[0, k, BY:YE, :]), (now1, halo1))
        for colour in (0, 1):
            one, two = now[colour]
            u[colour, k, own_rows, :] = jnp.where(free[colour, k, own_rows, :] > 0.5, one + wide, one)
            u[colour, k, BY:YE, :] = jnp.where(free[colour, k, BY:YE, :] > 0.5, two + halo, two)

    def level1_plane(m, second):
        one, two = (eu[1, m], eu[0, m]) if second else (eu[0, m], eu[1, m])
        return jnp.where(first1, one, two)

    def add(m, _):
        for second in (0, 1):
            k = 2 * m + second + 2
            halo = jnp.where(added, hal[pl.ds(pl.multiple_of(8 * (k - 2), 8), 8), :], before[1, k, BY:YE, :])
            widen(k, level1_plane(m + 1 + H1 // 2, second), before[1, k, own_rows, :], halo)
        return 0

    lax.fori_loop(0, X1 // 2, add, 0, unroll=4)

    def action_x(hi, lo):
        row = (xm0, xm1)[hi][XOWN:XMAIN, :]
        k = X1 + 2
        now = jnp.where(first[own_rows], row, before[1, k, own_rows, :])
        widen(k, level1_plane(1 + H1 // 2 + X1 // 2, 0), now, before[1, k, BY:YE, :])
        row = (xm0, xm1)[lo][XOWN:XMAIN, :]
        now = jnp.where(first[own_rows], before[1, 1, own_rows, :], row)
        widen(1, level1_plane(H1 // 2, 1), now, before[1, 1, BY:YE, :])

    by_parity("gx", action_x)
    for k in (0, NF - 1):
        u[1, k] = before[1, k]
    refs = (c, fin, fout, fyp, fym, fzp, fzm, src, scr, free)
    groups(1, X1 + 2, GF, lambda at: fine_half(u, at, GF, 0, refs))

    def last(at):
        n = 4
        new = fine_new(u, at, n, 1, refs)[:, own_rows]
        even = u[0, pl.ds(at, n), own_rows, :]
        mask = first[own_rows]
        for k in range(n):
            to = pl.multiple_of((at - 2 + k) * 2 * BY, 8)
            res[pl.ds(to, BY), :] = jnp.where(mask, even[k], new[k])
            res[pl.ds(to + BY, BY), :] = jnp.where(mask, new[k], even[k])

    copies = []
    for g in range(X1 // 4):
        last(2 + 4 * g)
        part = pl.ds(g * 8 * BY, 8 * BY)
        copies.append(pltpu.make_async_copy(res.at[part], result.at[part], sems.at[g]))
        copies[-1].start()
    for copy in copies:
        copy.wait()


def swap(pair, axis):
    count = lax.axis_size(axis)
    got = [None, None]
    for first in (1, 0):
        route = []
        for i in range(first, count - 1, 2):
            route += [(i, i + 1), (i + 1, i)]
        got[first] = lax.ppermute(pair[first], axis, route)
    return tuple(got)


def body(source, permittivity, screening, potential, fixed_cell):
    gx, gy = lax.axis_size("gx"), lax.axis_size("gy")
    args = [a.reshape(BX * BY, NL) for a in (potential, permittivity, source, screening, fixed_cell)]
    args = [pltpu.with_memory_space_constraint(a, pltpu.HBM) for a in args]

    whole = (sds(BX * BY, NL),) * 4 + (jax.ShapeDtypeStruct((BX * BY, NL), jnp.int32),)
    *args, p2, y0, y1, xm0, xm1 = call(
        pack_y,
        whole + (sds(8, NL),) + (sds(YROWS + 8, NL),) * 2 + (sds(12 * BY, NL),) * 2,
        [pltpu.SemaphoreType.DMA((5,)), pltpu.VMEM((BX // 4 * BY, NL), F32), pltpu.VMEM((8, NL), F32)],
        hbm=5,
    )(*args)
    y0 = (y0, y1)
    y0 = swap(y0, "gy")
    xm = swap((xm0, xm1), "gx")
    *halos, x0, x1 = call(pack_x, (sds(BX * 8, NL),) * 5 + (sds(XROWS + 24, NL),) * 2)(p2, *y0)
    gotx = swap((x0, x1), "gx")

    ext, one = (2, NF, YE, NL), (NF, YE, NL)
    fields = (sds(*ext),) * 3 + (sds(*one),) + (sds(*ext),) * 8
    fields += (sds(X1 * BY, NL),) * 2 + (sds((X1 + 2) * YE, NL), sds(X1 + 2, 8, NL))
    state = call(fine_own, fields)(*args, *halos)
    fine = call(
        fine_pre,
        fields + (sds(X1 // 2, 8, NL), sds(2, X1 // 2, 8, NL)) + (sds(YMSG, NL),) * 2 + (sds(XMAIN, NL),) * 2,
        alias={6 + k: k for k in range(STATE)},
    )(*y0, *xm, *gotx, *state)
    state, (c1, g1, m0, m1, *xm1) = (fine[0], *fine[2:12]), fine[STATE:]
    goty1 = swap((m0, m1), "gy")
    xm1 = swap(xm1, "gx")
    x1msg = call(pack_x1, (sds(XMSG, NL),) * 2)(*goty1, *gotx)
    gotx1 = swap(x1msg, "gx")

    mid, mid1 = (2, NM, YE, NL), (NM, YE, NL)
    fields1 = (sds(*mid),) * 4 + (sds(*mid1),) + (sds(*mid),) * 5
    fields1 += (sds(G1 // 2 * YE, NL), sds(X1 // 2 * 8, NL))
    level1 = call(mid_own, fields1)(m0, *goty1, c1)
    *level1, message = call(
        mid_pre,
        fields1 + (sds(gx * gy, 16, NL),),
        [
            pltpu.VMEM((X1 // 2 * 8, NL), F32),
            pltpu.VMEM((3, G1 // 2, NL), F32),
            pltpu.VMEM((24, NL), F32),
        ],
        alias={6 + k: k for k in range(MIDS)},
    )(*xm1, *gotx1, c1, g1, *level1)
    level1 = (*level1[:3], *level1[4:10])

    gathered = lax.all_to_all(message, ("gx", "gy"), 0, 0).reshape(gx, gy, 16, NL)
    wx, wy = min(gx, 6), min(gy, 8)
    if (wx, wy) != (gx, gy):
        first = (*window(gx, gy, wx, wy)[:2], 0, 0)
        gathered = lax.dynamic_slice(gathered, first, (wx, wy, 16, NL))

    inputs = (gathered, p2, *y0, *gotx, *level1, *state, *goty1, *xm1, *gotx1)
    result = pl.pallas_call(
        finish_kernel(len(inputs), (gx, gy, wx, wy)),
        out_shape=sds(BX * BY, NL),
        scratch_shapes=[
            pltpu.VMEM((2, wy + 2, wx * 4, NL), F32),
            pltpu.VMEM((2, wy + 2, wx * 4, NL), F32),
            pltpu.VMEM((2, wy, wx * 4, NL), F32),
            pltpu.VMEM((2, wy, wx * 4, NL), F32),
            pltpu.VMEM((2, 6, wy, wx * 4, NL), F32),
            pltpu.VMEM((wy + 6, wx + 4, 8, NL), F32),
            pltpu.VMEM((NF * YE, NL), F32),
            pltpu.VMEM(mid, F32),
            pltpu.VMEM(ext, F32),
            pltpu.VMEM((BX // 2 * 8, NL), F32),
            pltpu.VMEM((BX * BY, NL), F32),
            pltpu.SemaphoreType.DMA((X1 // 4,)),
        ],
        out_specs=pl.BlockSpec(memory_space=pltpu.HBM),
        compiler_params=pltpu.CompilerParams(vmem_limit_bytes=24 << 20),
        name="finish",
    )(*inputs)
    return result.reshape(BX, BY, NL)


def window(gx, gy, wx, wy):
    ix, iy = lax.axis_index("gx"), lax.axis_index("gy")
    fx = jnp.clip(ix - 2, 0, gx - wx)
    fy = jnp.clip(iy - 3, 0, gy - wy)
    return fx, fy, ix - fx, iy - fy


def finish_kernel(count, sizes):
    def kernel(*refs):
        ins, result, scratch = list(refs[:count]), refs[count], list(refs[1 + count :])
        finish(window(*sizes)[2:], *ins, result, *scratch)

    return kernel


def solution(mesh):
    placed = (P("gx", "gy", None),) * 5

    return jax.shard_map(body, mesh=mesh, in_specs=placed, out_specs=P("gx", "gy", None), check_vma=False)
```
